32 devices in a mesh: gx: 4 (over z), gy: 4 (over y, x), gz: 2 (over core).
Axes of the slice: x: 2, y: 2, z: 4, core: 2. Of those that a mesh axis runs over, the one named last changes fastest.
Arguments:
- rhs: float32 [2, 4, 32, 64, 256], P(None, None, 'gx', 'gy', 'gz'), may hold values from -6 to 6
- density: float32 [32, 64, 256], P('gx', 'gy', 'gz'), may hold values from 0.5 to 2
- shift_real: float32 [32, 64, 256], P('gx', 'gy', 'gz'), may hold values from 0 to 0.04
- shift_imag: float32 [32, 64, 256], P('gx', 'gy', 'gz'), may hold values from 0.02 to 0.08
Outputs:
- solution: float32 [2, 4, 32, 64, 256], P(None, None, 'gx', 'gy', 'gz')
The draws below stay inside these ranges and needn't reach their ends.
All inputs are finite; a program needn't handle non-finite values.
Results may differ from the reference program's by a relative error of at most 0.00002.
Values sent between devices are 32-bit elements; how exact they have to be, the bound alone decides.
No kernel may reach another device: no remote copies, remote signals or barrier semaphores. Data moves between devices by JAX's collectives and lax.ppermute only.
A program may use at most 192 MiB of HBM per device.

```python
import math
import jax
import jax.numpy as jnp

RHS = 4
NU = 2
CSWEEPS = 4
NX = 32
NY = 64
NZ = 256


def shard_levels(own_key, shape, cuts, least, largest):
    factor_of, own = 1.0, jax.random.fold_in(own_key, 6)
    for dim, parts in cuts:
        heights = jnp.exp(jax.random.uniform(jax.random.fold_in(own, dim), (parts,), jnp.float32, least / len(cuts), largest / len(cuts)))
        factor_of = factor_of * jnp.repeat(heights, shape[dim] // parts).reshape([-1 if axis == dim else 1 for axis in range(len(shape))])
    return factor_of


def noise(own_key, dims, deviation, limit, cuts=(), kind=jnp.bfloat16):
    result = deviation * jax.random.normal(own_key, dims, jnp.float32)
    if cuts:
        result = result * shard_levels(own_key, dims, cuts, -0.22, 0.18)
    return jnp.clip(result, -limit, limit).astype(kind)


def setup_inputs(seed: int = 0) -> dict:
    key_of = jax.random.split(jax.random.key(seed), 5)
    rhs = noise(key_of[0], (2, RHS, NX, NY, NZ), 1.0, 6.0, ((2, 4), (3, 4), (4, 2)), jnp.float32)
    density = jnp.clip(jnp.exp(math.log(2.0) - 1.3862944 * jax.random.uniform(key_of[1], (NX, NY, NZ), jnp.float32) ** shard_levels(key_of[1], (NX, NY, NZ), ((0, 4), (1, 4), (2, 2)), -0.2, 0.2)), 0.5, 2.0)
    shift_real = jnp.clip(0.04 * jax.random.uniform(key_of[2], (NX, NY, NZ), jnp.float32) ** shard_levels(key_of[2], (NX, NY, NZ), ((0, 4), (1, 4), (2, 2)), -0.2, 0.2), 0.0, 0.04)
    shift_imag = jnp.clip(0.02 + 0.06 * jax.random.uniform(key_of[3], (NX, NY, NZ), jnp.float32) ** shard_levels(key_of[3], (NX, NY, NZ), ((0, 4), (1, 4), (2, 2)), -0.2, 0.2), 0.02, 0.08)
    return {"rhs": rhs, "density": density, "shift_real": shift_real, "shift_imag": shift_imag}


omega_damp = 0.8


def pad_space(field):
    widths = [(0, 0)] * (field.ndim - 3) + [(1, 1)] * 3
    return jnp.pad(field, widths)


def face_coefs(rho_pad):
    center = rho_pad[1:-1, 1:-1, 1:-1]
    others = [rho_pad[2:, 1:-1, 1:-1], rho_pad[:-2, 1:-1, 1:-1], rho_pad[1:-1, 2:, 1:-1],
              rho_pad[1:-1, :-2, 1:-1], rho_pad[1:-1, 1:-1, 2:], rho_pad[1:-1, 1:-1, :-2]]
    return [2.0 / (center + other) for other in others]


def make_level(rho_pad, shift_re, shift_im, scale):
    coefs = face_coefs(rho_pad)
    bsum = coefs[0] + coefs[1] + coefs[2] + coefs[3] + coefs[4] + coefs[5]
    diag_re = scale * bsum - shift_re
    diag_im = -shift_im
    magnitude = diag_re * diag_re + diag_im * diag_im
    return (coefs, bsum, shift_re, shift_im, scale, diag_re / magnitude, -diag_im / magnitude)


def apply_op(upad, level):
    coefs, bsum, shift_re, shift_im, scale, inv_re, inv_im = level
    center = upad[:, :, 1:-1, 1:-1, 1:-1]
    nbsum = coefs[0] * upad[:, :, 2:, 1:-1, 1:-1] + coefs[1] * upad[:, :, :-2, 1:-1, 1:-1]
    nbsum = nbsum + coefs[2] * upad[:, :, 1:-1, 2:, 1:-1] + coefs[3] * upad[:, :, 1:-1, :-2, 1:-1]
    nbsum = nbsum + coefs[4] * upad[:, :, 1:-1, 1:-1, 2:] + coefs[5] * upad[:, :, 1:-1, 1:-1, :-2]
    lap = scale * (bsum * center - nbsum)
    out_re = lap[0] - shift_re * center[0] + shift_im * center[1]
    out_im = lap[1] - shift_re * center[1] - shift_im * center[0]
    return jnp.stack([out_re, out_im])


def precondition(resid, level):
    inv_re, inv_im = level[5], level[6]
    upd_re = inv_re * resid[0] - inv_im * resid[1]
    upd_im = inv_re * resid[1] + inv_im * resid[0]
    return omega_damp * jnp.stack([upd_re, upd_im])


def smooth(field, target, level, padder, count):
    for sweep in range(count):
        field = field + precondition(target - apply_op(padder(field), level), level)
    return field


def restrict(field):
    lead = field.shape[:-3]
    sx, sy, sz = field.shape[-3:]
    blocks = field.reshape(lead + (sx // 2, 2, sy // 2, 2, sz // 2, 2))
    return jnp.mean(blocks, axis=(-5, -3, -1))


def prolong(field):
    return jnp.repeat(jnp.repeat(jnp.repeat(field, 2, -3), 2, -2), 2, -1)


def reference(rhs, density, shift_real, shift_imag):
    level0 = make_level(pad_space(density), shift_real, shift_imag, 1.0)
    rho1, sr1, si1 = restrict(density), restrict(shift_real), restrict(shift_imag)
    level1 = make_level(pad_space(rho1), sr1, si1, 0.25)
    rho2, sr2, si2 = restrict(rho1), restrict(sr1), restrict(si1)
    level2 = make_level(pad_space(rho2), sr2, si2, 0.0625)
    fine = precondition(rhs, level0)
    fine = smooth(fine, rhs, level0, pad_space, NU - 1)
    coarse_rhs = restrict(rhs - apply_op(pad_space(fine), level0))
    middle = precondition(coarse_rhs, level1)
    middle = smooth(middle, coarse_rhs, level1, pad_space, NU - 1)
    lowest_rhs = restrict(coarse_rhs - apply_op(pad_space(middle), level1))
    lowest = precondition(lowest_rhs, level2)
    lowest = smooth(lowest, lowest_rhs, level2, pad_space, CSWEEPS - 1)
    middle = smooth(middle + prolong(lowest), coarse_rhs, level1, pad_space, NU)
    fine = smooth(fine + prolong(middle), rhs, level0, pad_space, NU)
    return fine
```

```python
import jax
import jax.numpy as jnp
from jax import lax
from jax.experimental import pallas as pl
from jax.experimental.pallas import tpu as pltpu
from jax.sharding import PartitionSpec as P

NU = 2
CSWEEPS = 4


omega_damp = 0.8


def padded(cells, sides, width):
    for axis, dim in sides:
        count = lax.axis_size(axis)
        ends = count - 1
        head = lax.slice_in_dim(cells, 0, width, axis=dim)
        tail = lax.slice_in_dim(cells, cells.shape[dim] - width, cells.shape[dim], axis=dim)
        cells = jnp.concatenate(
            [
                lax.ppermute(tail, axis, [(i, (i + 1) % count) for i in range(ends)]),
                cells,
                lax.ppermute(head, axis, [((i + 1) % count, i) for i in range(ends)]),
            ],
            axis=dim,
        )
    return cells


def face_coefs(rho_pad):
    center = rho_pad[1:-1, 1:-1, 1:-1]
    others = [
        rho_pad[2:, 1:-1, 1:-1],
        rho_pad[:-2, 1:-1, 1:-1],
        rho_pad[1:-1, 2:, 1:-1],
        rho_pad[1:-1, :-2, 1:-1],
        rho_pad[1:-1, 1:-1, 2:],
        rho_pad[1:-1, 1:-1, :-2],
    ]
    result = []
    for other in others:
        total = center + other
        result.append(2.0 / jnp.where(total > 0.0, total, 1.0))
    return result


def make_level(rho_pad, shift_re, shift_im, scale):
    coefs = face_coefs(rho_pad)
    bsum = coefs[0] + coefs[1] + coefs[2] + coefs[3] + coefs[4] + coefs[5]
    diag_re = scale * bsum - shift_re
    diag_im = -shift_im
    magnitude = diag_re * diag_re + diag_im * diag_im
    return (coefs, bsum, shift_re, shift_im, scale, diag_re / magnitude, -diag_im / magnitude)


def apply_op(upad, level):
    coefs, bsum, shift_re, shift_im, scale, inv_re, inv_im = level
    center = upad[:, :, 1:-1, 1:-1, 1:-1]
    nbsum = coefs[0] * upad[:, :, 2:, 1:-1, 1:-1] + coefs[1] * upad[:, :, :-2, 1:-1, 1:-1]
    nbsum = nbsum + coefs[2] * upad[:, :, 1:-1, 2:, 1:-1] + coefs[3] * upad[:, :, 1:-1, :-2, 1:-1]
    nbsum = nbsum + coefs[4] * upad[:, :, 1:-1, 1:-1, 2:] + coefs[5] * upad[:, :, 1:-1, 1:-1, :-2]
    lap = scale * (bsum * center - nbsum)
    out_re = lap[0] - shift_re * center[0] + shift_im * center[1]
    out_im = lap[1] - shift_re * center[1] - shift_im * center[0]
    return jnp.stack([out_re, out_im])


def precondition(resid, level):
    inv_re, inv_im = (level[5], level[6])
    upd_re = inv_re * resid[0] - inv_im * resid[1]
    upd_im = inv_re * resid[1] + inv_im * resid[0]
    return omega_damp * jnp.stack([upd_re, upd_im])


def smooth(field, target, level, padder, count):
    for sweep in range(count):
        field = field + precondition(target - apply_op(padder(field), level), level)
    return field


def restrict(field):
    lead = field.shape[:-3]
    sx, sy, sz = field.shape[-3:]
    blocks = field.reshape(lead + (sx // 2, 2, sy // 2, 2, sz // 2, 2))
    return jnp.mean(blocks, axis=(-5, -3, -1))


def prolong(field):
    return jnp.repeat(jnp.repeat(jnp.repeat(field, 2, -3), 2, -2), 2, -1)


def field_pad(field):
    return padded(field, (("gx", 2), ("gy", 3), ("gz", 4)), 1)


def brick_density(rho):
    return padded(rho, (("gx", 0), ("gy", 1), ("gz", 2)), 1)


def local_general(rhs, density, shift_real, shift_imag):
    rho1, sr1, si1 = (restrict(density), restrict(shift_real), restrict(shift_imag))
    level1 = make_level(brick_density(rho1), sr1, si1, 0.25)
    rho2, sr2, si2 = (restrict(rho1), restrict(sr1), restrict(si1))
    level0 = make_level(brick_density(density), shift_real, shift_imag, 1.0)
    fine = precondition(rhs, level0)
    fine = smooth(fine, rhs, level0, field_pad, NU - 1)
    coarse_rhs = restrict(rhs - apply_op(field_pad(fine), level0))
    middle = precondition(coarse_rhs, level1)
    middle = smooth(middle, coarse_rhs, level1, field_pad, NU - 1)
    lowest_rhs = restrict(coarse_rhs - apply_op(field_pad(middle), level1))
    level2 = make_level(brick_density(rho2), sr2, si2, 0.0625)
    lowest = precondition(lowest_rhs, level2)
    lowest = smooth(lowest, lowest_rhs, level2, field_pad, CSWEEPS - 1)
    middle = smooth(middle + prolong(lowest), coarse_rhs, level1, field_pad, NU)
    corrected = fine + prolong(middle)
    return smooth(corrected, rhs, level0, field_pad, NU)


HALO = 2
MIB = 1 << 20
F32 = jnp.float32


def loop(count, body):
    lax.fori_loop(0, count, lambda i, c: (body(i), c)[1], 0)


def safe(total):
    return jnp.where(total > 0.0, total, 1.0)


def level_coefs(rho, sr, si, scale, bx, by, bz, wr, wi, dr, step):
    n, ny, nz = sr.shape
    two = 2.0 * scale
    bx[pl.ds(0, 1)] = two / safe(rho[pl.ds(0, 1)] + rho[pl.ds(1, 1)])

    def body(i):
        p = i * step
        r = rho[pl.ds(p + 1, step)]
        row = lax.broadcasted_iota(jnp.int32, r.shape, 1)
        lane = lax.broadcasted_iota(jnp.int32, r.shape, 2)
        bx[pl.ds(p + 1, step)] = two / safe(r + rho[pl.ds(p + 2, step)])
        edge = two / safe(r)
        bsum = bx[pl.ds(p, step)] + bx[pl.ds(p + 1, step)]
        last = row == ny - 1
        up = jnp.where(last, 0.0, pltpu.roll(r, ny - 1, 1))
        face = two / safe(r + up)
        bsum = bsum + face + jnp.where(row == 0, edge, pltpu.roll(face, 1, 1))
        by[pl.ds(p, step)] = jnp.where(last, 0.0, face)
        last = lane == nz - 1
        up = jnp.where(last, 0.0, pltpu.roll(r, nz - 1, 2))
        face = two / safe(r + up)
        bsum = bsum + face + jnp.where(lane == 0, edge, pltpu.roll(face, 1, 2))
        bz[pl.ds(p, step)] = jnp.where(last, 0.0, face)
        d = bsum - sr[pl.ds(p, step)]
        e = si[pl.ds(p, step)]
        w = jnp.where(r > 0.0, omega_damp, 0.0) / (d * d + e * e)
        wr[pl.ds(p, step)] = w * d
        wi[pl.ds(p, step)] = w * e
        dr[pl.ds(p, step)] = d

    loop(n // step, body)


def near(u, at, c, p, step, bx, by, bz):
    mid = u[c, pl.ds(at, step)]
    ny, nz = mid.shape[1:]
    b = by[pl.ds(p, step)]
    total = bx[pl.ds(p, step)] * u[c, pl.ds(at - 1, step)] + bx[pl.ds(p + 1, step)] * u[c, pl.ds(at + 1, step)]
    total = total + (b * pltpu.roll(mid, ny - 1, 1) + pltpu.roll(b * mid, 1, 1))
    b = bz[pl.ds(p, step)]
    return mid, total + (b * pltpu.roll(mid, nz - 1, 2) + pltpu.roll(b * mid, 1, 2))


def weigh(tr, ti, p, step, wr, wi):
    a, b = wr[pl.ds(p, step)], wi[pl.ds(p, step)]
    return a * tr - b * ti, a * ti + b * tr


def sweep_planes(u, at, g, gat, p, step, coefs):
    bx, by, bz, wr, wi = coefs
    mr, nr = near(u, at, 0, p, step, bx, by, bz)
    mi, ni = near(u, at, 1, p, step, bx, by, bz)
    vr, vi = weigh(g[0, pl.ds(gat, step)] + nr, g[1, pl.ds(gat, step)] + ni, p, step, wr, wi)
    rest = 1.0 - omega_damp
    return rest * mr + vr, rest * mi + vi


def resid_planes(u, at, g, gat, p, step, coefs, dr, si):
    bx, by, bz = coefs[:3]
    mr, nr = near(u, at, 0, p, step, bx, by, bz)
    mi, ni = near(u, at, 1, p, step, bx, by, bz)
    d, e = dr[pl.ds(p, step)], si[pl.ds(p, step)]
    return g[0, pl.ds(gat, step)] + nr - (d * mr + e * mi), g[1, pl.ds(gat, step)] + ni - (d * mi - e * mr)


def pick(nrow, ncol, down, value):
    row = lax.broadcasted_iota(jnp.int32, (nrow, ncol), 0)
    col = lax.broadcasted_iota(jnp.int32, (nrow, ncol), 1)
    hit = (row // 2 == col) if down else (row == col // 2)
    return jnp.where(hit, value, 0.0).astype(F32)


def dot(a, b):
    return jnp.dot(a, b, precision=lax.Precision.HIGHEST, preferred_element_type=F32)


def send_kernel(rhs, rho, sr, si, out):
    half = out.shape[1]
    at = (1 - lax.axis_index("gz")) * half
    m = rhs.shape[1]
    for c in range(2):
        for r in range(m):
            out[2 * r + c] = rhs[c, r, pl.ds(at, half)]
    for j, ref in enumerate((rho, sr, si)):
        out[2 * m + j] = ref[pl.ds(at, half)]


def spread_kernel(rhs, rho, sr, si, came, out):
    half = came.shape[1]
    at = lax.axis_index("gz") * half
    m = rhs.shape[1]
    for r in range(m):
        for c in range(2):
            out[r, 0, c] = rhs[c, r, pl.ds(at, half)]
            out[r, 1, c] = came[2 * r + c]
        for j, ref in enumerate((rho, sr, si)):
            out[r, 0, 2 + j] = ref[pl.ds(at, half)]
            out[r, 1, 2 + j] = came[2 * m + j]


def edge_kernel(blocks, over_gz, over_gx):
    k = lax.axis_index("gz")
    half = blocks.shape[3]
    for out, high in ((over_gz, 1 - k), (over_gx, k)):
        two, three = high * (half - HALO), high * (half - HALO - 1)
        for s in range(blocks.shape[0]):
            for t in range(2):
                for j, f in enumerate((0, 1, 3, 4)):
                    out[s, t, pl.ds(HALO * j, HALO)] = blocks[s, t, f, pl.ds(two, HALO)]
                out[s, t, pl.ds(4 * HALO, HALO + 1)] = blocks[s, t, 2, pl.ds(three, HALO + 1)]


def fine_kernel(blocks, from_gz, from_gx, own, up_gz, up_gx, packed, g, bx, by, bz, wr, wi, rho, sr, si, dr, ua, ub, sums, narrow):
    k = lax.axis_index("gz")
    nsrc, _, _, half, rows, lanes = blocks.shape
    ny, nz = g.shape[2:]

    def place(ref, first, count, s, z, value):
        ref[pl.ds(first, count), s * rows : (s + 1) * rows, pl.ds(pl.multiple_of(z * lanes, lanes), lanes)] = value

    for s in range(nsrc):
        for t in range(2):
            z = k if t == 0 else 1 - k
            for f, ref in ((0, g.at[0]), (1, g.at[1]), (3, sr), (4, si)):
                place(ref, HALO, half, s, z, blocks[s, t, f])
            place(rho, HALO + 1, half, s, z, blocks[s, t, 2])

    def halo(came, low):
        for s in range(nsrc):
            for t in range(2):
                z = 1 - k if t == 0 else k
                first = 0 if low else half + HALO
                for j, ref in enumerate((g.at[0], g.at[1], sr, si)):
                    place(ref, first, HALO, s, z, came[s, t, HALO * j : HALO * (j + 1)])
                place(rho, 0 if low else half + HALO + 1, HALO + 1, s, z, came[s, t, 4 * HALO : 5 * HALO + 1])

    @pl.when(k == 0)
    def _():
        halo(from_gx, True)
        halo(from_gz, False)

    @pl.when(k == 1)
    def _():
        halo(from_gz, True)
        halo(from_gx, False)

    level_coefs(rho, sr, si, 1.0, bx, by, bz, wr, wi, dr, 1)
    coefs = (bx, by, bz, wr, wi)

    def first(p):
        ua[0, pl.ds(p, 1)], ua[1, pl.ds(p, 1)] = weigh(g[0, pl.ds(p, 1)], g[1, pl.ds(p, 1)], p, 1, wr, wi)

    loop(half + 2 * HALO, first)

    def second(i):
        p = i + 1
        ub[0, pl.ds(p, 1)], ub[1, pl.ds(p, 1)] = sweep_planes(ua, p, g, p, p, 1, coefs)

    loop(half + 2 * HALO - 2, second)
    for c in range(2):
        own[c] = ub[c, pl.ds(HALO, half)]
        up_gz[c] = ub[c, pl.ds(HALO + (1 - k) * (half - HALO), HALO)]
        up_gx[c] = ub[c, pl.ds(HALO + k * (half - HALO), HALO)]

    pairs = half // 2

    def down(q):
        p = HALO + 2 * q
        ar, ai = resid_planes(ub, p, g, p, p, 1, coefs, dr, si)
        br, bi = resid_planes(ub, p + 1, g, p + 1, p + 1, 1, coefs, dr, si)
        totals = (ar + br, ai + bi, rho[pl.ds(p + 1, 1)] + rho[pl.ds(p + 2, 1)], sr[pl.ds(p, 1)] + sr[pl.ds(p + 1, 1)], si[pl.ds(p, 1)] + si[pl.ds(p + 1, 1)])
        for j, v in enumerate(totals):
            sums[pl.ds(pl.multiple_of((j * pairs + q) * ny, ny), ny), :] = v[0]

    loop(pairs, down)
    narrow[...] = dot(sums[...], pick(nz, nz // 2, True, 0.125))
    n = 5 * pairs * ny // 2
    done = (narrow[pl.ds(0, n, 2), :] + narrow[pl.ds(1, n, 2), :]).reshape(5, pairs, ny // 2, nz // 2)
    for d in range(packed.shape[0]):
        packed[d] = done


def coarse_kernel(
    mine, other, own, from_gz, from_gx, g0, bx0, by0, bz0, wr0, wi0, out,
    rho1, sr1, si1, g1, bx1, by1, bz1, wr1, wi1, dr1, ua1, ub1,
    rho2, sr2, si2, g2, bx2, by2, bz2, wr2, wi2, dr2, ua2, ub2,
    sums, narrow, wide, tall, ua0, ub0,
):
    k = lax.axis_index("gz")
    chip = lax.axis_index("gx")
    chips, _, pairs, ny, nz = mine.shape
    n1 = sr1.shape[0]
    zero = jnp.zeros((1, ny, nz), F32)
    rho1[pl.ds(0, 1)] = zero
    rho1[pl.ds(n1 + 1, 1)] = zero
    for u in (ua1, ub1):
        for c in range(2):
            u[c, pl.ds(0, 1)] = zero
            u[c, pl.ds(n1 + 1, 1)] = zero
    for s in range(chips):
        for ref, z in ((mine, k), (other, 1 - k)):
            at = 2 * pairs * s + pairs * z
            for c in range(2):
                g1[c, pl.ds(at, pairs)] = ref[s, c]
            rho1[pl.ds(at + 1, pairs)] = ref[s, 2]
            sr1[pl.ds(at, pairs)] = ref[s, 3]
            si1[pl.ds(at, pairs)] = ref[s, 4]
    step1 = 4
    level_coefs(rho1, sr1, si1, 0.25, bx1, by1, bz1, wr1, wi1, dr1, step1)
    coefs1 = (bx1, by1, bz1, wr1, wi1)

    def first(i):
        p = i * step1
        r, m = weigh(g1[0, pl.ds(p, step1)], g1[1, pl.ds(p, step1)], p, step1, wr1, wi1)
        ua1[0, pl.ds(p + 1, step1)], ua1[1, pl.ds(p + 1, step1)] = r, m

    loop(n1 // step1, first)

    def sweep1(src, dst):
        def body(i):
            p = i * step1
            r, m = sweep_planes(src, p + 1, g1, p, p, step1, coefs1)
            dst[0, pl.ds(p + 1, step1)], dst[1, pl.ds(p + 1, step1)] = r, m

        loop(n1 // step1, body)

    sweep1(ua1, ub1)
    n2 = n1 // 2
    ny2 = ny // 2

    def down(q):
        p = 2 * q
        r, m = resid_planes(ub1, p + 1, g1, p, p, 2, coefs1, dr1, si1)
        totals = (r[0] + r[1], m[0] + m[1], rho1[p + 1] + rho1[p + 2], sr1[p] + sr1[p + 1], si1[p] + si1[p + 1])
        for j, v in enumerate(totals):
            sums[pl.ds(pl.multiple_of((j * n2 + q) * ny, ny), ny), :] = v

    loop(n2, down)
    narrow[...] = dot(sums[...], pick(nz, nz, True, 0.125))
    n = n2 * ny2
    zero2 = jnp.zeros((1, ny2, nz), F32)
    rho2[pl.ds(0, 1)] = zero2
    rho2[pl.ds(n2 + 1, 1)] = zero2
    for u in (ua2, ub2):
        for c in range(2):
            u[c, pl.ds(0, 1)] = zero2
            u[c, pl.ds(n2 + 1, 1)] = zero2
    for j, ref in enumerate((g2.at[0], g2.at[1], rho2.at[pl.ds(1, n2)], sr2, si2)):
        at = 2 * n * j
        ref[...] = (narrow[pl.ds(at, n, 2), :] + narrow[pl.ds(at + 1, n, 2), :]).reshape(n2, ny2, nz)
    level_coefs(rho2, sr2, si2, 0.0625, bx2, by2, bz2, wr2, wi2, dr2, n2)
    coefs2 = (bx2, by2, bz2, wr2, wi2)
    ua2[0, pl.ds(1, n2)], ua2[1, pl.ds(1, n2)] = weigh(g2[0], g2[1], 0, n2, wr2, wi2)
    src, dst = ua2, ub2
    for _ in range(CSWEEPS - 1):
        dst[0, pl.ds(1, n2)], dst[1, pl.ds(1, n2)] = sweep_planes(src, 1, g2, 0, 0, n2, coefs2)
        src, dst = dst, src

    widen = pick(nz, nz, False, 1.0)
    for c in range(2):
        wide[pl.ds(c * n, n), :] = dot(src[c, pl.ds(1, n2)].reshape(n, nz), widen)
    twice = wide[pl.ds(0, 2 * n), :]
    tall[pl.ds(0, 2 * n, 2), :] = twice
    tall[pl.ds(1, 2 * n, 2), :] = twice

    def lift(q):
        for c in range(2):
            v = tall[pl.ds(pl.multiple_of((c * n2 + q) * ny, ny), ny), :]
            for j in range(2):
                ub1[c, 2 * q + j + 1] = ub1[c, 2 * q + j + 1] + v

    loop(n2, lift)
    sweep1(ub1, ua1)
    sweep1(ua1, ub1)

    half = own.shape[1]
    pad = half + 2 * HALO
    quads = pad // 2
    base = (2 * chip + k) * pairs
    fine_z = own.shape[3]
    fine_y = own.shape[2]
    rows = quads * ny

    @pl.when(k == 0)
    def _():
        ua0[:, pl.ds(0, HALO)] = from_gx[...]
        ua0[:, pl.ds(HALO + half, HALO)] = from_gz[...]

    @pl.when(k == 1)
    def _():
        ua0[:, pl.ds(0, HALO)] = from_gz[...]
        ua0[:, pl.ds(HALO + half, HALO)] = from_gx[...]

    ua0[:, pl.ds(HALO, half)] = own[...]
    for h in range(fine_z // nz):
        col = lax.broadcasted_iota(jnp.int32, (nz, nz), 1) + h * nz
        row = lax.broadcasted_iota(jnp.int32, (nz, nz), 0)
        widen = jnp.where(row == col // 2, 1.0, 0.0).astype(F32)
        for c in range(2):
            v = dot(ub1[c, pl.ds(base, quads)].reshape(rows, nz), widen)
            tall[pl.ds(0, rows, 2), :] = v
            tall[pl.ds(1, rows, 2), :] = v
            for q in range(quads):
                w = tall[pl.ds(q * fine_y, fine_y), :]
                for j in range(2):
                    p = 2 * q + j
                    ua0[c, p, :, h * nz : (h + 1) * nz] = ua0[c, p, :, h * nz : (h + 1) * nz] + w
    coefs0 = (bx0, by0, bz0, wr0, wi0)

    def third(i):
        p = i + 1
        ub0[0, pl.ds(p, 1)], ub0[1, pl.ds(p, 1)] = sweep_planes(ua0, p, g0, p, p, 1, coefs0)

    loop(pad - 2, third)
    dests, _, _, _, drows, lanes = out.shape

    def fourth(i):
        p = i + HALO
        r, m = sweep_planes(ub0, p, g0, p, p, 1, coefs0)
        for c, v in enumerate((r, m)):
            for d in range(dests):
                for z in range(2):
                    slot = jnp.where(k == z, 0, 1)
                    out[d, slot, c, i] = v[0, d * drows : (d + 1) * drows, z * lanes : (z + 1) * lanes]

    loop(half, fourth)


def gather_kernel(kept, came, out):
    half = kept.shape[3]
    k = lax.axis_index("gz")
    for r in range(kept.shape[0]):
        for c in range(2):
            out[c, r, pl.ds(k * half, half)] = kept[r, 0, c]
            out[c, r, pl.ds((1 - k) * half, half)] = came[r, c]


def call(kernel, outs, args, scratch=(), limit=24):
    vm = pl.BlockSpec(memory_space=pltpu.VMEM)
    single = not isinstance(outs, list)
    shapes = [outs] if single else outs
    result = pl.pallas_call(
        kernel,
        out_shape=[jax.ShapeDtypeStruct(s, F32) for s in shapes],
        in_specs=[vm] * len(args),
        out_specs=[vm] * len(shapes),
        scratch_shapes=[pltpu.VMEM(s, F32) for s in scratch],
        compiler_params=pltpu.CompilerParams(vmem_limit_bytes=limit * MIB),
    )(*args)
    return result[0] if single else result


def local_planes(rhs, density, shift_real, shift_imag):
    _, m, xs, rows, lanes = rhs.shape
    half = xs // 2
    chips = lax.axis_size("gx")
    ny, nz = rows * m, 2 * lanes
    pad = half + 2 * HALO
    swap = [(0, 1), (1, 0)]
    ends = [p for c in range(chips - 1) for p in ((2 * c + 1, 2 * c + 2), (2 * c + 2, 2 * c + 1))]
    fields = (rhs, density, shift_real, shift_imag)

    away = call(send_kernel, (2 * m + 3, half, rows, lanes), fields)
    came = lax.ppermute(away, "gz", swap)
    spread = call(spread_kernel, (m, 2, 5, half, rows, lanes), fields + (came,))
    blocks = lax.all_to_all(spread, "gy", 0, 0, tiled=True)

    edges = (m, 2, 5 * HALO + 1, rows, lanes)
    to_gz, to_gx = call(edge_kernel, [edges, edges], (blocks,))
    from_gx = lax.ppermute(to_gx, ("gx", "gz"), ends)
    from_gz = lax.ppermute(to_gz, "gz", swap)

    pairs = half // 2
    plane = (ny, nz)
    own, up_gz, up_gx, packed, g, bx, by, bz, wr, wi = call(
        fine_kernel,
        [(2, half) + plane, (2, HALO) + plane, (2, HALO) + plane, (chips, 5, pairs, ny // 2, nz // 2), (2, pad) + plane, (pad + 1,) + plane]
        + [(pad,) + plane] * 4,
        (blocks, from_gz, from_gx),
        scratch=[(pad + 2,) + plane] + [(pad,) + plane] * 3 + [(2, pad) + plane] * 2 + [(5 * pairs * ny, nz), (5 * pairs * ny, nz // 2)],
        limit=40,
    )
    u_gx = lax.ppermute(up_gx, ("gx", "gz"), ends)
    u_gz = lax.ppermute(up_gz, "gz", swap)
    mine = lax.all_to_all(packed, "gx", 0, 0, tiled=True)
    other = lax.ppermute(mine, "gz", swap)

    n1, n2 = chips * xs // 2, chips * xs // 4
    p1, p2 = (ny // 2, nz // 2), (ny // 4, nz // 2)

    def level(n, p):
        return [(n + 2,) + p, (n,) + p, (n,) + p, (2, n) + p, (n + 1,) + p] + [(n,) + p] * 5 + [(2, n + 2) + p] * 2

    tall = max(2 * n2 * p1[0], pad * ny // 2 * 2)
    result = call(
        coarse_kernel,
        (m, 2, 2, half, rows, lanes),
        (mine, other, own, u_gz, u_gx, g, bx, by, bz, wr, wi),
        scratch=level(n1, p1)
        + level(n2, p2)
        + [(5 * n2 * p1[0], p1[1])] * 2
        + [(2 * n2 * p2[0], p1[1]), (tall, p1[1]), (2, pad) + plane, (2, pad) + plane],
        limit=40,
    )
    back = lax.all_to_all(result, "gy", 0, 0, tiled=True)
    last = lax.ppermute(back[:, 1], "gz", swap)
    return call(gather_kernel, rhs.shape, (back, last))


def solution(mesh):
    sizes = dict(mesh.shape)

    def local(rhs, density, shift_real, shift_imag):
        _, m, xs, rows, lanes = rhs.shape
        planes = sizes["gz"] == 2 and sizes["gy"] == m and xs % 8 == 0 and rows % 16 == 0 and lanes == 128
        return (local_planes if planes else local_general)(rhs, density, shift_real, shift_imag)

    placed = (
        P(None, None, "gx", "gy", "gz"),
        P("gx", "gy", "gz"),
        P("gx", "gy", "gz"),
        P("gx", "gy", "gz"),
    )
    return jax.shard_map(
        local,
        mesh=mesh,
        in_specs=placed,
        out_specs=P(None, None, "gx", "gy", "gz"),
        check_vma=False,
    )
```

```python
import jax
import jax.numpy as jnp
from jax import lax
from jax.experimental import pallas as pl
from jax.experimental.pallas import tpu as pltpu
from jax.sharding import PartitionSpec as P

NU = 2
CSWEEPS = 4


omega_damp = 0.8


def padded(cells, sides, width):
    for axis, dim in sides:
        count = lax.axis_size(axis)
        ends = count - 1
        head = lax.slice_in_dim(cells, 0, width, axis=dim)
        tail = lax.slice_in_dim(cells, cells.shape[dim] - width, cells.shape[dim], axis=dim)
        cells = jnp.concatenate(
            [
                lax.ppermute(tail, axis, [(i, (i + 1) % count) for i in range(ends)]),
                cells,
                lax.ppermute(head, axis, [((i + 1) % count, i) for i in range(ends)]),
            ],
            axis=dim,
        )
    return cells


def face_coefs(rho_pad):
    center = rho_pad[1:-1, 1:-1, 1:-1]
    others = [
        rho_pad[2:, 1:-1, 1:-1],
        rho_pad[:-2, 1:-1, 1:-1],
        rho_pad[1:-1, 2:, 1:-1],
        rho_pad[1:-1, :-2, 1:-1],
        rho_pad[1:-1, 1:-1, 2:],
        rho_pad[1:-1, 1:-1, :-2],
    ]
    result = []
    for other in others:
        total = center + other
        result.append(2.0 / jnp.where(total > 0.0, total, 1.0))
    return result


def make_level(rho_pad, shift_re, shift_im, scale):
    coefs = face_coefs(rho_pad)
    bsum = coefs[0] + coefs[1] + coefs[2] + coefs[3] + coefs[4] + coefs[5]
    diag_re = scale * bsum - shift_re
    diag_im = -shift_im
    magnitude = diag_re * diag_re + diag_im * diag_im
    return (coefs, bsum, shift_re, shift_im, scale, diag_re / magnitude, -diag_im / magnitude)


def apply_op(upad, level):
    coefs, bsum, shift_re, shift_im, scale, inv_re, inv_im = level
    center = upad[:, :, 1:-1, 1:-1, 1:-1]
    nbsum = coefs[0] * upad[:, :, 2:, 1:-1, 1:-1] + coefs[1] * upad[:, :, :-2, 1:-1, 1:-1]
    nbsum = nbsum + coefs[2] * upad[:, :, 1:-1, 2:, 1:-1] + coefs[3] * upad[:, :, 1:-1, :-2, 1:-1]
    nbsum = nbsum + coefs[4] * upad[:, :, 1:-1, 1:-1, 2:] + coefs[5] * upad[:, :, 1:-1, 1:-1, :-2]
    lap = scale * (bsum * center - nbsum)
    out_re = lap[0] - shift_re * center[0] + shift_im * center[1]
    out_im = lap[1] - shift_re * center[1] - shift_im * center[0]
    return jnp.stack([out_re, out_im])


def precondition(resid, level):
    inv_re, inv_im = (level[5], level[6])
    upd_re = inv_re * resid[0] - inv_im * resid[1]
    upd_im = inv_re * resid[1] + inv_im * resid[0]
    return omega_damp * jnp.stack([upd_re, upd_im])


def smooth(field, target, level, padder, count):
    for sweep in range(count):
        field = field + precondition(target - apply_op(padder(field), level), level)
    return field


def restrict(field):
    lead = field.shape[:-3]
    sx, sy, sz = field.shape[-3:]
    blocks = field.reshape(lead + (sx // 2, 2, sy // 2, 2, sz // 2, 2))
    return jnp.mean(blocks, axis=(-5, -3, -1))


def prolong(field):
    return jnp.repeat(jnp.repeat(jnp.repeat(field, 2, -3), 2, -2), 2, -1)


def field_pad(field):
    return padded(field, (("gx", 2), ("gy", 3), ("gz", 4)), 1)


def brick_density(rho):
    return padded(rho, (("gx", 0), ("gy", 1), ("gz", 2)), 1)


def local_general(rhs, density, shift_real, shift_imag):
    rho1, sr1, si1 = (restrict(density), restrict(shift_real), restrict(shift_imag))
    level1 = make_level(brick_density(rho1), sr1, si1, 0.25)
    rho2, sr2, si2 = (restrict(rho1), restrict(sr1), restrict(si1))
    level0 = make_level(brick_density(density), shift_real, shift_imag, 1.0)
    fine = precondition(rhs, level0)
    fine = smooth(fine, rhs, level0, field_pad, NU - 1)
    coarse_rhs = restrict(rhs - apply_op(field_pad(fine), level0))
    middle = precondition(coarse_rhs, level1)
    middle = smooth(middle, coarse_rhs, level1, field_pad, NU - 1)
    lowest_rhs = restrict(coarse_rhs - apply_op(field_pad(middle), level1))
    level2 = make_level(brick_density(rho2), sr2, si2, 0.0625)
    lowest = precondition(lowest_rhs, level2)
    lowest = smooth(lowest, lowest_rhs, level2, field_pad, CSWEEPS - 1)
    middle = smooth(middle + prolong(lowest), coarse_rhs, level1, field_pad, NU)
    corrected = fine + prolong(middle)
    return smooth(corrected, rhs, level0, field_pad, NU)


HALO = 2
MIB = 1 << 20
COARSE_COST = 5 * 10**9
LAY_COST = 5 * 10**9
F32 = jnp.float32


def loop(count, body):
    lax.fori_loop(0, count, lambda i, c: (body(i), c)[1], 0)


def safe(total):
    return jnp.where(total > 0.0, total, 1.0)


def level_coefs(rho, sr, si, scale, bx, by, bz, wr, wi, dr, step, start, count):
    ny, nz = sr.shape[1:]
    two = 2.0 * scale
    bx[pl.ds(start, 1)] = two / safe(rho[pl.ds(start, 1)] + rho[pl.ds(start + 1, 1)])

    def body(i):
        p = start + i * step
        r = rho[pl.ds(p + 1, step)]
        row = lax.broadcasted_iota(jnp.int32, r.shape, 1)
        lane = lax.broadcasted_iota(jnp.int32, r.shape, 2)
        bx[pl.ds(p + 1, step)] = two / safe(r + rho[pl.ds(p + 2, step)])
        edge = two / safe(r)
        bsum = bx[pl.ds(p, step)] + bx[pl.ds(p + 1, step)]
        last = row == ny - 1
        up = jnp.where(last, 0.0, pltpu.roll(r, ny - 1, 1))
        face = two / safe(r + up)
        bsum = bsum + face + jnp.where(row == 0, edge, pltpu.roll(face, 1, 1))
        by[pl.ds(p, step)] = jnp.where(last, 0.0, face)
        last = lane == nz - 1
        up = jnp.where(last, 0.0, pltpu.roll(r, nz - 1, 2))
        face = two / safe(r + up)
        bsum = bsum + face + jnp.where(lane == 0, edge, pltpu.roll(face, 1, 2))
        bz[pl.ds(p, step)] = jnp.where(last, 0.0, face)
        d = bsum - sr[pl.ds(p, step)]
        e = si[pl.ds(p, step)]
        w = jnp.where(r > 0.0, omega_damp, 0.0) / (d * d + e * e)
        wr[pl.ds(p, step)] = w * d
        wi[pl.ds(p, step)] = w * e
        dr[pl.ds(p, step)] = d

    loop(count // step, body)


def near(u, at, c, p, step, bx, by, bz):
    mid = u[c, pl.ds(at, step)]
    ny, nz = mid.shape[1:]
    b = by[pl.ds(p, step)]
    total = bx[pl.ds(p, step)] * u[c, pl.ds(at - 1, step)] + bx[pl.ds(p + 1, step)] * u[c, pl.ds(at + 1, step)]
    total = total + (b * pltpu.roll(mid, ny - 1, 1) + pltpu.roll(b * mid, 1, 1))
    b = bz[pl.ds(p, step)]
    return mid, total + (b * pltpu.roll(mid, nz - 1, 2) + pltpu.roll(b * mid, 1, 2))


def weigh(tr, ti, p, step, wr, wi):
    a, b = wr[pl.ds(p, step)], wi[pl.ds(p, step)]
    return a * tr - b * ti, a * ti + b * tr


def sweep_planes(u, at, g, gat, p, step, coefs):
    bx, by, bz, wr, wi = coefs
    mr, nr = near(u, at, 0, p, step, bx, by, bz)
    mi, ni = near(u, at, 1, p, step, bx, by, bz)
    vr, vi = weigh(g[0, pl.ds(gat, step)] + nr, g[1, pl.ds(gat, step)] + ni, p, step, wr, wi)
    rest = 1.0 - omega_damp
    return rest * mr + vr, rest * mi + vi


def resid_planes(u, at, g, gat, p, step, coefs, dr, si):
    bx, by, bz = coefs[:3]
    mr, nr = near(u, at, 0, p, step, bx, by, bz)
    mi, ni = near(u, at, 1, p, step, bx, by, bz)
    d, e = dr[pl.ds(p, step)], si[pl.ds(p, step)]
    return g[0, pl.ds(gat, step)] + nr - (d * mr + e * mi), g[1, pl.ds(gat, step)] + ni - (d * mi - e * mr)


def pick(nrow, ncol, down, value):
    row = lax.broadcasted_iota(jnp.int32, (nrow, ncol), 0)
    col = lax.broadcasted_iota(jnp.int32, (nrow, ncol), 1)
    hit = (row // 2 == col) if down else (row == col // 2)
    return jnp.where(hit, value, 0.0).astype(F32)


def dot(a, b):
    return jnp.dot(a, b, precision=lax.Precision.HIGHEST, preferred_element_type=F32)


def send_kernel(rhs, rho, sr, si, away, kept, sems):
    half = away.shape[1]
    m = rhs.shape[1]
    k = lax.axis_index("gz")
    copies = []
    for n, (out, side) in enumerate(((away, 1 - k), (kept, k))):
        planes = pl.ds(side * half, half)
        pieces = [(rhs.at[c, :, planes], out.at[pl.ds(c * m, m)]) for c in range(2)]
        pieces += [(ref.at[planes], out.at[2 * m + j]) for j, ref in enumerate((rho, sr, si))]
        copies += [pltpu.make_async_copy(src, dst, sems.at[5 * n + j]) for j, (src, dst) in enumerate(pieces)]
    for copy in copies:
        copy.start()
    for copy in copies:
        copy.wait()


def spread_kernel(kept, came, close, far):
    k = lax.axis_index("gz")
    m = close.shape[0]
    half = kept.shape[1]
    rest = half - HALO
    for t, ref in enumerate((kept, came)):
        for r in range(m):
            for j, f in enumerate((r, m + r, 2 * m + 1, 2 * m + 2)):
                close[r, t, HALO * j : HALO * (j + 1)] = ref[f, pl.ds(k * rest, HALO)]
                far[r, t, rest * j : rest * (j + 1)] = ref[f, pl.ds((1 - k) * HALO, rest)]
            close[r, t, 4 * HALO : 5 * HALO + 1] = ref[2 * m, pl.ds(k * (rest - 1), HALO + 1)]
            far[r, t, 4 * rest : 5 * rest - 1] = ref[2 * m, pl.ds((1 - k) * (HALO + 1), rest - 1)]


def edge_kernel(close, far, out):
    k = lax.axis_index("gz")
    for s in range(close.shape[0]):
        for t in range(2):
            out[s, t, 0 : 4 * HALO] = far[s, t, 0 : 4 * HALO]
            out[s, t, pl.ds(4 * HALO + k, HALO)] = close[s, t, pl.ds(5 * HALO - 1 - k, HALO)]
            out[s, t, 5 * HALO - k * HALO] = far[s, t, 4 * HALO]


def put_planes(came, other, arrays, rho, first, first_rho):
    k = lax.axis_index("gz")
    rows, lanes = came.shape[3:]
    count = came.shape[2] // 4
    for s in range(came.shape[0]):
        for t in range(2):
            z = jnp.where(k == t, 1, 0) if other else jnp.where(k == t, 0, 1)
            spot = (slice(s * rows, (s + 1) * rows), pl.ds(pl.multiple_of(z * lanes, lanes), lanes))
            for j, ref in enumerate(arrays):
                ref[(pl.ds(first, count), *spot)] = came[s, t, count * j : count * (j + 1)]
            rho[(pl.ds(first_rho, came.shape[2] - 4 * count), *spot)] = came[s, t, 4 * count :]


def lay_kernel(close, far, from_gx, g, rho, sr, si, bx, by, bz, wr, wi, dr):
    k = lax.axis_index("gz")
    pad = g.shape[1]
    half = pad - 2 * HALO
    rest = half - HALO
    arrays = (g.at[0], g.at[1], sr, si)
    put_planes(close, False, arrays, rho, HALO + k * rest, HALO + 1 + k * (rest - 1))
    put_planes(far, False, arrays, rho, HALO + (1 - k) * HALO, HALO + 1 + (1 - k) * (HALO + 1))
    put_planes(from_gx, True, arrays, rho, k * (half + HALO), k * (half + HALO + 1))
    level_coefs(rho, sr, si, 1.0, bx, by, bz, wr, wi, dr, 1, k * (HALO + 1), pad - HALO - 1)


def fine_kernel(from_gz, *refs):
    g, rho, sr, si, bx, by, bz, wr, wi, dr, own, up_gz, up_gx, packed, ua, sums, narrow = refs[10:]
    k = lax.axis_index("gz")
    pad, ny, nz = g.shape[1:]
    half = pad - 2 * HALO
    put_planes(from_gz, True, (g.at[0], g.at[1], sr, si), rho, (1 - k) * (half + HALO), (1 - k) * (half + HALO + 1))
    level_coefs(rho, sr, si, 1.0, bx, by, bz, wr, wi, dr, 1, (1 - k) * (pad - HALO - 1), HALO + 1)
    coefs = (bx, by, bz, wr, wi)

    def first(p):
        ua[0, pl.ds(p, 1)], ua[1, pl.ds(p, 1)] = weigh(g[0, pl.ds(p, 1)], g[1, pl.ds(p, 1)], p, 1, wr, wi)

    loop(pad, first)

    def second(i):
        p = i + 1
        own[0, pl.ds(i, 1)], own[1, pl.ds(i, 1)] = sweep_planes(ua, p, g, p, p, 1, coefs)

    loop(pad - 2, second)
    for c in range(2):
        up_gz[c] = own[c, 2 + (1 - k) * (half - 3)]
        up_gx[c] = own[c, 2 + k * (half - 3)]

    pairs = half // 2

    def down(q):
        p = HALO + 2 * q
        ar, ai = resid_planes(own, p - 1, g, p, p, 1, coefs, dr, si)
        br, bi = resid_planes(own, p, g, p + 1, p + 1, 1, coefs, dr, si)
        totals = (ar + br, ai + bi, rho[pl.ds(p + 1, 1)] + rho[pl.ds(p + 2, 1)], sr[pl.ds(p, 1)] + sr[pl.ds(p + 1, 1)], si[pl.ds(p, 1)] + si[pl.ds(p + 1, 1)])
        for j, v in enumerate(totals):
            sums[pl.ds(pl.multiple_of((j * pairs + q) * ny, ny), ny), :] = v[0]

    loop(pairs, down)
    narrow[...] = dot(sums[...], pick(nz, nz // 2, True, 0.125))
    n = 5 * pairs * ny // 2
    done = (narrow[pl.ds(0, n, 2), :] + narrow[pl.ds(1, n, 2), :]).reshape(5, pairs, ny // 2, nz // 2)
    for d in range(packed.shape[0]):
        packed[d] = done


def coarse_kernel(
    mine, other, out,
    rho1, sr1, si1, g1, bx1, by1, bz1, wr1, wi1, dr1, ua1, ub1,
    rho2, sr2, si2, g2, bx2, by2, bz2, wr2, wi2, dr2, ua2, ub2,
    sums, narrow, wide, tall,
):
    k = lax.axis_index("gz")
    chip = lax.axis_index("gx")
    chips, _, pairs, ny, nz = mine.shape
    n1 = sr1.shape[0]
    zero = jnp.zeros((1, ny, nz), F32)
    rho1[pl.ds(0, 1)] = zero
    rho1[pl.ds(n1 + 1, 1)] = zero
    for u in (ua1, ub1):
        for c in range(2):
            u[c, pl.ds(0, 1)] = zero
            u[c, pl.ds(n1 + 1, 1)] = zero
    for s in range(chips):
        for ref, z in ((mine, k), (other, 1 - k)):
            at = 2 * pairs * s + pairs * z
            for c in range(2):
                g1[c, pl.ds(at, pairs)] = ref[s, c]
            rho1[pl.ds(at + 1, pairs)] = ref[s, 2]
            sr1[pl.ds(at, pairs)] = ref[s, 3]
            si1[pl.ds(at, pairs)] = ref[s, 4]
    step1 = 4
    level_coefs(rho1, sr1, si1, 0.25, bx1, by1, bz1, wr1, wi1, dr1, step1, 0, n1)
    coefs1 = (bx1, by1, bz1, wr1, wi1)

    def first(i):
        p = i * step1
        r, m = weigh(g1[0, pl.ds(p, step1)], g1[1, pl.ds(p, step1)], p, step1, wr1, wi1)
        ua1[0, pl.ds(p + 1, step1)], ua1[1, pl.ds(p + 1, step1)] = r, m

    loop(n1 // step1, first)

    def sweep1(src, dst):
        def body(i):
            p = i * step1
            r, m = sweep_planes(src, p + 1, g1, p, p, step1, coefs1)
            dst[0, pl.ds(p + 1, step1)], dst[1, pl.ds(p + 1, step1)] = r, m

        loop(n1 // step1, body)

    sweep1(ua1, ub1)
    n2 = n1 // 2
    ny2 = ny // 2

    def down(q):
        p = 2 * q
        r, m = resid_planes(ub1, p + 1, g1, p, p, 2, coefs1, dr1, si1)
        totals = (r[0] + r[1], m[0] + m[1], rho1[p + 1] + rho1[p + 2], sr1[p] + sr1[p + 1], si1[p] + si1[p + 1])
        for j, v in enumerate(totals):
            sums[pl.ds(pl.multiple_of((j * n2 + q) * ny, ny), ny), :] = v

    loop(n2, down)
    narrow[...] = dot(sums[...], pick(nz, nz, True, 0.125))
    n = n2 * ny2
    zero2 = jnp.zeros((1, ny2, nz), F32)
    rho2[pl.ds(0, 1)] = zero2
    rho2[pl.ds(n2 + 1, 1)] = zero2
    for u in (ua2, ub2):
        for c in range(2):
            u[c, pl.ds(0, 1)] = zero2
            u[c, pl.ds(n2 + 1, 1)] = zero2
    for j, ref in enumerate((g2.at[0], g2.at[1], rho2.at[pl.ds(1, n2)], sr2, si2)):
        at = 2 * n * j
        ref[...] = (narrow[pl.ds(at, n, 2), :] + narrow[pl.ds(at + 1, n, 2), :]).reshape(n2, ny2, nz)
    level_coefs(rho2, sr2, si2, 0.0625, bx2, by2, bz2, wr2, wi2, dr2, n2, 0, n2)
    coefs2 = (bx2, by2, bz2, wr2, wi2)
    ua2[0, pl.ds(1, n2)], ua2[1, pl.ds(1, n2)] = weigh(g2[0], g2[1], 0, n2, wr2, wi2)
    src, dst = ua2, ub2
    for _ in range(CSWEEPS - 1):
        dst[0, pl.ds(1, n2)], dst[1, pl.ds(1, n2)] = sweep_planes(src, 1, g2, 0, 0, n2, coefs2)
        src, dst = dst, src

    widen = pick(nz, nz, False, 1.0)
    for c in range(2):
        wide[pl.ds(c * n, n), :] = dot(src[c, pl.ds(1, n2)].reshape(n, nz), widen)
    twice = wide[pl.ds(0, 2 * n), :]
    tall[pl.ds(0, 2 * n, 2), :] = twice
    tall[pl.ds(1, 2 * n, 2), :] = twice

    def lift(q):
        for c in range(2):
            v = tall[pl.ds(pl.multiple_of((c * n2 + q) * ny, ny), ny), :]
            for j in range(2):
                ub1[c, 2 * q + j + 1] = ub1[c, 2 * q + j + 1] + v

    loop(n2, lift)
    sweep1(ub1, ua1)
    sweep1(ua1, ub1)

    quads = out.shape[1]
    out[...] = ub1[:, pl.ds((2 * chip + k) * pairs, quads)]


def last_kernel(u1, own, from_gz, from_gx, g0, bx0, by0, bz0, wr0, wi0, out, ua0, ub0, tall):
    k = lax.axis_index("gz")
    quads, ny, nz = u1.shape[1:]
    pad, fine_y, fine_z = ua0.shape[1:]
    half = pad - 2 * HALO
    rows = quads * ny
    ua0[:, pl.ds(1, pad - 2)] = own[...]
    ua0[:, k * (pad - 1)] = from_gx[...]
    ua0[:, (1 - k) * (pad - 1)] = from_gz[...]
    for h in range(fine_z // nz):
        col = lax.broadcasted_iota(jnp.int32, (nz, nz), 1) + h * nz
        row = lax.broadcasted_iota(jnp.int32, (nz, nz), 0)
        widen = jnp.where(row == col // 2, 1.0, 0.0).astype(F32)
        for c in range(2):
            v = dot(u1[c].reshape(rows, nz), widen)
            tall[pl.ds(0, rows, 2), :] = v
            tall[pl.ds(1, rows, 2), :] = v
            for q in range(quads):
                w = tall[pl.ds(q * fine_y, fine_y), :]
                for j in range(2):
                    p = 2 * q + j
                    ua0[c, p, :, h * nz : (h + 1) * nz] = ua0[c, p, :, h * nz : (h + 1) * nz] + w
    coefs0 = (bx0, by0, bz0, wr0, wi0)

    def third(i):
        p = i + 1
        ub0[0, pl.ds(p, 1)], ub0[1, pl.ds(p, 1)] = sweep_planes(ua0, p, g0, p, p, 1, coefs0)

    loop(pad - 2, third)
    dests, _, _, _, drows, lanes = out.shape

    def fourth(i):
        p = i + HALO
        r, m = sweep_planes(ub0, p, g0, p, p, 1, coefs0)
        for c, v in enumerate((r, m)):
            for d in range(dests):
                for z in range(2):
                    out[d, z, c, i] = v[0, d * drows : (d + 1) * drows, z * lanes : (z + 1) * lanes]

    loop(half, fourth)


def gather_kernel(came, out):
    half = came.shape[3]
    for r in range(came.shape[0]):
        for z in range(2):
            for c in range(2):
                out[c, r, z * half : (z + 1) * half] = came[r, z, c]


def call(kernel, outs, args, scratch=(), limit=24, space=pltpu.VMEM, sems=None, cost=None, aliases=None):
    single = not isinstance(outs, list)
    shapes = [outs] if single else outs
    result = pl.pallas_call(
        kernel,
        out_shape=[jax.ShapeDtypeStruct(s, F32) for s in shapes],
        in_specs=[pl.BlockSpec(memory_space=space)] * len(args),
        out_specs=[pl.BlockSpec(memory_space=pltpu.VMEM)] * len(shapes),
        scratch_shapes=[pltpu.VMEM(s, F32) for s in scratch] + ([pltpu.SemaphoreType.DMA((sems,))] if sems else []),
        compiler_params=pltpu.CompilerParams(vmem_limit_bytes=limit * MIB),
        input_output_aliases=aliases or {},
        cost_estimate=cost and pl.CostEstimate(flops=cost, bytes_accessed=0, transcendentals=0),
    )(*args)
    return result[0] if single else result


def local_planes(rhs, density, shift_real, shift_imag):
    _, m, xs, rows, lanes = rhs.shape
    half = xs // 2
    chips = lax.axis_size("gx")
    ny, nz = rows * m, 2 * lanes
    pad = half + 2 * HALO
    swap = [(0, 1), (1, 0)]
    ends = [p for c in range(chips - 1) for p in ((2 * c + 1, 2 * c + 2), (2 * c + 2, 2 * c + 1))]
    fields = (rhs, density, shift_real, shift_imag)

    own_half = (2 * m + 3, half, rows, lanes)
    away, kept = call(send_kernel, [own_half, own_half], tuple(pltpu.with_memory_space_constraint(f, pltpu.HBM) for f in fields), space=pltpu.HBM, sems=10)
    came = lax.ppermute(away, "gz", swap)
    edges = (m, 2, 5 * HALO + 1, rows, lanes)
    close, far = call(spread_kernel, [edges, (m, 2, 5 * (half - HALO) - 1, rows, lanes)], (kept, came))
    close = lax.all_to_all(close, "gy", 0, 0, tiled=True)
    from_gx = lax.ppermute(close, ("gx", "gz"), ends)
    far = lax.all_to_all(far, "gy", 0, 0, tiled=True)
    to_gz = call(edge_kernel, edges, (close, far))
    from_gz = lax.ppermute(to_gz, "gz", swap)

    pairs = half // 2
    plane = (ny, nz)
    laid = [(2, pad) + plane, (pad + 2,) + plane, (pad,) + plane, (pad,) + plane, (pad + 1,) + plane] + [(pad,) + plane] * 5
    state = call(lay_kernel, laid, (close, far, from_gx), limit=24, cost=LAY_COST)
    g, _, _, _, bx, by, bz, wr, wi, _, own, up_gz, up_gx, packed = call(
        fine_kernel,
        laid + [(2, pad - 2) + plane, (2,) + plane, (2,) + plane, (chips, 5, pairs, ny // 2, nz // 2)],
        (from_gz, *state),
        scratch=[(2, pad) + plane] + [(5 * pairs * ny, nz), (5 * pairs * ny, nz // 2)],
        limit=24,
        aliases={i + 1: i for i in range(len(laid))},
    )
    u_gx = lax.ppermute(up_gx, ("gx", "gz"), ends)
    u_gz = lax.ppermute(up_gz, "gz", swap)
    mine = lax.all_to_all(packed, "gx", 0, 0, tiled=True)
    other = lax.ppermute(mine, "gz", swap)

    n1, n2 = chips * xs // 2, chips * xs // 4
    p1, p2 = (ny // 2, nz // 2), (ny // 4, nz // 2)

    def level(n, p):
        return [(n + 2,) + p, (n,) + p, (n,) + p, (2, n) + p, (n + 1,) + p] + [(n,) + p] * 5 + [(2, n + 2) + p] * 2

    u1 = call(
        coarse_kernel,
        (2, pad // 2) + p1,
        (mine, other),
        scratch=level(n1, p1) + level(n2, p2) + [(5 * n2 * p1[0], p1[1])] * 2 + [(2 * n2 * p2[0], p1[1]), (2 * n2 * p1[0], p1[1])],
        limit=32,
        cost=COARSE_COST,
    )
    result = call(
        last_kernel,
        (m, 2, 2, half, rows, lanes),
        (u1, own, u_gz, u_gx, g, bx, by, bz, wr, wi),
        scratch=[(2, pad) + plane, (2, pad) + plane, (pad * ny // 2, p1[1])],
        limit=32,
    )
    back = lax.all_to_all(result.reshape((2 * m,) + result.shape[2:]), ("gy", "gz"), 0, 0, tiled=True)
    return call(gather_kernel, rhs.shape, (back.reshape(result.shape),))


def solution(mesh):
    sizes = dict(mesh.shape)

    def local(rhs, density, shift_real, shift_imag):
        _, m, xs, rows, lanes = rhs.shape
        planes = sizes["gz"] == 2 and sizes["gy"] == m and xs == 8 and rows % 16 == 0 and lanes == 128
        return (local_planes if planes else local_general)(rhs, density, shift_real, shift_imag)

    placed = (
        P(None, None, "gx", "gy", "gz"),
        P("gx", "gy", "gz"),
        P("gx", "gy", "gz"),
        P("gx", "gy", "gz"),
    )
    return jax.shard_map(
        local,
        mesh=mesh,
        in_specs=placed,
        out_specs=P(None, None, "gx", "gy", "gz"),
        check_vma=False,
    )
```

```python
import jax
import jax.numpy as jnp
from jax import lax
from jax.experimental import pallas as pl
from jax.experimental.pallas import tpu as pltpu
from jax.sharding import PartitionSpec as P

NU = 2
CSWEEPS = 4


omega_damp = 0.8


def padded(cells, sides, width):
    for axis, dim in sides:
        count = lax.axis_size(axis)
        ends = count - 1
        head = lax.slice_in_dim(cells, 0, width, axis=dim)
        tail = lax.slice_in_dim(cells, cells.shape[dim] - width, cells.shape[dim], axis=dim)
        cells = jnp.concatenate(
            [
                lax.ppermute(tail, axis, [(i, (i + 1) % count) for i in range(ends)]),
                cells,
                lax.ppermute(head, axis, [((i + 1) % count, i) for i in range(ends)]),
            ],
            axis=dim,
        )
    return cells


def face_coefs(rho_pad):
    center = rho_pad[1:-1, 1:-1, 1:-1]
    others = [
        rho_pad[2:, 1:-1, 1:-1],
        rho_pad[:-2, 1:-1, 1:-1],
        rho_pad[1:-1, 2:, 1:-1],
        rho_pad[1:-1, :-2, 1:-1],
        rho_pad[1:-1, 1:-1, 2:],
        rho_pad[1:-1, 1:-1, :-2],
    ]
    result = []
    for other in others:
        total = center + other
        result.append(2.0 / jnp.where(total > 0.0, total, 1.0))
    return result


def make_level(rho_pad, shift_re, shift_im, scale):
    coefs = face_coefs(rho_pad)
    bsum = coefs[0] + coefs[1] + coefs[2] + coefs[3] + coefs[4] + coefs[5]
    diag_re = scale * bsum - shift_re
    diag_im = -shift_im
    magnitude = diag_re * diag_re + diag_im * diag_im
    return (coefs, bsum, shift_re, shift_im, scale, diag_re / magnitude, -diag_im / magnitude)


def apply_op(upad, level):
    coefs, bsum, shift_re, shift_im, scale, inv_re, inv_im = level
    center = upad[:, :, 1:-1, 1:-1, 1:-1]
    nbsum = coefs[0] * upad[:, :, 2:, 1:-1, 1:-1] + coefs[1] * upad[:, :, :-2, 1:-1, 1:-1]
    nbsum = nbsum + coefs[2] * upad[:, :, 1:-1, 2:, 1:-1] + coefs[3] * upad[:, :, 1:-1, :-2, 1:-1]
    nbsum = nbsum + coefs[4] * upad[:, :, 1:-1, 1:-1, 2:] + coefs[5] * upad[:, :, 1:-1, 1:-1, :-2]
    lap = scale * (bsum * center - nbsum)
    out_re = lap[0] - shift_re * center[0] + shift_im * center[1]
    out_im = lap[1] - shift_re * center[1] - shift_im * center[0]
    return jnp.stack([out_re, out_im])


def precondition(resid, level):
    inv_re, inv_im = (level[5], level[6])
    upd_re = inv_re * resid[0] - inv_im * resid[1]
    upd_im = inv_re * resid[1] + inv_im * resid[0]
    return omega_damp * jnp.stack([upd_re, upd_im])


def smooth(field, target, level, padder, count):
    for sweep in range(count):
        field = field + precondition(target - apply_op(padder(field), level), level)
    return field


def restrict(field):
    lead = field.shape[:-3]
    sx, sy, sz = field.shape[-3:]
    blocks = field.reshape(lead + (sx // 2, 2, sy // 2, 2, sz // 2, 2))
    return jnp.mean(blocks, axis=(-5, -3, -1))


def prolong(field):
    return jnp.repeat(jnp.repeat(jnp.repeat(field, 2, -3), 2, -2), 2, -1)


def field_pad(field):
    return padded(field, (("gx", 2), ("gy", 3), ("gz", 4)), 1)


def brick_density(rho):
    return padded(rho, (("gx", 0), ("gy", 1), ("gz", 2)), 1)


def local_general(rhs, density, shift_real, shift_imag):
    rho1, sr1, si1 = (restrict(density), restrict(shift_real), restrict(shift_imag))
    level1 = make_level(brick_density(rho1), sr1, si1, 0.25)
    rho2, sr2, si2 = (restrict(rho1), restrict(sr1), restrict(si1))
    level0 = make_level(brick_density(density), shift_real, shift_imag, 1.0)
    fine = precondition(rhs, level0)
    fine = smooth(fine, rhs, level0, field_pad, NU - 1)
    coarse_rhs = restrict(rhs - apply_op(field_pad(fine), level0))
    middle = precondition(coarse_rhs, level1)
    middle = smooth(middle, coarse_rhs, level1, field_pad, NU - 1)
    lowest_rhs = restrict(coarse_rhs - apply_op(field_pad(middle), level1))
    level2 = make_level(brick_density(rho2), sr2, si2, 0.0625)
    lowest = precondition(lowest_rhs, level2)
    lowest = smooth(lowest, lowest_rhs, level2, field_pad, CSWEEPS - 1)
    middle = smooth(middle + prolong(lowest), coarse_rhs, level1, field_pad, NU)
    corrected = fine + prolong(middle)
    return smooth(corrected, rhs, level0, field_pad, NU)


HALO = 2
SIDE = 4
MIB = 1 << 20
COARSE_COST = 5 * 10**9
F32 = jnp.float32


def loop(count, body):
    lax.fori_loop(0, count, lambda i, c: (body(i), c)[1], 0)


def safe(total):
    return jnp.where(total > 0.0, total, 1.0)


def level_coefs(rho, sr, si, scale, bx, by, bz, wr, wi, dr, step, start, count):
    ny, nz = sr.shape[1:]
    two = 2.0 * scale
    bx[pl.ds(start, 1)] = two / safe(rho[pl.ds(start, 1)] + rho[pl.ds(start + 1, 1)])

    def body(i):
        p = start + i * step
        r = rho[pl.ds(p + 1, step)]
        row = lax.broadcasted_iota(jnp.int32, r.shape, 1)
        lane = lax.broadcasted_iota(jnp.int32, r.shape, 2)
        bx[pl.ds(p + 1, step)] = two / safe(r + rho[pl.ds(p + 2, step)])
        edge = two / safe(r)
        bsum = bx[pl.ds(p, step)] + bx[pl.ds(p + 1, step)]
        last = row == ny - 1
        up = jnp.where(last, 0.0, pltpu.roll(r, ny - 1, 1))
        face = two / safe(r + up)
        bsum = bsum + face + jnp.where(row == 0, edge, pltpu.roll(face, 1, 1))
        by[pl.ds(p, step)] = jnp.where(last, 0.0, face)
        last = lane == nz - 1
        up = jnp.where(last, 0.0, pltpu.roll(r, nz - 1, 2))
        face = two / safe(r + up)
        bsum = bsum + face + jnp.where(lane == 0, edge, pltpu.roll(face, 1, 2))
        bz[pl.ds(p, step)] = jnp.where(last, 0.0, face)
        d = bsum - sr[pl.ds(p, step)]
        e = si[pl.ds(p, step)]
        w = jnp.where(r > 0.0, omega_damp, 0.0) / (d * d + e * e)
        wr[pl.ds(p, step)] = w * d
        wi[pl.ds(p, step)] = w * e
        dr[pl.ds(p, step)] = d

    loop(count // step, body)


def near(u, f, at, p, step, bx, by, bz):
    mid = u[f, pl.ds(at, step)]
    ny, nz = mid.shape[1:]
    b = by[pl.ds(p, step)]
    total = bx[pl.ds(p, step)] * u[f, pl.ds(at - 1, step)] + bx[pl.ds(p + 1, step)] * u[f, pl.ds(at + 1, step)]
    total = total + (b * pltpu.roll(mid, ny - 1, 1) + pltpu.roll(b * mid, 1, 1))
    b = bz[pl.ds(p, step)]
    return mid, total + (b * pltpu.roll(mid, nz - 1, 2) + pltpu.roll(b * mid, 1, 2))


def weigh(tr, ti, p, step, wr, wi):
    a, b = wr[pl.ds(p, step)], wi[pl.ds(p, step)]
    return a * tr - b * ti, a * ti + b * tr


def sweep_planes(u, fields, at, g, gat, p, step, coefs):
    bx, by, bz, wr, wi = coefs
    re, im = fields
    mr, nr = near(u, re, at, p, step, bx, by, bz)
    mi, ni = near(u, im, at, p, step, bx, by, bz)
    vr, vi = weigh(g[re, pl.ds(gat, step)] + nr, g[im, pl.ds(gat, step)] + ni, p, step, wr, wi)
    rest = 1.0 - omega_damp
    return rest * mr + vr, rest * mi + vi


def resid_planes(u, fields, at, g, gat, p, step, coefs, dr, si):
    bx, by, bz = coefs[:3]
    re, im = fields
    mr, nr = near(u, re, at, p, step, bx, by, bz)
    mi, ni = near(u, im, at, p, step, bx, by, bz)
    d, e = dr[pl.ds(p, step)], si[pl.ds(p, step)]
    return g[re, pl.ds(gat, step)] + nr - (d * mr + e * mi), g[im, pl.ds(gat, step)] + ni - (d * mi - e * mr)


def pick(nrow, ncol, down, value):
    row = lax.broadcasted_iota(jnp.int32, (nrow, ncol), 0)
    col = lax.broadcasted_iota(jnp.int32, (nrow, ncol), 1)
    hit = (row // 2 == col) if down else (row == col // 2)
    return jnp.where(hit, value, 0.0).astype(F32)


def dot(a, b):
    return jnp.dot(a, b, precision=lax.Precision.HIGHEST, preferred_element_type=F32)


def send_kernel(rhs, rho, sr, si, away, kept, sems):
    half = away.shape[1]
    m = rhs.shape[1]
    k = lax.axis_index("gz")
    copies = []
    for n, (out, side) in enumerate(((away, 1 - k), (kept, k))):
        planes = pl.ds(side * half, half)
        pieces = [(rhs.at[c, :, planes], out.at[pl.ds(c * m, m)]) for c in range(2)]
        pieces += [(ref.at[planes], out.at[2 * m + j]) for j, ref in enumerate((rho, sr, si))]
        copies += [pltpu.make_async_copy(src, dst, sems.at[5 * n + j]) for j, (src, dst) in enumerate(pieces)]
    for copy in copies:
        copy.start()
    for copy in copies:
        copy.wait()


def rows_kernel(kept, came, out, ends):
    y = lax.axis_index("gy")
    fields, half, rows, _ = kept.shape
    rho = fields - 3
    for t, ref in enumerate((kept, came)):
        for h in range(2):
            at = 0
            for f in range(fields):
                n = HALO + 1 if f == rho else HALO
                for i in range(half):
                    ends[h, t, at : at + n, :] = ref[f, i, (rows - n if h else 0) : (rows if h else n), :]
                    at += n
    for d in range(out.shape[0]):
        out[d] = ends[jnp.where(y < d, 1, 0)]


def lay_kernel(kept, came, ends, g, rho, sr, si, to_gz, to_gx):
    k = lax.axis_index("gz")
    y = lax.axis_index("gy")
    fields, half, rows, lanes = kept.shape
    m2 = fields - 3
    arrays = [g.at[f] for f in range(m2)] + [rho, sr, si]
    for f, ref in enumerate(arrays):
        first = HALO + 1 if f == m2 else HALO
        for i in range(half):
            ref[first + i] = jnp.zeros(ref.shape[1:], F32)
        for t, src in enumerate((kept, came)):
            z = k if t == 0 else 1 - k
            spot = pl.ds(pl.multiple_of(z * lanes, lanes), lanes)
            for i in range(half):
                ref[first + i, SIDE : SIDE + rows, spot] = src[f, i]
    for high in range(2):
        count = ends.shape[0]
        there = jnp.where(y < count - 1, 1.0, 0.0) if high else jnp.where(y > 0, 1.0, 0.0)
        peer = jnp.minimum(y + 1, count - 1) if high else jnp.maximum(y - 1, 0)
        for z in range(2):
            slot = jnp.where(k == z, 0, 1)
            at = 0
            for f, ref in enumerate(arrays):
                n = HALO + 1 if f == m2 else HALO
                row = SIDE + rows if high else SIDE - n
                for i in range(half):
                    ref[n + i, row : row + n, z * lanes : (z + 1) * lanes] = ends[peer, slot, at : at + n, :] * there
                    at += n
    for out, up in ((to_gz, 1 - k), (to_gx, k)):
        two, three = HALO + up * (half - HALO), HALO + 1 + up * (half - HALO - 1)
        for j, ref in enumerate(arrays[:m2] + [sr, si]):
            out[HALO * j : HALO * (j + 1)] = ref[pl.ds(two, HALO)]
        out[HALO * (m2 + 2) :] = rho[pl.ds(three, HALO + 1)]


def fine_kernel(from_gz, from_gx, _g, _rho, _sr, _si, g, rho, sr, si, bx, by, bz, wr, wi, own, up_gz, up_gx, up_gy, packed, dr, ua, left, right, narrow):
    k = lax.axis_index("gz")
    m2, pad, ny, nz = g.shape
    m = m2 // 2
    half = pad - 2 * HALO
    rows = ny - 2 * SIDE
    for came, low in ((from_gx, k), (from_gz, 1 - k)):
        two, three = low * (half + HALO), low * (half + HALO + 1)
        for j, ref in enumerate([g.at[f] for f in range(m2)] + [sr, si]):
            ref[pl.ds(two, HALO)] = came[HALO * j : HALO * (j + 1)]
        rho[pl.ds(three, HALO + 1)] = came[HALO * (m2 + 2) :]
    level_coefs(rho, sr, si, 1.0, bx, by, bz, wr, wi, dr, 1, 0, pad)
    coefs = (bx, by, bz, wr, wi)

    def first(p):
        for r in range(m):
            ua[r, pl.ds(p, 1)], ua[m + r, pl.ds(p, 1)] = weigh(g[r, pl.ds(p, 1)], g[m + r, pl.ds(p, 1)], p, 1, wr, wi)

    loop(pad, first)

    def second(i):
        p = i + 1
        for r in range(m):
            own[r, pl.ds(i, 1)], own[m + r, pl.ds(i, 1)] = sweep_planes(ua, (r, m + r), p, g, p, p, 1, coefs)

    loop(pad - 2, second)
    lanes = nz // 2
    for f in range(m2):
        up_gz[f] = own[f, 2 + (1 - k) * (half - 3), SIDE : SIDE + rows, :]
        up_gx[f] = own[f, 2 + k * (half - 3), SIDE : SIDE + rows, :]
        for i in range(half):
            for h, row in enumerate((SIDE + 1, SIDE + rows - 2)):
                for z in range(2):
                    at = z * m2 * half + f * half + i
                    up_gy[h, at : at + 1, :] = own[f, i + 1, row : row + 1, z * lanes : (z + 1) * lanes]
    pairs = half // 2

    def down(q):
        p = HALO + 2 * q
        totals = {}
        for r in range(m):
            ar, ai = resid_planes(own, (r, m + r), p - 1, g, p, p, 1, coefs, dr, si)
            br, bi = resid_planes(own, (r, m + r), p, g, p + 1, p + 1, 1, coefs, dr, si)
            totals[r], totals[m + r] = ar + br, ai + bi
        totals[m2] = rho[pl.ds(p + 1, 1)] + rho[pl.ds(p + 2, 1)]
        for j, ref in ((m2 + 1, sr), (m2 + 2, si)):
            totals[j] = ref[pl.ds(p, 1)] + ref[pl.ds(p + 1, 1)]
        for j, v in totals.items():
            spot = pl.ds(pl.multiple_of((j * pairs + q) * ny, ny), ny)
            left[spot, :] = v[0, :, :lanes]
            right[spot, :] = v[0, :, lanes:]

    loop(pairs, down)
    n = (m2 + 3) * pairs * ny // 2
    both = [ref[pl.ds(0, n, 2), :] + ref[pl.ds(1, n, 2), :] for ref in (left, right)]
    narrow[...] = dot(jnp.concatenate(both, axis=1), pick(nz, lanes, True, 0.125))
    for q in range(pairs):
        done = []
        for j in range(m2 + 3):
            at = (j * pairs + q) * (ny // 2) + SIDE // 2
            done.append(narrow[at : at + rows // 2, :])
        for d in range(packed.shape[0]):
            r = d % m
            for a, j in enumerate((r, m + r, m2, m2 + 1, m2 + 2)):
                packed[d, a, q] = done[j]


def coarse_kernel(
    mine, other, out,
    rho1, sr1, si1, g1, bx1, by1, bz1, wr1, wi1, dr1, ua1, ub1,
    rho2, sr2, si2, g2, bx2, by2, bz2, wr2, wi2, dr2, ua2, ub2,
    sums, narrow, wide, tall,
):
    k = lax.axis_index("gz")
    chip = lax.axis_index("gx")
    _, _, pairs, rows, nz = mine.shape
    n1, ny = sr1.shape[:2]
    parts = ny // rows
    chips = mine.shape[0] // parts
    zero = jnp.zeros((1, ny, nz), F32)
    rho1[pl.ds(0, 1)] = zero
    rho1[pl.ds(n1 + 1, 1)] = zero
    for u in (ua1, ub1):
        for c in range(2):
            u[c, pl.ds(0, 1)] = zero
            u[c, pl.ds(n1 + 1, 1)] = zero
    for s in range(chips):
        for ref, z in ((mine, k), (other, 1 - k)):
            at = 2 * pairs * s + pairs * z
            for y in range(parts):
                spot = slice(y * rows, (y + 1) * rows)
                e = s * parts + y
                for c in range(2):
                    g1[c, pl.ds(at, pairs), spot] = ref[e, c]
                rho1[pl.ds(at + 1, pairs), spot] = ref[e, 2]
                sr1[pl.ds(at, pairs), spot] = ref[e, 3]
                si1[pl.ds(at, pairs), spot] = ref[e, 4]
    step1 = 4
    level_coefs(rho1, sr1, si1, 0.25, bx1, by1, bz1, wr1, wi1, dr1, step1, 0, n1)
    coefs1 = (bx1, by1, bz1, wr1, wi1)

    def first(i):
        p = i * step1
        r, m = weigh(g1[0, pl.ds(p, step1)], g1[1, pl.ds(p, step1)], p, step1, wr1, wi1)
        ua1[0, pl.ds(p + 1, step1)], ua1[1, pl.ds(p + 1, step1)] = r, m

    loop(n1 // step1, first)

    def sweep1(src, dst):
        def body(i):
            p = i * step1
            r, m = sweep_planes(src, (0, 1), p + 1, g1, p, p, step1, coefs1)
            dst[0, pl.ds(p + 1, step1)], dst[1, pl.ds(p + 1, step1)] = r, m

        loop(n1 // step1, body)

    sweep1(ua1, ub1)
    n2 = n1 // 2
    ny2 = ny // 2

    def down(q):
        p = 2 * q
        r, m = resid_planes(ub1, (0, 1), p + 1, g1, p, p, 2, coefs1, dr1, si1)
        totals = (r[0] + r[1], m[0] + m[1], rho1[p + 1] + rho1[p + 2], sr1[p] + sr1[p + 1], si1[p] + si1[p + 1])
        for j, v in enumerate(totals):
            sums[pl.ds(pl.multiple_of((j * n2 + q) * ny, ny), ny), :] = v

    loop(n2, down)
    narrow[...] = dot(sums[...], pick(nz, nz, True, 0.125))
    n = n2 * ny2
    zero2 = jnp.zeros((1, ny2, nz), F32)
    rho2[pl.ds(0, 1)] = zero2
    rho2[pl.ds(n2 + 1, 1)] = zero2
    for u in (ua2, ub2):
        for c in range(2):
            u[c, pl.ds(0, 1)] = zero2
            u[c, pl.ds(n2 + 1, 1)] = zero2
    for j, ref in enumerate((g2.at[0], g2.at[1], rho2.at[pl.ds(1, n2)], sr2, si2)):
        at = 2 * n * j
        ref[...] = (narrow[pl.ds(at, n, 2), :] + narrow[pl.ds(at + 1, n, 2), :]).reshape(n2, ny2, nz)
    level_coefs(rho2, sr2, si2, 0.0625, bx2, by2, bz2, wr2, wi2, dr2, n2, 0, n2)
    coefs2 = (bx2, by2, bz2, wr2, wi2)
    ua2[0, pl.ds(1, n2)], ua2[1, pl.ds(1, n2)] = weigh(g2[0], g2[1], 0, n2, wr2, wi2)
    src, dst = ua2, ub2
    for _ in range(CSWEEPS - 1):
        dst[0, pl.ds(1, n2)], dst[1, pl.ds(1, n2)] = sweep_planes(src, (0, 1), 1, g2, 0, 0, n2, coefs2)
        src, dst = dst, src

    widen = pick(nz, nz, False, 1.0)
    for c in range(2):
        wide[pl.ds(c * n, n), :] = dot(src[c, pl.ds(1, n2)].reshape(n, nz), widen)
    twice = wide[pl.ds(0, 2 * n), :]
    tall[pl.ds(0, 2 * n, 2), :] = twice
    tall[pl.ds(1, 2 * n, 2), :] = twice

    def lift(q):
        for c in range(2):
            v = tall[pl.ds(pl.multiple_of((c * n2 + q) * ny, ny), ny), :]
            for j in range(2):
                ub1[c, 2 * q + j + 1] = ub1[c, 2 * q + j + 1] + v

    loop(n2, lift)
    sweep1(ub1, ua1)
    sweep1(ua1, ub1)

    out[...] = ub1[:, pl.ds((2 * chip + k) * pairs, 2 + pairs)]


def pack_kernel(u1, up_gy, from_gz, from_gx, out, edges):
    k = lax.axis_index("gz")
    me = lax.axis_index("gy")
    edges[k] = from_gz[...]
    edges[1 - k] = from_gx[...]
    _, quads, ny, nz = u1.shape
    parts = out.shape[0]
    rows = ny // parts
    edge = SIDE // 2
    tall_rows = rows + 2 * edge
    for y in range(parts):
        low, high = max(y * rows - edge, 0), min((y + 1) * rows + edge, ny)
        for c in range(2):
            for q in range(quads):
                at = (c * quads + q) * tall_rows
                skip = low - (y * rows - edge)
                end = skip + high - low
                if skip:
                    out[y, at : at + skip, :] = jnp.zeros((skip, nz), F32)
                out[y, at + skip : at + end, :] = u1[c, q, low:high, :]
                if end < tall_rows:
                    out[y, at + end : at + tall_rows, :] = jnp.zeros((tall_rows - end, nz), F32)
        out[y, 2 * quads * tall_rows :, :] = up_gy[jnp.where(me < y, 1, 0)]


def last_kernel(back, own, edges, g, bx, by, bz, wr, wi, out, ua, ub, tall):
    k = lax.axis_index("gz")
    y = lax.axis_index("gy")
    m2, pad, ny, nz = ua.shape
    m = m2 // 2
    half = pad - 2 * HALO
    rows = ny - 2 * SIDE
    quads = pad // 2
    lanes = nz // 2
    ua[:, pl.ds(1, pad - 2)] = own[...]
    parts = back.shape[0]
    blank = jnp.zeros((m2, ny, nz), F32)
    for p, side in ((0, 1), (pad - 1, 0)):
        ua[:, p] = blank
        ua[:, p, SIDE : SIDE + rows, :] = edges[side]
    used = 2 * quads * ny // 2
    for high in range(2):
        there = jnp.where(y < parts - 1, 1.0, 0.0) if high else jnp.where(y > 0, 1.0, 0.0)
        peer = jnp.minimum(y + 1, parts - 1) if high else jnp.maximum(y - 1, 0)
        row = SIDE + rows + 1 if high else SIDE - 2
        block = back[peer, used:, :] * there
        for z in range(2):
            for f in range(m2):
                for i in range(half):
                    at = z * m2 * half + f * half + i
                    ua[f, HALO + i, row : row + 1, z * lanes : (z + 1) * lanes] = block[at : at + 1, :]
    u1 = back[:, :used, :].reshape(m * used, lanes)
    for h in range(2):
        col = lax.broadcasted_iota(jnp.int32, (lanes, lanes), 1) + h * lanes
        line = lax.broadcasted_iota(jnp.int32, (lanes, lanes), 0)
        v = dot(u1, jnp.where(line == col // 2, 1.0, 0.0).astype(F32))
        tall[pl.ds(0, m * used, 2), :] = v
        tall[pl.ds(1, m * used, 2), :] = v
        spot = slice(h * lanes, (h + 1) * lanes)
        for r in range(m):
            for c in range(2):
                for q in range(quads):
                    at = ((r * 2 + c) * quads + q) * ny
                    w = tall[at : at + ny, :]
                    f = c * m + r
                    for j in range(2):
                        ua[f, 2 * q + j, :, spot] = ua[f, 2 * q + j, :, spot] + w
    coefs = (bx, by, bz, wr, wi)

    def third(i):
        p = i + 1
        for r in range(m):
            ub[r, pl.ds(p, 1)], ub[m + r, pl.ds(p, 1)] = sweep_planes(ua, (r, m + r), p, g, p, p, 1, coefs)

    loop(pad - 2, third)

    def fourth(i):
        p = i + HALO
        for r in range(m):
            for c, v in enumerate(sweep_planes(ub, (r, m + r), p, g, p, p, 1, coefs)):
                for z in range(2):
                    slot = jnp.where(k == z, 0, 1)
                    out[slot, c, r, i] = v[0, SIDE : SIDE + rows, z * lanes : (z + 1) * lanes]

    loop(half, fourth)


def gather_kernel(kept, came, out):
    k = lax.axis_index("gz")
    half = kept.shape[2]
    for side, ref in ((k, kept), (1 - k, came)):
        for c in range(2):
            for r in range(kept.shape[1]):
                out[c, r, pl.ds(side * half, half)] = ref[c, r]


def call(kernel, outs, args, scratch=(), limit=14, space=pltpu.VMEM, sems=None, cost=None, aliases=None):
    single = not isinstance(outs, list)
    shapes = [outs] if single else outs
    result = pl.pallas_call(
        kernel,
        out_shape=[jax.ShapeDtypeStruct(s, F32) for s in shapes],
        in_specs=[pl.BlockSpec(memory_space=space)] * len(args),
        out_specs=[pl.BlockSpec(memory_space=pltpu.VMEM)] * len(shapes),
        scratch_shapes=[pltpu.VMEM(s, F32) for s in scratch] + ([pltpu.SemaphoreType.DMA((sems,))] if sems else []),
        compiler_params=pltpu.CompilerParams(vmem_limit_bytes=limit * MIB),
        input_output_aliases=aliases or {},
        cost_estimate=cost and pl.CostEstimate(flops=cost, bytes_accessed=0, transcendentals=0),
    )(*args)
    return result[0] if single else result


def local_planes(rhs, density, shift_real, shift_imag):
    _, m, xs, rows, lanes = rhs.shape
    half = xs // 2
    chips = lax.axis_size("gx")
    ny, nz = rows * m, 2 * lanes
    pad = half + 2 * HALO
    swap = [(0, 1), (1, 0)]
    ends = [p for c in range(chips - 1) for p in ((2 * c + 1, 2 * c + 2), (2 * c + 2, 2 * c + 1))]
    fields = (rhs, density, shift_real, shift_imag)

    own_half = (2 * m + 3, half, rows, lanes)
    placed = tuple(pltpu.with_memory_space_constraint(f, pltpu.HBM) for f in fields)
    away, kept = call(send_kernel, [own_half, own_half], placed, space=pltpu.HBM, sems=10)
    came = lax.ppermute(away, "gz", swap)
    rim = ((2 * m + 3) * HALO + 1) * half
    rim = (m, 2, -(-rim // 8) * 8, lanes)
    ends_y = call(rows_kernel, rim, (kept, came), scratch=[(2,) + rim[1:]])
    ends_y = lax.all_to_all(ends_y, "gy", 0, 0, tiled=True)

    plane = (rows + 2 * SIDE, nz)
    laid = [(2 * m, pad) + plane, (pad + 2,) + plane, (pad,) + plane, (pad,) + plane]
    edges = (HALO * (2 * m + 2) + HALO + 1,) + plane
    *state, to_gz, to_gx = call(lay_kernel, laid + [edges, edges], (kept, came, ends_y))
    from_gx = lax.ppermute(to_gx, ("gx", "gz"), ends)
    from_gz = lax.ppermute(to_gz, "gz", swap)

    pairs = half // 2
    brow = (rows, nz)
    tall0 = (2 * m + 3) * pairs * plane[0]
    g, _, _, _, bx, by, bz, wr, wi, own, up_gz, up_gx, up_gy, packed = call(
        fine_kernel,
        laid
        + [(pad + 1,) + plane]
        + [(pad,) + plane] * 4
        + [(2 * m, pad - 2) + plane, (2 * m,) + brow, (2 * m,) + brow, (2, 4 * m * half, lanes), (chips * m, 5, pairs, rows // 2, lanes)],
        (from_gz, from_gx, *state),
        scratch=[(pad,) + plane, (2 * m, pad) + plane, (tall0, lanes), (tall0, lanes), (tall0 // 2, lanes)],
        aliases={i + 2: i for i in range(len(laid))},
    )
    u_gx = lax.ppermute(up_gx, ("gx", "gz"), ends)
    u_gz = lax.ppermute(up_gz, "gz", swap)
    mine = lax.all_to_all(packed, ("gx", "gy"), 0, 0, tiled=True)
    other = lax.ppermute(mine, "gz", swap)

    n1, n2 = chips * xs // 2, chips * xs // 4
    p1, p2 = (ny // 2, nz // 2), (ny // 4, nz // 2)

    def level(n, p):
        return [(n + 2,) + p, (n,) + p, (n,) + p, (2, n) + p, (n + 1,) + p] + [(n,) + p] * 5 + [(2, n + 2) + p] * 2

    used = (2 + pairs) * plane[0]
    u1 = call(
        coarse_kernel,
        (2, 2 + pairs) + p1,
        (mine, other),
        scratch=level(n1, p1) + level(n2, p2) + [(5 * n2 * p1[0], p1[1])] * 2 + [(2 * n2 * p2[0], p1[1]), (2 * n2 * p1[0], p1[1])],
        limit=14,
        cost=COARSE_COST,
    )
    packed, halo = call(pack_kernel, [(m, used + 4 * m * half, lanes), (2, 2 * m) + brow], (u1, up_gy, u_gz, u_gx))
    back = lax.all_to_all(packed, "gy", 0, 0, tiled=True)
    result = call(
        last_kernel,
        (2, 2, m, half, rows, lanes),
        (back, own, halo, g, bx, by, bz, wr, wi),
        scratch=[(2 * m, pad) + plane, (2 * m, pad) + plane, (2 * m * used, lanes)],
    )
    last = lax.ppermute(result[1], "gz", swap)
    return call(gather_kernel, rhs.shape, (result[0], last))


def solution(mesh):
    sizes = dict(mesh.shape)

    def local(rhs, density, shift_real, shift_imag):
        _, m, xs, rows, lanes = rhs.shape
        planes = sizes["gz"] == 2 and sizes["gy"] == m and xs == 8 and rows % 16 == 0 and lanes == 128
        return (local_planes if planes else local_general)(rhs, density, shift_real, shift_imag)

    placed = (
        P(None, None, "gx", "gy", "gz"),
        P("gx", "gy", "gz"),
        P("gx", "gy", "gz"),
        P("gx", "gy", "gz"),
    )
    return jax.shard_map(
        local,
        mesh=mesh,
        in_specs=placed,
        out_specs=P(None, None, "gx", "gy", "gz"),
        check_vma=False,
    )
```

```python
import jax
import jax.numpy as jnp
from jax import lax
from jax.experimental import pallas as pl
from jax.experimental.pallas import tpu as pltpu
from jax.sharding import PartitionSpec as P

NU = 2
CSWEEPS = 4


omega_damp = 0.8


def padded(cells, sides, width):
    for axis, dim in sides:
        count = lax.axis_size(axis)
        ends = count - 1
        head = lax.slice_in_dim(cells, 0, width, axis=dim)
        tail = lax.slice_in_dim(cells, cells.shape[dim] - width, cells.shape[dim], axis=dim)
        cells = jnp.concatenate(
            [
                lax.ppermute(tail, axis, [(i, (i + 1) % count) for i in range(ends)]),
                cells,
                lax.ppermute(head, axis, [((i + 1) % count, i) for i in range(ends)]),
            ],
            axis=dim,
        )
    return cells


def face_coefs(rho_pad):
    center = rho_pad[1:-1, 1:-1, 1:-1]
    others = [
        rho_pad[2:, 1:-1, 1:-1],
        rho_pad[:-2, 1:-1, 1:-1],
        rho_pad[1:-1, 2:, 1:-1],
        rho_pad[1:-1, :-2, 1:-1],
        rho_pad[1:-1, 1:-1, 2:],
        rho_pad[1:-1, 1:-1, :-2],
    ]
    result = []
    for other in others:
        total = center + other
        result.append(2.0 / jnp.where(total > 0.0, total, 1.0))
    return result


def make_level(rho_pad, shift_re, shift_im, scale):
    coefs = face_coefs(rho_pad)
    bsum = coefs[0] + coefs[1] + coefs[2] + coefs[3] + coefs[4] + coefs[5]
    diag_re = scale * bsum - shift_re
    diag_im = -shift_im
    magnitude = diag_re * diag_re + diag_im * diag_im
    return (coefs, bsum, shift_re, shift_im, scale, diag_re / magnitude, -diag_im / magnitude)


def apply_op(upad, level):
    coefs, bsum, shift_re, shift_im, scale, inv_re, inv_im = level
    center = upad[:, :, 1:-1, 1:-1, 1:-1]
    nbsum = coefs[0] * upad[:, :, 2:, 1:-1, 1:-1] + coefs[1] * upad[:, :, :-2, 1:-1, 1:-1]
    nbsum = nbsum + coefs[2] * upad[:, :, 1:-1, 2:, 1:-1] + coefs[3] * upad[:, :, 1:-1, :-2, 1:-1]
    nbsum = nbsum + coefs[4] * upad[:, :, 1:-1, 1:-1, 2:] + coefs[5] * upad[:, :, 1:-1, 1:-1, :-2]
    lap = scale * (bsum * center - nbsum)
    out_re = lap[0] - shift_re * center[0] + shift_im * center[1]
    out_im = lap[1] - shift_re * center[1] - shift_im * center[0]
    return jnp.stack([out_re, out_im])


def precondition(resid, level):
    inv_re, inv_im = (level[5], level[6])
    upd_re = inv_re * resid[0] - inv_im * resid[1]
    upd_im = inv_re * resid[1] + inv_im * resid[0]
    return omega_damp * jnp.stack([upd_re, upd_im])


def smooth(field, target, level, padder, count):
    for sweep in range(count):
        field = field + precondition(target - apply_op(padder(field), level), level)
    return field


def restrict(field):
    lead = field.shape[:-3]
    sx, sy, sz = field.shape[-3:]
    blocks = field.reshape(lead + (sx // 2, 2, sy // 2, 2, sz // 2, 2))
    return jnp.mean(blocks, axis=(-5, -3, -1))


def prolong(field):
    return jnp.repeat(jnp.repeat(jnp.repeat(field, 2, -3), 2, -2), 2, -1)


def field_pad(field):
    return padded(field, (("gx", 2), ("gy", 3), ("gz", 4)), 1)


def brick_density(rho):
    return padded(rho, (("gx", 0), ("gy", 1), ("gz", 2)), 1)


def local_general(rhs, density, shift_real, shift_imag):
    rho1, sr1, si1 = (restrict(density), restrict(shift_real), restrict(shift_imag))
    level1 = make_level(brick_density(rho1), sr1, si1, 0.25)
    rho2, sr2, si2 = (restrict(rho1), restrict(sr1), restrict(si1))
    level0 = make_level(brick_density(density), shift_real, shift_imag, 1.0)
    fine = precondition(rhs, level0)
    fine = smooth(fine, rhs, level0, field_pad, NU - 1)
    coarse_rhs = restrict(rhs - apply_op(field_pad(fine), level0))
    middle = precondition(coarse_rhs, level1)
    middle = smooth(middle, coarse_rhs, level1, field_pad, NU - 1)
    lowest_rhs = restrict(coarse_rhs - apply_op(field_pad(middle), level1))
    level2 = make_level(brick_density(rho2), sr2, si2, 0.0625)
    lowest = precondition(lowest_rhs, level2)
    lowest = smooth(lowest, lowest_rhs, level2, field_pad, CSWEEPS - 1)
    middle = smooth(middle + prolong(lowest), coarse_rhs, level1, field_pad, NU)
    corrected = fine + prolong(middle)
    return smooth(corrected, rhs, level0, field_pad, NU)


HALO = 2
SIDE = 4
MIB = 1 << 20
COARSE_COST = 5 * 10**9
NEAR_COST = 2 * 10**9
F32 = jnp.float32


def loop(count, body):
    lax.fori_loop(0, count, lambda i, c: (body(i), c)[1], 0)


def safe(total):
    return jnp.where(total > 0.0, total, 1.0)


def level_coefs(rho, sr, si, scale, bx, by, bz, wr, wi, dr, step, start, count):
    ny, nz = sr.shape[1:]
    two = 2.0 * scale
    bx[pl.ds(start, 1)] = two / safe(rho[pl.ds(start, 1)] + rho[pl.ds(start + 1, 1)])

    def body(i):
        p = start + i * step
        r = rho[pl.ds(p + 1, step)]
        row = lax.broadcasted_iota(jnp.int32, r.shape, 1)
        lane = lax.broadcasted_iota(jnp.int32, r.shape, 2)
        bx[pl.ds(p + 1, step)] = two / safe(r + rho[pl.ds(p + 2, step)])
        edge = two / safe(r)
        bsum = bx[pl.ds(p, step)] + bx[pl.ds(p + 1, step)]
        last = row == ny - 1
        up = jnp.where(last, 0.0, pltpu.roll(r, ny - 1, 1))
        face = two / safe(r + up)
        bsum = bsum + face + jnp.where(row == 0, edge, pltpu.roll(face, 1, 1))
        by[pl.ds(p, step)] = jnp.where(last, 0.0, face)
        last = lane == nz - 1
        up = jnp.where(last, 0.0, pltpu.roll(r, nz - 1, 2))
        face = two / safe(r + up)
        bsum = bsum + face + jnp.where(lane == 0, edge, pltpu.roll(face, 1, 2))
        bz[pl.ds(p, step)] = jnp.where(last, 0.0, face)
        d = bsum - sr[pl.ds(p, step)]
        e = si[pl.ds(p, step)]
        w = jnp.where(r > 0.0, omega_damp, 0.0) / (d * d + e * e)
        wr[pl.ds(p, step)] = w * d
        wi[pl.ds(p, step)] = w * e
        dr[pl.ds(p, step)] = d

    loop(count // step, body)


def near(u, f, at, p, step, bx, by, bz):
    mid = u[f, pl.ds(at, step)]
    ny, nz = mid.shape[1:]
    b = by[pl.ds(p, step)]
    total = bx[pl.ds(p, step)] * u[f, pl.ds(at - 1, step)] + bx[pl.ds(p + 1, step)] * u[f, pl.ds(at + 1, step)]
    total = total + (b * pltpu.roll(mid, ny - 1, 1) + pltpu.roll(b * mid, 1, 1))
    b = bz[pl.ds(p, step)]
    return mid, total + (b * pltpu.roll(mid, nz - 1, 2) + pltpu.roll(b * mid, 1, 2))


def weigh(tr, ti, p, step, wr, wi):
    a, b = wr[pl.ds(p, step)], wi[pl.ds(p, step)]
    return a * tr - b * ti, a * ti + b * tr


def sweep_planes(u, fields, at, g, gat, p, step, coefs):
    bx, by, bz, wr, wi = coefs
    re, im = fields
    mr, nr = near(u, re, at, p, step, bx, by, bz)
    mi, ni = near(u, im, at, p, step, bx, by, bz)
    vr, vi = weigh(g[re, pl.ds(gat, step)] + nr, g[im, pl.ds(gat, step)] + ni, p, step, wr, wi)
    rest = 1.0 - omega_damp
    return rest * mr + vr, rest * mi + vi


def resid_planes(u, fields, at, g, gat, p, step, coefs, dr, si):
    bx, by, bz = coefs[:3]
    re, im = fields
    mr, nr = near(u, re, at, p, step, bx, by, bz)
    mi, ni = near(u, im, at, p, step, bx, by, bz)
    d, e = dr[pl.ds(p, step)], si[pl.ds(p, step)]
    return g[re, pl.ds(gat, step)] + nr - (d * mr + e * mi), g[im, pl.ds(gat, step)] + ni - (d * mi - e * mr)


def pick(nrow, ncol, down, value):
    row = lax.broadcasted_iota(jnp.int32, (nrow, ncol), 0)
    col = lax.broadcasted_iota(jnp.int32, (nrow, ncol), 1)
    hit = (row // 2 == col) if down else (row == col // 2)
    return jnp.where(hit, value, 0.0).astype(F32)


def dot(a, b):
    return jnp.dot(a, b, precision=lax.Precision.HIGHEST, preferred_element_type=F32)


def send_kernel(rhs, rho, sr, si, away, kept, sems):
    half = away.shape[1]
    m = rhs.shape[1]
    k = lax.axis_index("gz")
    copies = []
    for n, (out, side) in enumerate(((away, 1 - k), (kept, k))):
        planes = pl.ds(side * half, half)
        pieces = [(rhs.at[c, :, planes], out.at[pl.ds(c * m, m)]) for c in range(2)]
        pieces += [(ref.at[planes], out.at[2 * m + j]) for j, ref in enumerate((rho, sr, si))]
        copies += [pltpu.make_async_copy(src, dst, sems.at[5 * n + j]) for j, (src, dst) in enumerate(pieces)]
    for copy in copies:
        copy.start()
    for copy in copies:
        copy.wait()


def rows_kernel(kept, came, to_even, to_odd, ends):
    y = lax.axis_index("gy")
    fields, half, rows, _ = kept.shape
    rho = fields - 3
    for t, ref in enumerate((kept, came)):
        for h in range(2):
            at = 0
            for f in range(fields):
                n = HALO + 1 if f == rho else HALO
                for i in range(half):
                    ends[h, t, at : at + n, :] = ref[f, i, (rows - n if h else 0) : (rows if h else n), :]
                    at += n
    even = lax.rem(y, 2)
    to_even[...] = ends[1 - even]
    to_odd[...] = ends[even]


def lay_kernel(kept, came, even, odd, g, rho, sr, si, to_gz, to_gx, ends):
    k = lax.axis_index("gz")
    y = lax.axis_index("gy")
    fields, half, rows, lanes = kept.shape
    m2 = fields - 3
    arrays = [g.at[f] for f in range(m2)] + [rho, sr, si]
    for f, ref in enumerate(arrays):
        first = HALO + 1 if f == m2 else HALO
        for i in range(half):
            ref[first + i] = jnp.zeros(ref.shape[1:], F32)
        for t, src in enumerate((kept, came)):
            z = k if t == 0 else 1 - k
            spot = pl.ds(pl.multiple_of(z * lanes, lanes), lanes)
            for i in range(half):
                ref[first + i, SIDE : SIDE + rows, spot] = src[f, i]
    ends[0] = even[...]
    ends[1] = odd[...]
    for high in range(2):
        there = jnp.where(y < lax.axis_size("gy") - 1, 1.0, 0.0) if high else jnp.where(y > 0, 1.0, 0.0)
        peer = lax.rem(y, 2) if high else 1 - lax.rem(y, 2)
        for z in range(2):
            slot = jnp.where(k == z, 0, 1)
            at = 0
            for f, ref in enumerate(arrays):
                n = HALO + 1 if f == m2 else HALO
                row = SIDE + rows if high else SIDE - n
                for i in range(half):
                    ref[n + i, row : row + n, z * lanes : (z + 1) * lanes] = ends[peer, slot, at : at + n, :] * there
                    at += n
    for out, up in ((to_gz, 1 - k), (to_gx, k)):
        two, three = HALO + up * (half - HALO), HALO + 1 + up * (half - HALO - 1)
        for j, ref in enumerate(arrays[:m2] + [sr, si]):
            out[HALO * j : HALO * (j + 1)] = ref[pl.ds(two, HALO)]
        out[HALO * (m2 + 2) :] = rho[pl.ds(three, HALO + 1)]


def side_planes(came, low, g, rho, sr, si, bx, by, bz, wr, wi, dr, ua, own, rest):
    m2, pad = g.shape[:2]
    m = m2 // 2
    half = pad - 2 * HALO
    two, three = low * (half + HALO), low * (half + HALO + 1)
    for j, ref in enumerate([g.at[f] for f in range(m2)] + [sr, si]):
        ref[pl.ds(two, HALO)] = came[HALO * j : HALO * (j + 1)]
    rho[pl.ds(three, HALO + 1)] = came[HALO * (m2 + 2) :]
    count = HALO + 1 if rest else pad - HALO - 1
    start = low * (pad - count)
    level_coefs(rho, sr, si, 1.0, bx, by, bz, wr, wi, dr, 1, start, count)

    def first(i):
        p = start + i
        for r in range(m):
            ua[r, pl.ds(p, 1)], ua[m + r, pl.ds(p, 1)] = weigh(g[r, pl.ds(p, 1)], g[m + r, pl.ds(p, 1)], p, 1, wr, wi)

    loop(count, first)
    done = HALO + 1 if rest else half - 1
    begin = low * (pad - 2 - done)

    def second(i):
        at = begin + i
        p = at + 1
        for r in range(m):
            own[r, pl.ds(at, 1)], own[m + r, pl.ds(at, 1)] = sweep_planes(ua, (r, m + r), p, g, p, p, 1, (bx, by, bz, wr, wi))

    loop(done, second)


def near_kernel(from_gz, _g, _rho, _sr, _si, *state):
    side_planes(from_gz, 1 - lax.axis_index("gz"), *state, False)


def fine_kernel(from_gx, *refs):
    g, rho, sr, si, bx, by, bz, wr, wi, dr, ua, own, up_gz, up_gx, up_gy, packed, left, right, narrow = refs[12:]
    k = lax.axis_index("gz")
    side_planes(from_gx, k, g, rho, sr, si, bx, by, bz, wr, wi, dr, ua, own, True)
    coefs = (bx, by, bz, wr, wi)
    m2, pad, ny, nz = g.shape
    m = m2 // 2
    half = pad - 2 * HALO
    rows = ny - 2 * SIDE
    lanes = nz // 2
    for f in range(m2):
        up_gz[f] = own[f, 2 + (1 - k) * (half - 3), SIDE : SIDE + rows, :]
        up_gx[f] = own[f, 2 + k * (half - 3), SIDE : SIDE + rows, :]
        for i in range(half):
            for h, row in enumerate((SIDE + 1, SIDE + rows - 2)):
                for z in range(2):
                    at = z * m2 * half + f * half + i
                    up_gy[h, at : at + 1, :] = own[f, i + 1, row : row + 1, z * lanes : (z + 1) * lanes]
    pairs = half // 2

    def down(q):
        p = HALO + 2 * q
        totals = {}
        for r in range(m):
            ar, ai = resid_planes(own, (r, m + r), p - 1, g, p, p, 1, coefs, dr, si)
            br, bi = resid_planes(own, (r, m + r), p, g, p + 1, p + 1, 1, coefs, dr, si)
            totals[r], totals[m + r] = ar + br, ai + bi
        totals[m2] = rho[pl.ds(p + 1, 1)] + rho[pl.ds(p + 2, 1)]
        for j, ref in ((m2 + 1, sr), (m2 + 2, si)):
            totals[j] = ref[pl.ds(p, 1)] + ref[pl.ds(p + 1, 1)]
        for j, v in totals.items():
            spot = pl.ds(pl.multiple_of((j * pairs + q) * ny, ny), ny)
            left[spot, :] = v[0, :, :lanes]
            right[spot, :] = v[0, :, lanes:]

    loop(pairs, down)
    n = (m2 + 3) * pairs * ny // 2
    both = [ref[pl.ds(0, n, 2), :] + ref[pl.ds(1, n, 2), :] for ref in (left, right)]
    narrow[...] = dot(jnp.concatenate(both, axis=1), pick(nz, lanes, True, 0.125))
    for q in range(pairs):
        done = []
        for j in range(m2 + 3):
            at = (j * pairs + q) * (ny // 2) + SIDE // 2
            done.append(narrow[at : at + rows // 2, :])
        for d in range(packed.shape[0]):
            r = d % m
            for a, j in enumerate((r, m + r, m2, m2 + 1, m2 + 2)):
                packed[d, a, q] = done[j]


def coarse_kernel(
    mine, other, out,
    rho1, sr1, si1, g1, bx1, by1, bz1, wr1, wi1, dr1, ua1, ub1,
    rho2, sr2, si2, g2, bx2, by2, bz2, wr2, wi2, dr2, ua2, ub2,
    sums, narrow, wide, tall,
):
    k = lax.axis_index("gz")
    chip = lax.axis_index("gx")
    _, _, pairs, rows, nz = mine.shape
    n1, ny = sr1.shape[:2]
    parts = ny // rows
    chips = mine.shape[0] // parts
    zero = jnp.zeros((1, ny, nz), F32)
    rho1[pl.ds(0, 1)] = zero
    rho1[pl.ds(n1 + 1, 1)] = zero
    for u in (ua1, ub1):
        for c in range(2):
            u[c, pl.ds(0, 1)] = zero
            u[c, pl.ds(n1 + 1, 1)] = zero
    for s in range(chips):
        for ref, z in ((mine, k), (other, 1 - k)):
            at = 2 * pairs * s + pairs * z
            for y in range(parts):
                spot = slice(y * rows, (y + 1) * rows)
                e = s * parts + y
                for c in range(2):
                    g1[c, pl.ds(at, pairs), spot] = ref[e, c]
                rho1[pl.ds(at + 1, pairs), spot] = ref[e, 2]
                sr1[pl.ds(at, pairs), spot] = ref[e, 3]
                si1[pl.ds(at, pairs), spot] = ref[e, 4]
    step1 = 4
    level_coefs(rho1, sr1, si1, 0.25, bx1, by1, bz1, wr1, wi1, dr1, step1, 0, n1)
    coefs1 = (bx1, by1, bz1, wr1, wi1)

    def first(i):
        p = i * step1
        r, m = weigh(g1[0, pl.ds(p, step1)], g1[1, pl.ds(p, step1)], p, step1, wr1, wi1)
        ua1[0, pl.ds(p + 1, step1)], ua1[1, pl.ds(p + 1, step1)] = r, m

    loop(n1 // step1, first)

    def sweep1(src, dst):
        def body(i):
            p = i * step1
            r, m = sweep_planes(src, (0, 1), p + 1, g1, p, p, step1, coefs1)
            dst[0, pl.ds(p + 1, step1)], dst[1, pl.ds(p + 1, step1)] = r, m

        loop(n1 // step1, body)

    sweep1(ua1, ub1)
    n2 = n1 // 2
    ny2 = ny // 2

    def down(q):
        p = 2 * q
        r, m = resid_planes(ub1, (0, 1), p + 1, g1, p, p, 2, coefs1, dr1, si1)
        totals = (r[0] + r[1], m[0] + m[1], rho1[p + 1] + rho1[p + 2], sr1[p] + sr1[p + 1], si1[p] + si1[p + 1])
        for j, v in enumerate(totals):
            sums[pl.ds(pl.multiple_of((j * n2 + q) * ny, ny), ny), :] = v

    loop(n2, down)
    narrow[...] = dot(sums[...], pick(nz, nz, True, 0.125))
    n = n2 * ny2
    zero2 = jnp.zeros((1, ny2, nz), F32)
    rho2[pl.ds(0, 1)] = zero2
    rho2[pl.ds(n2 + 1, 1)] = zero2
    for u in (ua2, ub2):
        for c in range(2):
            u[c, pl.ds(0, 1)] = zero2
            u[c, pl.ds(n2 + 1, 1)] = zero2
    for j, ref in enumerate((g2.at[0], g2.at[1], rho2.at[pl.ds(1, n2)], sr2, si2)):
        at = 2 * n * j
        ref[...] = (narrow[pl.ds(at, n, 2), :] + narrow[pl.ds(at + 1, n, 2), :]).reshape(n2, ny2, nz)
    level_coefs(rho2, sr2, si2, 0.0625, bx2, by2, bz2, wr2, wi2, dr2, n2, 0, n2)
    coefs2 = (bx2, by2, bz2, wr2, wi2)
    ua2[0, pl.ds(1, n2)], ua2[1, pl.ds(1, n2)] = weigh(g2[0], g2[1], 0, n2, wr2, wi2)
    src, dst = ua2, ub2
    for _ in range(CSWEEPS - 1):
        dst[0, pl.ds(1, n2)], dst[1, pl.ds(1, n2)] = sweep_planes(src, (0, 1), 1, g2, 0, 0, n2, coefs2)
        src, dst = dst, src

    widen = pick(nz, nz, False, 1.0)
    for c in range(2):
        wide[pl.ds(c * n, n), :] = dot(src[c, pl.ds(1, n2)].reshape(n, nz), widen)
    twice = wide[pl.ds(0, 2 * n), :]
    tall[pl.ds(0, 2 * n, 2), :] = twice
    tall[pl.ds(1, 2 * n, 2), :] = twice

    def lift(q):
        for c in range(2):
            v = tall[pl.ds(pl.multiple_of((c * n2 + q) * ny, ny), ny), :]
            for j in range(2):
                ub1[c, 2 * q + j + 1] = ub1[c, 2 * q + j + 1] + v

    loop(n2, lift)
    sweep1(ub1, ua1)
    sweep1(ua1, ub1)

    out[...] = ub1[:, pl.ds((2 * chip + k) * pairs, 2 + pairs)]


def pack_kernel(u1, up_gy, from_gz, from_gx, *refs):
    *outs, edges, blocks = refs
    k = lax.axis_index("gz")
    me = lax.axis_index("gy")
    edges[k] = from_gz[...]
    edges[1 - k] = from_gx[...]
    _, quads, ny, nz = u1.shape
    parts = len(outs)
    rows = ny // parts
    edge = SIDE // 2
    tall_rows = rows + 2 * edge
    for y in range(parts):
        low, high = max(y * rows - edge, 0), min((y + 1) * rows + edge, ny)
        for c in range(2):
            for q in range(quads):
                at = (c * quads + q) * tall_rows
                skip = low - (y * rows - edge)
                end = skip + high - low
                if skip:
                    blocks[y, at : at + skip, :] = jnp.zeros((skip, nz), F32)
                blocks[y, at + skip : at + end, :] = u1[c, q, low:high, :]
                if end < tall_rows:
                    blocks[y, at + end : at + tall_rows, :] = jnp.zeros((tall_rows - end, nz), F32)
    used = 2 * quads * tall_rows
    for v, out in enumerate(outs):
        out[:used, :] = blocks[me ^ v]
        out[used:, :] = up_gy[jnp.where(me < (me ^ v), 1, 0)]


def last_kernel(*refs):
    *back, own, edges, g, bx, by, bz, wr, wi, out, ua, ub, tall, flat = refs
    k = lax.axis_index("gz")
    y = lax.axis_index("gy")
    m2, pad, ny, nz = ua.shape
    m = m2 // 2
    half = pad - 2 * HALO
    rows = ny - 2 * SIDE
    quads = pad // 2
    lanes = nz // 2
    ua[:, pl.ds(1, pad - 2)] = own[...]
    blank = jnp.zeros((m2, ny, nz), F32)
    for p, side in ((0, 1), (pad - 1, 0)):
        ua[:, p] = blank
        ua[:, p, SIDE : SIDE + rows, :] = edges[side]
    used = 2 * quads * ny // 2
    for v, ref in enumerate(back):
        flat[y ^ v] = ref[...]
    for high in range(2):
        there = jnp.where(y < m - 1, 1.0, 0.0) if high else jnp.where(y > 0, 1.0, 0.0)
        peer = jnp.minimum(y + 1, m - 1) if high else jnp.maximum(y - 1, 0)
        row = SIDE + rows + 1 if high else SIDE - 2
        block = flat[peer, used:, :] * there
        for z in range(2):
            for f in range(m2):
                for i in range(half):
                    at = z * m2 * half + f * half + i
                    ua[f, HALO + i, row : row + 1, z * lanes : (z + 1) * lanes] = block[at : at + 1, :]
    u1 = flat[:, :used, :].reshape(m * used, lanes)
    for h in range(2):
        col = lax.broadcasted_iota(jnp.int32, (lanes, lanes), 1) + h * lanes
        line = lax.broadcasted_iota(jnp.int32, (lanes, lanes), 0)
        v = dot(u1, jnp.where(line == col // 2, 1.0, 0.0).astype(F32))
        tall[pl.ds(0, m * used, 2), :] = v
        tall[pl.ds(1, m * used, 2), :] = v
        spot = slice(h * lanes, (h + 1) * lanes)
        for r in range(m):
            for c in range(2):
                for q in range(quads):
                    at = ((r * 2 + c) * quads + q) * ny
                    w = tall[at : at + ny, :]
                    f = c * m + r
                    for j in range(2):
                        ua[f, 2 * q + j, :, spot] = ua[f, 2 * q + j, :, spot] + w
    coefs = (bx, by, bz, wr, wi)

    def third(i):
        p = i + 1
        for r in range(m):
            ub[r, pl.ds(p, 1)], ub[m + r, pl.ds(p, 1)] = sweep_planes(ua, (r, m + r), p, g, p, p, 1, coefs)

    loop(pad - 2, third)

    def fourth(i):
        p = i + HALO
        for r in range(m):
            for c, v in enumerate(sweep_planes(ub, (r, m + r), p, g, p, p, 1, coefs)):
                for z in range(2):
                    slot = jnp.where(k == z, 0, 1)
                    out[slot, c, r, i] = v[0, SIDE : SIDE + rows, z * lanes : (z + 1) * lanes]

    loop(half, fourth)


def gather_kernel(kept, came, out):
    k = lax.axis_index("gz")
    half = kept.shape[2]
    for side, ref in ((k, kept), (1 - k, came)):
        for c in range(2):
            for r in range(kept.shape[1]):
                out[c, r, pl.ds(side * half, half)] = ref[c, r]


def call(kernel, outs, args, scratch=(), limit=14, space=pltpu.VMEM, sems=None, cost=None, aliases=None):
    single = not isinstance(outs, list)
    shapes = [outs] if single else outs
    result = pl.pallas_call(
        kernel,
        out_shape=[jax.ShapeDtypeStruct(s, F32) for s in shapes],
        in_specs=[pl.BlockSpec(memory_space=space)] * len(args),
        out_specs=[pl.BlockSpec(memory_space=pltpu.VMEM)] * len(shapes),
        scratch_shapes=[pltpu.VMEM(s, F32) for s in scratch] + ([pltpu.SemaphoreType.DMA((sems,))] if sems else []),
        compiler_params=pltpu.CompilerParams(vmem_limit_bytes=limit * MIB),
        input_output_aliases=aliases or {},
        cost_estimate=cost and pl.CostEstimate(flops=cost, bytes_accessed=0, transcendentals=0),
    )(*args)
    return result[0] if single else result


def local_planes(rhs, density, shift_real, shift_imag):
    _, m, xs, rows, lanes = rhs.shape
    half = xs // 2
    chips = lax.axis_size("gx")
    ny, nz = rows * m, 2 * lanes
    pad = half + 2 * HALO
    swap = [(0, 1), (1, 0)]
    ends = [p for c in range(chips - 1) for p in ((2 * c + 1, 2 * c + 2), (2 * c + 2, 2 * c + 1))]
    fields = (rhs, density, shift_real, shift_imag)

    own_half = (2 * m + 3, half, rows, lanes)
    placed = tuple(pltpu.with_memory_space_constraint(f, pltpu.HBM) for f in fields)
    away, kept = call(send_kernel, [own_half, own_half], placed, space=pltpu.HBM, sems=10)
    came = lax.ppermute(away, "gz", swap)
    rim = ((2 * m + 3) * HALO + 1) * half
    rim = (2, -(-rim // 8) * 8, lanes)
    to_even, to_odd = call(rows_kernel, [rim, rim], (kept, came), scratch=[(2,) + rim])
    even = lax.ppermute(to_even, "gy", [(i, i ^ 1) for i in range(m)])
    odd = lax.ppermute(to_odd, "gy", [(i, (i + 2 * (i % 2) - 1) % m) for i in range(m)])

    plane = (rows + 2 * SIDE, nz)
    laid = [(2 * m, pad) + plane, (pad + 2,) + plane, (pad,) + plane, (pad,) + plane]
    edges = (HALO * (2 * m + 2) + HALO + 1,) + plane
    *state, to_gz, to_gx = call(lay_kernel, laid + [edges, edges], (kept, came, even, odd), scratch=[(2,) + rim])
    from_gx = lax.ppermute(to_gx, ("gx", "gz"), ends)
    from_gz = lax.ppermute(to_gz, "gz", swap)

    pairs = half // 2
    brow = (rows, nz)
    tall0 = (2 * m + 3) * pairs * plane[0]
    full = laid + [(pad + 1,) + plane] + [(pad,) + plane] * 5 + [(2 * m, pad) + plane, (2 * m, pad - 2) + plane]
    state = call(near_kernel, full, (from_gz, *state), aliases={i + 1: i for i in range(len(laid))}, cost=NEAR_COST)
    g, _, _, _, bx, by, bz, wr, wi, _, _, own, up_gz, up_gx, up_gy, packed = call(
        fine_kernel,
        full + [(2 * m,) + brow, (2 * m,) + brow, (2, 4 * m * half, lanes), (chips * m, 5, pairs, rows // 2, lanes)],
        (from_gx, *state),
        scratch=[(tall0, lanes), (tall0, lanes), (tall0 // 2, lanes)],
        aliases={i + 1: i for i in range(len(full))},
    )
    u_gx = lax.ppermute(up_gx, ("gx", "gz"), ends)
    u_gz = lax.ppermute(up_gz, "gz", swap)
    mine = lax.all_to_all(packed, ("gx", "gy"), 0, 0, tiled=True)
    other = lax.ppermute(mine, "gz", swap)

    n1, n2 = chips * xs // 2, chips * xs // 4
    p1, p2 = (ny // 2, nz // 2), (ny // 4, nz // 2)

    def level(n, p):
        return [(n + 2,) + p, (n,) + p, (n,) + p, (2, n) + p, (n + 1,) + p] + [(n,) + p] * 5 + [(2, n + 2) + p] * 2

    used = (2 + pairs) * plane[0]
    u1 = call(
        coarse_kernel,
        (2, 2 + pairs) + p1,
        (mine, other),
        scratch=level(n1, p1) + level(n2, p2) + [(5 * n2 * p1[0], p1[1])] * 2 + [(2 * n2 * p2[0], p1[1]), (2 * n2 * p1[0], p1[1])],
        limit=14,
        cost=COARSE_COST,
    )
    block = (used + 4 * m * half, lanes)
    *blocks, halo = call(pack_kernel, [block] * m + [(2, 2 * m) + brow], (u1, up_gy, u_gz, u_gx), scratch=[(m, used, lanes)])
    back = [lax.ppermute(b, "gy", [(i, i ^ v) for i in range(m)]) if v else b for v, b in enumerate(blocks)]
    result = call(
        last_kernel,
        (2, 2, m, half, rows, lanes),
        (*back, own, halo, g, bx, by, bz, wr, wi),
        scratch=[(2 * m, pad) + plane, (2 * m, pad) + plane, (2 * m * used, lanes), (m,) + block],
    )
    last = lax.ppermute(result[1], "gz", swap)
    return call(gather_kernel, rhs.shape, (result[0], last))


def solution(mesh):
    sizes = dict(mesh.shape)

    def local(rhs, density, shift_real, shift_imag):
        _, m, xs, rows, lanes = rhs.shape
        planes = sizes["gz"] == 2 and sizes["gy"] == m == 4 and xs == 8 and rows % 16 == 0 and lanes == 128
        return (local_planes if planes else local_general)(rhs, density, shift_real, shift_imag)

    placed = (
        P(None, None, "gx", "gy", "gz"),
        P("gx", "gy", "gz"),
        P("gx", "gy", "gz"),
        P("gx", "gy", "gz"),
    )
    return jax.shard_map(
        local,
        mesh=mesh,
        in_specs=placed,
        out_specs=P(None, None, "gx", "gy", "gz"),
        check_vma=False,
    )
```

```python
import functools

import jax
import jax.numpy as jnp
from jax import lax
from jax.experimental import pallas as pl
from jax.experimental.pallas import tpu as pltpu
from jax.sharding import PartitionSpec as P

NU = 2
CSWEEPS = 4


omega_damp = 0.8


def padded(cells, sides, width):
    for axis, dim in sides:
        count = lax.axis_size(axis)
        ends = count - 1
        head = lax.slice_in_dim(cells, 0, width, axis=dim)
        tail = lax.slice_in_dim(cells, cells.shape[dim] - width, cells.shape[dim], axis=dim)
        cells = jnp.concatenate(
            [
                lax.ppermute(tail, axis, [(i, (i + 1) % count) for i in range(ends)]),
                cells,
                lax.ppermute(head, axis, [((i + 1) % count, i) for i in range(ends)]),
            ],
            axis=dim,
        )
    return cells


def face_coefs(rho_pad):
    center = rho_pad[1:-1, 1:-1, 1:-1]
    others = [
        rho_pad[2:, 1:-1, 1:-1],
        rho_pad[:-2, 1:-1, 1:-1],
        rho_pad[1:-1, 2:, 1:-1],
        rho_pad[1:-1, :-2, 1:-1],
        rho_pad[1:-1, 1:-1, 2:],
        rho_pad[1:-1, 1:-1, :-2],
    ]
    result = []
    for other in others:
        total = center + other
        result.append(2.0 / jnp.where(total > 0.0, total, 1.0))
    return result


def make_level(rho_pad, shift_re, shift_im, scale):
    coefs = face_coefs(rho_pad)
    bsum = coefs[0] + coefs[1] + coefs[2] + coefs[3] + coefs[4] + coefs[5]
    diag_re = scale * bsum - shift_re
    diag_im = -shift_im
    magnitude = diag_re * diag_re + diag_im * diag_im
    return (coefs, bsum, shift_re, shift_im, scale, diag_re / magnitude, -diag_im / magnitude)


def apply_op(upad, level):
    coefs, bsum, shift_re, shift_im, scale, inv_re, inv_im = level
    center = upad[:, :, 1:-1, 1:-1, 1:-1]
    nbsum = coefs[0] * upad[:, :, 2:, 1:-1, 1:-1] + coefs[1] * upad[:, :, :-2, 1:-1, 1:-1]
    nbsum = nbsum + coefs[2] * upad[:, :, 1:-1, 2:, 1:-1] + coefs[3] * upad[:, :, 1:-1, :-2, 1:-1]
    nbsum = nbsum + coefs[4] * upad[:, :, 1:-1, 1:-1, 2:] + coefs[5] * upad[:, :, 1:-1, 1:-1, :-2]
    lap = scale * (bsum * center - nbsum)
    out_re = lap[0] - shift_re * center[0] + shift_im * center[1]
    out_im = lap[1] - shift_re * center[1] - shift_im * center[0]
    return jnp.stack([out_re, out_im])


def precondition(resid, level):
    inv_re, inv_im = (level[5], level[6])
    upd_re = inv_re * resid[0] - inv_im * resid[1]
    upd_im = inv_re * resid[1] + inv_im * resid[0]
    return omega_damp * jnp.stack([upd_re, upd_im])


def smooth(field, target, level, padder, count):
    for sweep in range(count):
        field = field + precondition(target - apply_op(padder(field), level), level)
    return field


def restrict(field):
    lead = field.shape[:-3]
    sx, sy, sz = field.shape[-3:]
    blocks = field.reshape(lead + (sx // 2, 2, sy // 2, 2, sz // 2, 2))
    return jnp.mean(blocks, axis=(-5, -3, -1))


def prolong(field):
    return jnp.repeat(jnp.repeat(jnp.repeat(field, 2, -3), 2, -2), 2, -1)


def field_pad(field):
    return padded(field, (("gx", 2), ("gy", 3), ("gz", 4)), 1)


def brick_density(rho):
    return padded(rho, (("gx", 0), ("gy", 1), ("gz", 2)), 1)


def local_general(rhs, density, shift_real, shift_imag):
    rho1, sr1, si1 = (restrict(density), restrict(shift_real), restrict(shift_imag))
    level1 = make_level(brick_density(rho1), sr1, si1, 0.25)
    rho2, sr2, si2 = (restrict(rho1), restrict(sr1), restrict(si1))
    level0 = make_level(brick_density(density), shift_real, shift_imag, 1.0)
    fine = precondition(rhs, level0)
    fine = smooth(fine, rhs, level0, field_pad, NU - 1)
    coarse_rhs = restrict(rhs - apply_op(field_pad(fine), level0))
    middle = precondition(coarse_rhs, level1)
    middle = smooth(middle, coarse_rhs, level1, field_pad, NU - 1)
    lowest_rhs = restrict(coarse_rhs - apply_op(field_pad(middle), level1))
    level2 = make_level(brick_density(rho2), sr2, si2, 0.0625)
    lowest = precondition(lowest_rhs, level2)
    lowest = smooth(lowest, lowest_rhs, level2, field_pad, CSWEEPS - 1)
    middle = smooth(middle + prolong(lowest), coarse_rhs, level1, field_pad, NU)
    corrected = fine + prolong(middle)
    return smooth(corrected, rhs, level0, field_pad, NU)


HALO = 2
SIDE = 4
MIB = 1 << 20
COARSE_COST = 5 * 10**9
NEAR_COST = 2 * 10**9
F32 = jnp.float32


def loop(count, body):
    lax.fori_loop(0, count, lambda i, c: (body(i), c)[1], 0)


def safe(total):
    return jnp.where(total > 0.0, total, 1.0)


def level_coefs(rho, sr, si, scale, bx, by, bz, wr, wi, dr, step, start, count):
    ny, nz = sr.shape[1:]
    two = 2.0 * scale
    bx[pl.ds(start, 1)] = two / safe(rho[pl.ds(start, 1)] + rho[pl.ds(start + 1, 1)])

    def body(i):
        p = start + i * step
        r = rho[pl.ds(p + 1, step)]
        row = lax.broadcasted_iota(jnp.int32, r.shape, 1)
        lane = lax.broadcasted_iota(jnp.int32, r.shape, 2)
        bx[pl.ds(p + 1, step)] = two / safe(r + rho[pl.ds(p + 2, step)])
        edge = two / safe(r)
        bsum = bx[pl.ds(p, step)] + bx[pl.ds(p + 1, step)]
        last = row == ny - 1
        up = jnp.where(last, 0.0, pltpu.roll(r, ny - 1, 1))
        face = two / safe(r + up)
        bsum = bsum + face + jnp.where(row == 0, edge, pltpu.roll(face, 1, 1))
        by[pl.ds(p, step)] = jnp.where(last, 0.0, face)
        last = lane == nz - 1
        up = jnp.where(last, 0.0, pltpu.roll(r, nz - 1, 2))
        face = two / safe(r + up)
        bsum = bsum + face + jnp.where(lane == 0, edge, pltpu.roll(face, 1, 2))
        bz[pl.ds(p, step)] = jnp.where(last, 0.0, face)
        d = bsum - sr[pl.ds(p, step)]
        e = si[pl.ds(p, step)]
        w = jnp.where(r > 0.0, omega_damp, 0.0) / (d * d + e * e)
        wr[pl.ds(p, step)] = w * d
        wi[pl.ds(p, step)] = w * e
        dr[pl.ds(p, step)] = d

    loop(count // step, body)


def near(u, f, at, p, step, bx, by, bz):
    mid = u[f, pl.ds(at, step)]
    ny, nz = mid.shape[1:]
    b = by[pl.ds(p, step)]
    total = bx[pl.ds(p, step)] * u[f, pl.ds(at - 1, step)] + bx[pl.ds(p + 1, step)] * u[f, pl.ds(at + 1, step)]
    total = total + (b * pltpu.roll(mid, ny - 1, 1) + pltpu.roll(b * mid, 1, 1))
    b = bz[pl.ds(p, step)]
    return mid, total + (b * pltpu.roll(mid, nz - 1, 2) + pltpu.roll(b * mid, 1, 2))


def weigh(tr, ti, p, step, wr, wi):
    a, b = wr[pl.ds(p, step)], wi[pl.ds(p, step)]
    return a * tr - b * ti, a * ti + b * tr


def sweep_planes(u, fields, at, g, gat, p, step, coefs):
    bx, by, bz, wr, wi = coefs
    re, im = fields
    mr, nr = near(u, re, at, p, step, bx, by, bz)
    mi, ni = near(u, im, at, p, step, bx, by, bz)
    vr, vi = weigh(g[re, pl.ds(gat, step)] + nr, g[im, pl.ds(gat, step)] + ni, p, step, wr, wi)
    rest = 1.0 - omega_damp
    return rest * mr + vr, rest * mi + vi


def resid_planes(u, fields, at, g, gat, p, step, coefs, dr, si):
    bx, by, bz = coefs[:3]
    re, im = fields
    mr, nr = near(u, re, at, p, step, bx, by, bz)
    mi, ni = near(u, im, at, p, step, bx, by, bz)
    d, e = dr[pl.ds(p, step)], si[pl.ds(p, step)]
    return g[re, pl.ds(gat, step)] + nr - (d * mr + e * mi), g[im, pl.ds(gat, step)] + ni - (d * mi - e * mr)


def pick(nrow, ncol, down, value):
    row = lax.broadcasted_iota(jnp.int32, (nrow, ncol), 0)
    col = lax.broadcasted_iota(jnp.int32, (nrow, ncol), 1)
    hit = (row // 2 == col) if down else (row == col // 2)
    return jnp.where(hit, value, 0.0).astype(F32)


def dot(a, b):
    return jnp.dot(a, b, precision=lax.Precision.HIGHEST, preferred_element_type=F32)


def send_kernel(rhs, rho, sr, si, away, kept, sems):
    half = away.shape[1]
    m = rhs.shape[1]
    k = lax.axis_index("gz")
    copies = []
    for n, (out, side) in enumerate(((away, 1 - k), (kept, k))):
        planes = pl.ds(side * half, half)
        pieces = [(rhs.at[c, :, planes], out.at[pl.ds(c * m, m)]) for c in range(2)]
        pieces += [(ref.at[planes], out.at[2 * m + j]) for j, ref in enumerate((rho, sr, si))]
        copies += [pltpu.make_async_copy(src, dst, sems.at[5 * n + j]) for j, (src, dst) in enumerate(pieces)]
    for copy in copies:
        copy.start()
    for copy in copies:
        copy.wait()


def rows_kernel(kept, came, to_even, to_odd, ends):
    y = lax.axis_index("gy")
    fields, half, rows, _ = kept.shape
    rho = fields - 3
    for t, ref in enumerate((kept, came)):
        for h in range(2):
            at = 0
            for f in range(fields):
                n = HALO + 1 if f == rho else HALO
                for i in range(half):
                    ends[h, t, at : at + n, :] = ref[f, i, (rows - n if h else 0) : (rows if h else n), :]
                    at += n
    even = lax.rem(y, 2)
    to_even[...] = ends[1 - even]
    to_odd[...] = ends[even]


def means_kernel(kept, came, out, slots, sums):
    k = lax.axis_index("gz")
    fields, half, rows, lanes = kept.shape
    pairs = half // 2
    for t, ref in enumerate((kept, came)):
        for j in range(3):
            for q in range(pairs):
                at = (j * pairs + q) * rows
                slots[at : at + rows, :] = ref[fields - 3 + j, 2 * q] + ref[fields - 3 + j, 2 * q + 1]
        n = 3 * pairs * rows // 2
        sums[t] = slots[pl.ds(0, n, 2), :] + slots[pl.ds(1, n, 2), :]
    done = dot(jnp.concatenate([sums[k], sums[1 - k]], axis=1), pick(2 * lanes, lanes, True, 0.125))
    out[...] = done.reshape(3, pairs, rows // 2, lanes)


def join(axis, parts, out):
    me = lax.axis_index(axis)
    n = out.shape[0] // len(parts)
    for v, ref in enumerate(parts):
        out[pl.ds((me ^ v) * n, n)] = ref[...].reshape((n,) + out.shape[1:])


def lay_kernel(kept, came, even, odd, *refs):
    *means, g, rho, sr, si, to_gz, to_gx, joined, ends = refs
    join("gx", means, joined)
    k = lax.axis_index("gz")
    y = lax.axis_index("gy")
    fields, half, rows, lanes = kept.shape
    m2 = fields - 3
    arrays = [g.at[f] for f in range(m2)] + [rho, sr, si]
    for f, ref in enumerate(arrays):
        first = HALO + 1 if f == m2 else HALO
        for i in range(half):
            ref[first + i] = jnp.zeros(ref.shape[1:], F32)
        for t, src in enumerate((kept, came)):
            z = k if t == 0 else 1 - k
            spot = pl.ds(pl.multiple_of(z * lanes, lanes), lanes)
            for i in range(half):
                ref[first + i, SIDE : SIDE + rows, spot] = src[f, i]
    ends[0] = even[...]
    ends[1] = odd[...]
    for high in range(2):
        there = jnp.where(y < lax.axis_size("gy") - 1, 1.0, 0.0) if high else jnp.where(y > 0, 1.0, 0.0)
        peer = lax.rem(y, 2) if high else 1 - lax.rem(y, 2)
        for z in range(2):
            slot = jnp.where(k == z, 0, 1)
            at = 0
            for f, ref in enumerate(arrays):
                n = HALO + 1 if f == m2 else HALO
                row = SIDE + rows if high else SIDE - n
                for i in range(half):
                    ref[n + i, row : row + n, z * lanes : (z + 1) * lanes] = ends[peer, slot, at : at + n, :] * there
                    at += n
    for out, up in ((to_gz, 1 - k), (to_gx, k)):
        two, three = HALO + up * (half - HALO), HALO + 1 + up * (half - HALO - 1)
        for j, ref in enumerate(arrays[:m2] + [sr, si]):
            out[HALO * j : HALO * (j + 1)] = ref[pl.ds(two, HALO)]
        out[HALO * (m2 + 2) :] = rho[pl.ds(three, HALO + 1)]


def side_planes(came, low, g, rho, sr, si, bx, by, bz, wr, wi, dr, ua, own, rest):
    m2, pad = g.shape[:2]
    m = m2 // 2
    half = pad - 2 * HALO
    two, three = low * (half + HALO), low * (half + HALO + 1)
    for j, ref in enumerate([g.at[f] for f in range(m2)] + [sr, si]):
        ref[pl.ds(two, HALO)] = came[HALO * j : HALO * (j + 1)]
    rho[pl.ds(three, HALO + 1)] = came[HALO * (m2 + 2) :]
    count = HALO + 1 if rest else pad - HALO - 1
    start = low * (pad - count)
    level_coefs(rho, sr, si, 1.0, bx, by, bz, wr, wi, dr, 1, start, count)

    def first(i):
        p = start + i
        for r in range(m):
            ua[r, pl.ds(p, 1)], ua[m + r, pl.ds(p, 1)] = weigh(g[r, pl.ds(p, 1)], g[m + r, pl.ds(p, 1)], p, 1, wr, wi)

    loop(count, first)
    done = HALO + 1 if rest else half - 1
    begin = low * (pad - 2 - done)

    def second(i):
        at = begin + i
        p = at + 1
        for r in range(m):
            own[r, pl.ds(at, 1)], own[m + r, pl.ds(at, 1)] = sweep_planes(ua, (r, m + r), p, g, p, p, 1, (bx, by, bz, wr, wi))

    loop(done, second)


def near_kernel(from_gz, _g, _rho, _sr, _si, *refs):
    means, *state, out = refs
    out[...] = means[...]
    side_planes(from_gz, 1 - lax.axis_index("gz"), *state, False)


def fine_kernel(from_gx, *refs):
    g, rho, sr, si, bx, by, bz, wr, wi, dr, ua, own, up_gz, up_gx, up_gy, packed, joined, left, right, narrow = refs[-20:]
    join("gy", refs[12:-20], joined)
    k = lax.axis_index("gz")
    side_planes(from_gx, k, g, rho, sr, si, bx, by, bz, wr, wi, dr, ua, own, True)
    coefs = (bx, by, bz, wr, wi)
    m2, pad, ny, nz = g.shape
    m = m2 // 2
    half = pad - 2 * HALO
    rows = ny - 2 * SIDE
    lanes = nz // 2
    for f in range(m2):
        up_gz[f] = own[f, 2 + (1 - k) * (half - 3), SIDE : SIDE + rows, :]
        up_gx[f] = own[f, 2 + k * (half - 3), SIDE : SIDE + rows, :]
        for i in range(half):
            for h, row in enumerate((SIDE + 1, SIDE + rows - 2)):
                for z in range(2):
                    at = z * m2 * half + f * half + i
                    up_gy[h, at : at + 1, :] = own[f, i + 1, row : row + 1, z * lanes : (z + 1) * lanes]
    pairs = half // 2

    def down(q):
        p = HALO + 2 * q
        totals = {}
        for r in range(m):
            ar, ai = resid_planes(own, (r, m + r), p - 1, g, p, p, 1, coefs, dr, si)
            br, bi = resid_planes(own, (r, m + r), p, g, p + 1, p + 1, 1, coefs, dr, si)
            totals[r], totals[m + r] = ar + br, ai + bi
        for j, v in totals.items():
            spot = pl.ds(pl.multiple_of((j * pairs + q) * ny, ny), ny)
            left[spot, :] = v[0, :, :lanes]
            right[spot, :] = v[0, :, lanes:]

    loop(pairs, down)
    n = m2 * pairs * ny // 2
    both = [ref[pl.ds(0, n, 2), :] + ref[pl.ds(1, n, 2), :] for ref in (left, right)]
    narrow[...] = dot(jnp.concatenate(both, axis=1), pick(nz, lanes, True, 0.125))
    for q in range(pairs):
        done = []
        for j in range(m2):
            at = (j * pairs + q) * (ny // 2) + SIDE // 2
            done.append(narrow[at : at + rows // 2, :])
        for d in range(packed.shape[0]):
            for c in range(2):
                packed[d, c, q] = done[c * m + d % m]


def merge_kernel(chips, fields, means, out):
    parts = fields.shape[0] // chips
    for e in range(fields.shape[0]):
        x, y = divmod(e, parts)
        out[e, :2] = fields[e]
        out[e, 2:] = means[y * chips + x]


def put_coarse(mine, other, refs, offsets, parts, skip):
    k = lax.axis_index("gz")
    _, _, pairs, rows, _ = mine.shape
    for e in range(mine.shape[0]):
        s, y = divmod(e, parts)
        for came, z in ((mine, k), (other, 1 - k)):
            for j, ref in enumerate(refs):
                ref[pl.ds(2 * pairs * s + pairs * z + offsets[j], pairs), y * rows : (y + 1) * rows] = came[e, skip + j]


def halve(sums, narrow, ny, count, total, values):
    nz = sums.shape[1]

    def body(q):
        for j, v in enumerate(values(q)):
            sums[pl.ds(pl.multiple_of((j * total + q) * ny, ny), ny), :] = v

    loop(total, body)
    n = count * total * ny // 2
    narrow[pl.ds(0, n), :] = dot(sums[pl.ds(0, n, 2), :] + sums[pl.ds(1, n, 2), :], pick(nz, nz, True, 0.125))


def levels(mine, other, si1, bx1, by1, bz1, wr1, wi1, dr1, bx2, by2, bz2, wr2, wi2, rho1, sr1, rho2, sr2, si2, dr2, sums, narrow):
    n1, ny, nz = si1.shape
    zero = jnp.zeros((1, ny, nz), F32)
    rho1[pl.ds(0, 1)] = zero
    rho1[pl.ds(n1 + 1, 1)] = zero
    put_coarse(mine, other, (rho1, sr1, si1), (1, 0, 0), ny // mine.shape[3], 2)
    level_coefs(rho1, sr1, si1, 0.25, bx1, by1, bz1, wr1, wi1, dr1, 4, 0, n1)
    n2, ny2 = sr2.shape[:2]
    halve(sums, narrow, ny, 3, n2, lambda q: (rho1[2 * q + 1] + rho1[2 * q + 2], sr1[2 * q] + sr1[2 * q + 1], si1[2 * q] + si1[2 * q + 1]))
    zero2 = jnp.zeros((1, ny2, nz), F32)
    rho2[pl.ds(0, 1)] = zero2
    rho2[pl.ds(n2 + 1, 1)] = zero2
    n = n2 * ny2
    for j, ref in enumerate((rho2.at[pl.ds(1, n2)], sr2, si2)):
        ref[...] = narrow[j * n : (j + 1) * n, :].reshape(n2, ny2, nz)
    level_coefs(rho2, sr2, si2, 0.0625, bx2, by2, bz2, wr2, wi2, dr2, n2, 0, n2)


def coarse_kernel(mine, other, out, si1, bx1, by1, bz1, wr1, wi1, dr1, bx2, by2, bz2, wr2, wi2, rho1, sr1, rho2, sr2, si2, dr2, sums, narrow, g1, ua1, ub1, g2, ua2, ub2, wide, tall):
    levels(mine, other, si1, bx1, by1, bz1, wr1, wi1, dr1, bx2, by2, bz2, wr2, wi2, rho1, sr1, rho2, sr2, si2, dr2, sums, narrow)
    k = lax.axis_index("gz")
    chip = lax.axis_index("gx")
    pairs = mine.shape[2]
    n1, ny, nz = si1.shape
    zero = jnp.zeros((1, ny, nz), F32)
    for u in (ua1, ub1):
        for c in range(2):
            u[c, pl.ds(0, 1)] = zero
            u[c, pl.ds(n1 + 1, 1)] = zero
    put_coarse(mine, other, (g1.at[0], g1.at[1]), (0, 0), ny // mine.shape[3], 0)
    step1 = 4
    coefs1 = (bx1, by1, bz1, wr1, wi1)

    def first(i):
        p = i * step1
        r, m = weigh(g1[0, pl.ds(p, step1)], g1[1, pl.ds(p, step1)], p, step1, wr1, wi1)
        ua1[0, pl.ds(p + 1, step1)], ua1[1, pl.ds(p + 1, step1)] = r, m

    loop(n1 // step1, first)

    def sweep1(src, dst):
        def body(i):
            p = i * step1
            r, m = sweep_planes(src, (0, 1), p + 1, g1, p, p, step1, coefs1)
            dst[0, pl.ds(p + 1, step1)], dst[1, pl.ds(p + 1, step1)] = r, m

        loop(n1 // step1, body)

    sweep1(ua1, ub1)
    n2, ny2 = n1 // 2, ny // 2

    def down(q):
        r, m = resid_planes(ub1, (0, 1), 2 * q + 1, g1, 2 * q, 2 * q, 2, coefs1, dr1, si1)
        return r[0] + r[1], m[0] + m[1]

    halve(sums, narrow, ny, 2, n2, down)
    zero2 = jnp.zeros((1, ny2, nz), F32)
    n = n2 * ny2
    for c in range(2):
        g2[c] = narrow[c * n : (c + 1) * n, :].reshape(n2, ny2, nz)
        for u in (ua2, ub2):
            u[c, pl.ds(0, 1)] = zero2
            u[c, pl.ds(n2 + 1, 1)] = zero2
    coefs2 = (bx2, by2, bz2, wr2, wi2)
    ua2[0, pl.ds(1, n2)], ua2[1, pl.ds(1, n2)] = weigh(g2[0], g2[1], 0, n2, wr2, wi2)
    src, dst = ua2, ub2
    for _ in range(CSWEEPS - 1):
        dst[0, pl.ds(1, n2)], dst[1, pl.ds(1, n2)] = sweep_planes(src, (0, 1), 1, g2, 0, 0, n2, coefs2)
        src, dst = dst, src

    widen = pick(nz, nz, False, 1.0)
    for c in range(2):
        wide[pl.ds(c * n, n), :] = dot(src[c, pl.ds(1, n2)].reshape(n, nz), widen)
    twice = wide[pl.ds(0, 2 * n), :]
    tall[pl.ds(0, 2 * n, 2), :] = twice
    tall[pl.ds(1, 2 * n, 2), :] = twice

    def lift(q):
        for c in range(2):
            v = tall[pl.ds(pl.multiple_of((c * n2 + q) * ny, ny), ny), :]
            for j in range(2):
                ub1[c, 2 * q + j + 1] = ub1[c, 2 * q + j + 1] + v

    loop(n2, lift)
    sweep1(ub1, ua1)
    sweep1(ua1, ub1)
    out[...] = ub1[:, pl.ds((2 * chip + k) * pairs, 2 + pairs)]


def pack_kernel(u1, up_gy, from_gz, from_gx, *refs):
    *outs, edges, blocks = refs
    k = lax.axis_index("gz")
    me = lax.axis_index("gy")
    edges[k] = from_gz[...]
    edges[1 - k] = from_gx[...]
    _, quads, ny, nz = u1.shape
    parts = len(outs)
    rows = ny // parts
    edge = SIDE // 2
    tall_rows = rows + 2 * edge
    for y in range(parts):
        low, high = max(y * rows - edge, 0), min((y + 1) * rows + edge, ny)
        for c in range(2):
            for q in range(quads):
                at = (c * quads + q) * tall_rows
                skip = low - (y * rows - edge)
                end = skip + high - low
                if skip:
                    blocks[y, at : at + skip, :] = jnp.zeros((skip, nz), F32)
                blocks[y, at + skip : at + end, :] = u1[c, q, low:high, :]
                if end < tall_rows:
                    blocks[y, at + end : at + tall_rows, :] = jnp.zeros((tall_rows - end, nz), F32)
    used = 2 * quads * tall_rows
    for v, out in enumerate(outs):
        out[:used, :] = blocks[me ^ v]
        out[used:, :] = up_gy[jnp.where(me < (me ^ v), 1, 0)]


def last_kernel(*refs):
    *back, own, edges, g, bx, by, bz, wr, wi, out, ua, ub, tall, flat = refs
    k = lax.axis_index("gz")
    y = lax.axis_index("gy")
    m2, pad, ny, nz = ua.shape
    m = m2 // 2
    half = pad - 2 * HALO
    rows = ny - 2 * SIDE
    quads = pad // 2
    lanes = nz // 2
    ua[:, pl.ds(1, pad - 2)] = own[...]
    blank = jnp.zeros((m2, ny, nz), F32)
    for p, side in ((0, 1), (pad - 1, 0)):
        ua[:, p] = blank
        ua[:, p, SIDE : SIDE + rows, :] = edges[side]
    used = 2 * quads * ny // 2
    for v, ref in enumerate(back):
        flat[y ^ v] = ref[...]
    for high in range(2):
        there = jnp.where(y < m - 1, 1.0, 0.0) if high else jnp.where(y > 0, 1.0, 0.0)
        peer = jnp.minimum(y + 1, m - 1) if high else jnp.maximum(y - 1, 0)
        row = SIDE + rows + 1 if high else SIDE - 2
        block = flat[peer, used:, :] * there
        for z in range(2):
            for f in range(m2):
                for i in range(half):
                    at = z * m2 * half + f * half + i
                    ua[f, HALO + i, row : row + 1, z * lanes : (z + 1) * lanes] = block[at : at + 1, :]
    u1 = flat[:, :used, :].reshape(m * used, lanes)
    for h in range(2):
        col = lax.broadcasted_iota(jnp.int32, (lanes, lanes), 1) + h * lanes
        line = lax.broadcasted_iota(jnp.int32, (lanes, lanes), 0)
        v = dot(u1, jnp.where(line == col // 2, 1.0, 0.0).astype(F32))
        tall[pl.ds(0, m * used, 2), :] = v
        tall[pl.ds(1, m * used, 2), :] = v
        spot = slice(h * lanes, (h + 1) * lanes)
        for r in range(m):
            for c in range(2):
                for q in range(quads):
                    at = ((r * 2 + c) * quads + q) * ny
                    w = tall[at : at + ny, :]
                    f = c * m + r
                    for j in range(2):
                        ua[f, 2 * q + j, :, spot] = ua[f, 2 * q + j, :, spot] + w
    coefs = (bx, by, bz, wr, wi)

    def third(i):
        p = i + 1
        for r in range(m):
            ub[r, pl.ds(p, 1)], ub[m + r, pl.ds(p, 1)] = sweep_planes(ua, (r, m + r), p, g, p, p, 1, coefs)

    loop(pad - 2, third)

    def fourth(i):
        p = i + HALO
        for r in range(m):
            for c, v in enumerate(sweep_planes(ub, (r, m + r), p, g, p, p, 1, coefs)):
                for z in range(2):
                    slot = jnp.where(k == z, 0, 1)
                    out[slot, c, r, i] = v[0, SIDE : SIDE + rows, z * lanes : (z + 1) * lanes]

    loop(half, fourth)


def gather_kernel(kept, came, out):
    k = lax.axis_index("gz")
    half = kept.shape[2]
    for side, ref in ((k, kept), (1 - k, came)):
        for c in range(2):
            for r in range(kept.shape[1]):
                out[c, r, pl.ds(side * half, half)] = ref[c, r]


def call(kernel, outs, args, scratch=(), limit=14, space=pltpu.VMEM, sems=None, cost=None, aliases=None):
    single = not isinstance(outs, list)
    shapes = [outs] if single else outs
    result = pl.pallas_call(
        kernel,
        out_shape=[jax.ShapeDtypeStruct(s, F32) for s in shapes],
        in_specs=[pl.BlockSpec(memory_space=space)] * len(args),
        out_specs=[pl.BlockSpec(memory_space=pltpu.VMEM)] * len(shapes),
        scratch_shapes=[pltpu.VMEM(s, F32) for s in scratch] + ([pltpu.SemaphoreType.DMA((sems,))] if sems else []),
        compiler_params=pltpu.CompilerParams(vmem_limit_bytes=limit * MIB),
        input_output_aliases=aliases or {},
        cost_estimate=cost and pl.CostEstimate(flops=cost, bytes_accessed=0, transcendentals=0),
    )(*args)
    return result[0] if single else result


def local_planes(rhs, density, shift_real, shift_imag):
    _, m, xs, rows, lanes = rhs.shape
    half = xs // 2
    chips = lax.axis_size("gx")
    ny, nz = rows * m, 2 * lanes
    pad = half + 2 * HALO
    swap = [(0, 1), (1, 0)]
    ends = [p for c in range(chips - 1) for p in ((2 * c + 1, 2 * c + 2), (2 * c + 2, 2 * c + 1))]
    fields = (rhs, density, shift_real, shift_imag)

    own_half = (2 * m + 3, half, rows, lanes)
    placed = tuple(pltpu.with_memory_space_constraint(f, pltpu.HBM) for f in fields)
    away, kept = call(send_kernel, [own_half, own_half], placed, space=pltpu.HBM, sems=10)
    came = lax.ppermute(away, "gz", swap)
    pairs = half // 2
    means = (3, pairs, rows // 2, lanes)
    n = 3 * pairs * rows
    coarse = call(means_kernel, means, (kept, came), scratch=[(n, lanes), (2, n // 2, lanes)])

    def spread(array, axis, count):
        return [lax.ppermute(array, axis, [(i, i ^ v) for i in range(count)]) if v else array for v in range(count)]

    coarse = spread(coarse, "gx", chips)

    rim = ((2 * m + 3) * HALO + 1) * half
    rim = (2, -(-rim // 8) * 8, lanes)
    to_even, to_odd = call(rows_kernel, [rim, rim], (kept, came), scratch=[(2,) + rim])
    even = lax.ppermute(to_even, "gy", [(i, i ^ 1) for i in range(m)])
    odd = lax.ppermute(to_odd, "gy", [(i, (i + 2 * (i % 2) - 1) % m) for i in range(m)])

    plane = (rows + 2 * SIDE, nz)
    laid = [(2 * m, pad) + plane, (pad + 2,) + plane, (pad,) + plane, (pad,) + plane]
    edges = (HALO * (2 * m + 2) + HALO + 1,) + plane
    *state, to_gz, to_gx, coarse = call(lay_kernel, laid + [edges, edges, (chips, *means)], (kept, came, even, odd, *coarse), scratch=[(2,) + rim])
    from_gx = lax.ppermute(to_gx, ("gx", "gz"), ends)
    from_gz = lax.ppermute(to_gz, "gz", swap)

    brow = (rows, nz)
    tall0 = 2 * m * pairs * plane[0]
    full = laid + [(pad + 1,) + plane] + [(pad,) + plane] * 5 + [(2 * m, pad) + plane, (2 * m, pad - 2) + plane]
    *state, coarse = call(near_kernel, full + [(chips, *means)], (from_gz, *state, coarse), aliases={i + 1: i for i in range(len(laid))}, cost=NEAR_COST)
    coarse = spread(coarse, "gy", m)
    g, _, _, _, bx, by, bz, wr, wi, _, _, own, up_gz, up_gx, up_gy, packed, coarse = call(
        fine_kernel,
        full + [(2 * m,) + brow, (2 * m,) + brow, (2, 4 * m * half, lanes), (chips * m, 2, pairs, rows // 2, lanes), (m * chips, *means)],
        (from_gx, *state, *coarse),
        scratch=[(tall0, lanes), (tall0, lanes), (tall0 // 2, lanes)],
        aliases={i + 1: i for i in range(len(full))},
    )
    u_gx = lax.ppermute(up_gx, ("gx", "gz"), ends)
    u_gz = lax.ppermute(up_gz, "gz", swap)
    mine = lax.all_to_all(packed, ("gx", "gy"), 0, 0, tiled=True)
    mine = call(functools.partial(merge_kernel, chips), (chips * m, 5) + packed.shape[2:], (mine, coarse))
    other = lax.ppermute(mine, "gz", swap)

    n1, n2 = chips * xs // 2, chips * xs // 4
    p1, p2 = (ny // 2, nz // 2), (ny // 4, nz // 2)

    u1 = call(
        coarse_kernel,
        (2, 2 + pairs) + p1,
        (mine, other),
        scratch=[(n1,) + p1, (n1 + 1,) + p1]
        + [(n1,) + p1] * 5
        + [(n2 + 1,) + p2]
        + [(n2,) + p2] * 4
        + [(n1 + 2,) + p1, (n1,) + p1, (n2 + 2,) + p2, (n2,) + p2, (n2,) + p2, (n2,) + p2, (3 * n2 * p1[0], lanes), (3 * n2 * p2[0], lanes)]
        + [(2, n1) + p1, (2, n1 + 2) + p1, (2, n1 + 2) + p1, (2, n2) + p2, (2, n2 + 2) + p2, (2, n2 + 2) + p2]
        + [(2 * n2 * p2[0], lanes), (2 * n2 * p1[0], lanes)],
        cost=COARSE_COST,
    )
    used = (2 + pairs) * plane[0]
    block = (used + 4 * m * half, lanes)
    *blocks, halo = call(pack_kernel, [block] * m + [(2, 2 * m) + brow], (u1, up_gy, u_gz, u_gx), scratch=[(m, used, lanes)])
    back = [lax.ppermute(b, "gy", [(i, i ^ v) for i in range(m)]) if v else b for v, b in enumerate(blocks)]
    result = call(
        last_kernel,
        (2, 2, m, half, rows, lanes),
        (*back, own, halo, g, bx, by, bz, wr, wi),
        scratch=[(2 * m, pad) + plane, (2 * m, pad) + plane, (2 * m * used, lanes), (m,) + block],
    )
    last = lax.ppermute(result[1], "gz", swap)
    return call(gather_kernel, rhs.shape, (result[0], last))


def solution(mesh):
    sizes = dict(mesh.shape)

    def local(rhs, density, shift_real, shift_imag):
        _, m, xs, rows, lanes = rhs.shape
        planes = sizes["gz"] == 2 and sizes["gy"] == m == 4 and sizes["gx"] in (2, 4, 8) and xs == 8 and rows % 16 == 0 and lanes == 128
        return (local_planes if planes else local_general)(rhs, density, shift_real, shift_imag)

    placed = (
        P(None, None, "gx", "gy", "gz"),
        P("gx", "gy", "gz"),
        P("gx", "gy", "gz"),
        P("gx", "gy", "gz"),
    )
    return jax.shard_map(
        local,
        mesh=mesh,
        in_specs=placed,
        out_specs=P(None, None, "gx", "gy", "gz"),
        check_vma=False,
    )
```

```python
import functools

import jax
import jax.numpy as jnp
from jax import lax
from jax.experimental import pallas as pl
from jax.experimental.pallas import tpu as pltpu
from jax.sharding import PartitionSpec as P

NU = 2
CSWEEPS = 4


omega_damp = 0.8


def padded(cells, sides, width):
    for axis, dim in sides:
        count = lax.axis_size(axis)
        ends = count - 1
        head = lax.slice_in_dim(cells, 0, width, axis=dim)
        tail = lax.slice_in_dim(cells, cells.shape[dim] - width, cells.shape[dim], axis=dim)
        cells = jnp.concatenate(
            [
                lax.ppermute(tail, axis, [(i, (i + 1) % count) for i in range(ends)]),
                cells,
                lax.ppermute(head, axis, [((i + 1) % count, i) for i in range(ends)]),
            ],
            axis=dim,
        )
    return cells


def face_coefs(rho_pad):
    center = rho_pad[1:-1, 1:-1, 1:-1]
    others = [
        rho_pad[2:, 1:-1, 1:-1],
        rho_pad[:-2, 1:-1, 1:-1],
        rho_pad[1:-1, 2:, 1:-1],
        rho_pad[1:-1, :-2, 1:-1],
        rho_pad[1:-1, 1:-1, 2:],
        rho_pad[1:-1, 1:-1, :-2],
    ]
    result = []
    for other in others:
        total = center + other
        result.append(2.0 / jnp.where(total > 0.0, total, 1.0))
    return result


def make_level(rho_pad, shift_re, shift_im, scale):
    coefs = face_coefs(rho_pad)
    bsum = coefs[0] + coefs[1] + coefs[2] + coefs[3] + coefs[4] + coefs[5]
    diag_re = scale * bsum - shift_re
    diag_im = -shift_im
    magnitude = diag_re * diag_re + diag_im * diag_im
    return (coefs, bsum, shift_re, shift_im, scale, diag_re / magnitude, -diag_im / magnitude)


def apply_op(upad, level):
    coefs, bsum, shift_re, shift_im, scale, inv_re, inv_im = level
    center = upad[:, :, 1:-1, 1:-1, 1:-1]
    nbsum = coefs[0] * upad[:, :, 2:, 1:-1, 1:-1] + coefs[1] * upad[:, :, :-2, 1:-1, 1:-1]
    nbsum = nbsum + coefs[2] * upad[:, :, 1:-1, 2:, 1:-1] + coefs[3] * upad[:, :, 1:-1, :-2, 1:-1]
    nbsum = nbsum + coefs[4] * upad[:, :, 1:-1, 1:-1, 2:] + coefs[5] * upad[:, :, 1:-1, 1:-1, :-2]
    lap = scale * (bsum * center - nbsum)
    out_re = lap[0] - shift_re * center[0] + shift_im * center[1]
    out_im = lap[1] - shift_re * center[1] - shift_im * center[0]
    return jnp.stack([out_re, out_im])


def precondition(resid, level):
    inv_re, inv_im = (level[5], level[6])
    upd_re = inv_re * resid[0] - inv_im * resid[1]
    upd_im = inv_re * resid[1] + inv_im * resid[0]
    return omega_damp * jnp.stack([upd_re, upd_im])


def smooth(field, target, level, padder, count):
    for sweep in range(count):
        field = field + precondition(target - apply_op(padder(field), level), level)
    return field


def restrict(field):
    lead = field.shape[:-3]
    sx, sy, sz = field.shape[-3:]
    blocks = field.reshape(lead + (sx // 2, 2, sy // 2, 2, sz // 2, 2))
    return jnp.mean(blocks, axis=(-5, -3, -1))


def prolong(field):
    return jnp.repeat(jnp.repeat(jnp.repeat(field, 2, -3), 2, -2), 2, -1)


def field_pad(field):
    return padded(field, (("gx", 2), ("gy", 3), ("gz", 4)), 1)


def brick_density(rho):
    return padded(rho, (("gx", 0), ("gy", 1), ("gz", 2)), 1)


def local_general(rhs, density, shift_real, shift_imag):
    rho1, sr1, si1 = (restrict(density), restrict(shift_real), restrict(shift_imag))
    level1 = make_level(brick_density(rho1), sr1, si1, 0.25)
    rho2, sr2, si2 = (restrict(rho1), restrict(sr1), restrict(si1))
    level0 = make_level(brick_density(density), shift_real, shift_imag, 1.0)
    fine = precondition(rhs, level0)
    fine = smooth(fine, rhs, level0, field_pad, NU - 1)
    coarse_rhs = restrict(rhs - apply_op(field_pad(fine), level0))
    middle = precondition(coarse_rhs, level1)
    middle = smooth(middle, coarse_rhs, level1, field_pad, NU - 1)
    lowest_rhs = restrict(coarse_rhs - apply_op(field_pad(middle), level1))
    level2 = make_level(brick_density(rho2), sr2, si2, 0.0625)
    lowest = precondition(lowest_rhs, level2)
    lowest = smooth(lowest, lowest_rhs, level2, field_pad, CSWEEPS - 1)
    middle = smooth(middle + prolong(lowest), coarse_rhs, level1, field_pad, NU)
    corrected = fine + prolong(middle)
    return smooth(corrected, rhs, level0, field_pad, NU)


HALO = 2
SIDE = 4
MIB = 1 << 20
COARSE_COST = 5 * 10**9
NEAR_COST = 2 * 10**9
F32 = jnp.float32


def loop(count, body):
    for i in range(count):
        body(i)


def safe(total):
    return jnp.where(total > 0.0, total, 1.0)


def level_coefs(rho, sr, si, scale, bx, by, bz, wr, wi, dr, step, start, count):
    ny, nz = sr.shape[1:]
    two = 2.0 * scale
    bx[pl.ds(start, 1)] = two / safe(rho[pl.ds(start, 1)] + rho[pl.ds(start + 1, 1)])

    def body(i):
        p = start + i * step
        r = rho[pl.ds(p + 1, step)]
        row = lax.broadcasted_iota(jnp.int32, r.shape, 1)
        lane = lax.broadcasted_iota(jnp.int32, r.shape, 2)
        last_y, last_z = row == ny - 1, lane == nz - 1
        tx = safe(r + rho[pl.ds(p + 2, step)])
        ty = safe(r + jnp.where(last_y, 0.0, pltpu.roll(r, ny - 1, 1)))
        tz = safe(r + jnp.where(last_z, 0.0, pltpu.roll(r, nz - 1, 2)))
        te = safe(r)
        pair, other = tx * ty, tz * te
        whole = two / (pair * other)
        per_pair, per_other = whole * other, whole * pair
        bx[pl.ds(p + 1, step)] = per_pair * ty
        edge = per_other * tz
        bsum = bx[pl.ds(p, step)] + bx[pl.ds(p + 1, step)]
        face = per_pair * tx
        bsum = bsum + face + jnp.where(row == 0, edge, pltpu.roll(face, 1, 1))
        by[pl.ds(p, step)] = jnp.where(last_y, 0.0, face)
        face = per_other * te
        bsum = bsum + face + jnp.where(lane == 0, edge, pltpu.roll(face, 1, 2))
        bz[pl.ds(p, step)] = jnp.where(last_z, 0.0, face)
        d = bsum - sr[pl.ds(p, step)]
        e = si[pl.ds(p, step)]
        w = jnp.where(r > 0.0, omega_damp, 0.0) / (d * d + e * e)
        wr[pl.ds(p, step)] = w * d
        wi[pl.ds(p, step)] = w * e
        dr[pl.ds(p, step)] = d

    loop(count // step, body)


def near(u, f, at, p, step, bx, by, bz):
    mid = u[f, pl.ds(at, step)]
    ny, nz = mid.shape[1:]
    b = by[pl.ds(p, step)]
    total = bx[pl.ds(p, step)] * u[f, pl.ds(at - 1, step)] + bx[pl.ds(p + 1, step)] * u[f, pl.ds(at + 1, step)]
    total = total + (b * pltpu.roll(mid, ny - 1, 1) + pltpu.roll(b * mid, 1, 1))
    b = bz[pl.ds(p, step)]
    return mid, total + (b * pltpu.roll(mid, nz - 1, 2) + pltpu.roll(b * mid, 1, 2))


def weigh(tr, ti, p, step, wr, wi):
    a, b = wr[pl.ds(p, step)], wi[pl.ds(p, step)]
    return a * tr - b * ti, a * ti + b * tr


def sweep_planes(u, fields, at, g, gat, p, step, coefs):
    bx, by, bz, wr, wi = coefs
    re, im = fields
    mr, nr = near(u, re, at, p, step, bx, by, bz)
    mi, ni = near(u, im, at, p, step, bx, by, bz)
    vr, vi = weigh(g[re, pl.ds(gat, step)] + nr, g[im, pl.ds(gat, step)] + ni, p, step, wr, wi)
    rest = 1.0 - omega_damp
    return rest * mr + vr, rest * mi + vi


def resid_planes(u, fields, at, g, gat, p, step, coefs, dr, si):
    bx, by, bz = coefs[:3]
    re, im = fields
    mr, nr = near(u, re, at, p, step, bx, by, bz)
    mi, ni = near(u, im, at, p, step, bx, by, bz)
    d, e = dr[pl.ds(p, step)], si[pl.ds(p, step)]
    return g[re, pl.ds(gat, step)] + nr - (d * mr + e * mi), g[im, pl.ds(gat, step)] + ni - (d * mi - e * mr)


def pick(nrow, ncol, down, value):
    row = lax.broadcasted_iota(jnp.int32, (nrow, ncol), 0)
    col = lax.broadcasted_iota(jnp.int32, (nrow, ncol), 1)
    hit = (row // 2 == col) if down else (row == col // 2)
    return jnp.where(hit, value, 0.0).astype(F32)


def dot(a, b):
    b = b.astype(jnp.bfloat16)
    high = a.astype(jnp.bfloat16)
    a = a - high.astype(F32)
    middle = a.astype(jnp.bfloat16)
    low = (a - middle.astype(F32)).astype(jnp.bfloat16)
    parts = [jnp.dot(part, b, preferred_element_type=F32) for part in (low, middle, high)]
    return parts[0] + parts[1] + parts[2]


def send_kernel(rhs, rho, sr, si, away, kept, sems):
    half = away.shape[1]
    m = rhs.shape[1]
    k = lax.axis_index("gz")
    copies = []
    for n, (out, side) in enumerate(((away, 1 - k), (kept, k))):
        planes = pl.ds(side * half, half)
        pieces = [(rhs.at[c, :, planes], out.at[pl.ds(c * m, m)]) for c in range(2)]
        pieces += [(ref.at[planes], out.at[2 * m + j]) for j, ref in enumerate((rho, sr, si))]
        copies += [pltpu.make_async_copy(src, dst, sems.at[5 * n + j]) for j, (src, dst) in enumerate(pieces)]
    for copy in copies:
        copy.start()
    for copy in copies:
        copy.wait()


def rows_kernel(kept, came, to_even, to_odd, ends):
    y = lax.axis_index("gy")
    fields, half, rows, _ = kept.shape
    rho = fields - 3
    for t, ref in enumerate((kept, came)):
        for h in range(2):
            at = 0
            for f in range(fields):
                n = HALO + 1 if f == rho else HALO
                for i in range(half):
                    ends[h, t, at : at + n, :] = ref[f, i, (rows - n if h else 0) : (rows if h else n), :]
                    at += n
    even = lax.rem(y, 2)
    to_even[...] = ends[1 - even]
    to_odd[...] = ends[even]


def means_kernel(kept, came, out, slots, sums):
    k = lax.axis_index("gz")
    fields, half, rows, lanes = kept.shape
    pairs = half // 2
    for t, ref in enumerate((kept, came)):
        for j in range(3):
            for q in range(pairs):
                at = (j * pairs + q) * rows
                slots[at : at + rows, :] = ref[fields - 3 + j, 2 * q] + ref[fields - 3 + j, 2 * q + 1]
        n = 3 * pairs * rows // 2
        sums[t] = slots[pl.ds(0, n, 2), :] + slots[pl.ds(1, n, 2), :]
    done = dot(jnp.concatenate([sums[k], sums[1 - k]], axis=1), pick(2 * lanes, lanes, True, 0.125))
    out[...] = done.reshape(3, pairs, rows // 2, lanes)


def join(axis, parts, out):
    me = lax.axis_index(axis)
    n = out.shape[0] // len(parts)
    for v, ref in enumerate(parts):
        out[pl.ds((me ^ v) * n, n)] = ref[...].reshape((n,) + out.shape[1:])


def lay_kernel(kept, came, even, odd, *refs):
    *means, g, rho, sr, si, to_gz, to_gx, joined, ends = refs
    join("gx", means, joined)
    k = lax.axis_index("gz")
    y = lax.axis_index("gy")
    fields, half, rows, lanes = kept.shape
    m2 = fields - 3
    arrays = [g.at[f] for f in range(m2)] + [rho, sr, si]
    for f, ref in enumerate(arrays):
        first = HALO + 1 if f == m2 else HALO
        for i in range(half):
            ref[first + i] = jnp.zeros(ref.shape[1:], F32)
        for t, src in enumerate((kept, came)):
            z = k if t == 0 else 1 - k
            spot = pl.ds(pl.multiple_of(z * lanes, lanes), lanes)
            for i in range(half):
                ref[first + i, SIDE : SIDE + rows, spot] = src[f, i]
    ends[0] = even[...]
    ends[1] = odd[...]
    for high in range(2):
        there = jnp.where(y < lax.axis_size("gy") - 1, 1.0, 0.0) if high else jnp.where(y > 0, 1.0, 0.0)
        peer = lax.rem(y, 2) if high else 1 - lax.rem(y, 2)
        for z in range(2):
            slot = jnp.where(k == z, 0, 1)
            at = 0
            for f, ref in enumerate(arrays):
                n = HALO + 1 if f == m2 else HALO
                row = SIDE + rows if high else SIDE - n
                for i in range(half):
                    ref[n + i, row : row + n, z * lanes : (z + 1) * lanes] = ends[peer, slot, at : at + n, :] * there
                    at += n
    for out, up in ((to_gz, 1 - k), (to_gx, k)):
        two, three = HALO + up * (half - HALO), HALO + 1 + up * (half - HALO - 1)
        rows, ny = ref.shape[1] - 2 * (SIDE - HALO), ref.shape[1]
        for j, ref in enumerate(arrays[:m2] + [sr, si]):
            for i in range(HALO):
                at = (HALO * j + i) * rows
                out[at : at + rows, :] = ref[two + i, SIDE - HALO : SIDE - HALO + rows, :]
        for i in range(HALO + 1):
            at = HALO * (m2 + 2) * rows + i * ny
            out[at : at + ny, :] = rho[three + i]


def lay_side(came, low, g, rho, sr, si):
    m2, pad = g.shape[:2]
    half = pad - 2 * HALO
    two, three = low * (half + HALO), low * (half + HALO + 1)
    ny, nz = sr.shape[1:]
    rows = ny - 2 * (SIDE - HALO)
    blank = jnp.zeros((ny, nz), F32)
    for j, ref in enumerate([g.at[f] for f in range(m2)] + [sr, si]):
        for i in range(HALO):
            at = (HALO * j + i) * rows
            ref[two + i] = blank
            ref[two + i, SIDE - HALO : SIDE - HALO + rows, :] = came[at : at + rows, :]
    for i in range(HALO + 1):
        at = HALO * (m2 + 2) * rows + i * ny
        rho[three + i] = came[at : at + ny, :]


def side_planes(low, g, rho, sr, si, bx, by, bz, wr, wi, dr, ua, own, rest):
    m2, pad = g.shape[:2]
    m = m2 // 2
    half = pad - 2 * HALO
    count = HALO + 1 if rest else pad - HALO - 1
    start = low * (pad - count)
    level_coefs(rho, sr, si, 1.0, bx, by, bz, wr, wi, dr, count, start, count)

    def first(i):
        p = start + i
        for r in range(m):
            ua[r, pl.ds(p, 1)], ua[m + r, pl.ds(p, 1)] = weigh(g[r, pl.ds(p, 1)], g[m + r, pl.ds(p, 1)], p, 1, wr, wi)

    loop(count, first)
    done = HALO + 1 if rest else half - 1
    begin = low * (pad - 2 - done)

    def second(i):
        at = begin + i
        p = at + 1
        for r in range(m):
            own[r, pl.ds(at, 1)], own[m + r, pl.ds(at, 1)] = sweep_planes(ua, (r, m + r), p, g, p, p, 1, (bx, by, bz, wr, wi))

    loop(done, second)


def beside_kernel(from_gz, _g, _rho, _sr, _si, means, g, rho, sr, si, out):
    lay_side(from_gz, 1 - lax.axis_index("gz"), g, rho, sr, si)
    out[...] = means[...]


def near_kernel(_g, _rho, _sr, _si, *state):
    side_planes(1 - lax.axis_index("gz"), *state, False)


def fine_kernel(from_gx, *refs):
    g, rho, sr, si, bx, by, bz, wr, wi, dr, ua, own, up_gz, up_gx, up_gy, packed, joined, left, right, narrow = refs[-20:]
    join("gy", refs[12:-20], joined)
    k = lax.axis_index("gz")
    lay_side(from_gx, k, g, rho, sr, si)
    side_planes(k, g, rho, sr, si, bx, by, bz, wr, wi, dr, ua, own, True)
    coefs = (bx, by, bz, wr, wi)
    m2, pad, ny, nz = g.shape
    m = m2 // 2
    half = pad - 2 * HALO
    rows = ny - 2 * SIDE
    lanes = nz // 2
    for f in range(m2):
        up_gz[f] = own[f, 2 + (1 - k) * (half - 3), SIDE : SIDE + rows, :]
        up_gx[f] = own[f, 2 + k * (half - 3), SIDE : SIDE + rows, :]
        for i in range(half):
            for h, row in enumerate((SIDE + 1, SIDE + rows - 2)):
                for z in range(2):
                    at = z * m2 * half + f * half + i
                    up_gy[h, at : at + 1, :] = own[f, i + 1, row : row + 1, z * lanes : (z + 1) * lanes]
    pairs = half // 2

    def down(q):
        p = HALO + 2 * q
        totals = {}
        for r in range(m):
            ar, ai = resid_planes(own, (r, m + r), p - 1, g, p, p, 1, coefs, dr, si)
            br, bi = resid_planes(own, (r, m + r), p, g, p + 1, p + 1, 1, coefs, dr, si)
            totals[r], totals[m + r] = ar + br, ai + bi
        for j, v in totals.items():
            spot = pl.ds((j * pairs + q) * ny, ny)
            left[spot, :] = v[0, :, :lanes]
            right[spot, :] = v[0, :, lanes:]

    loop(pairs, down)
    n = m2 * pairs * ny // 2
    both = [ref[pl.ds(0, n, 2), :] + ref[pl.ds(1, n, 2), :] for ref in (left, right)]
    narrow[...] = dot(jnp.concatenate(both, axis=1), pick(nz, lanes, True, 0.125))
    for q in range(pairs):
        done = []
        for j in range(m2):
            at = (j * pairs + q) * (ny // 2) + SIDE // 2
            done.append(narrow[at : at + rows // 2, :])
        for d in range(packed.shape[0]):
            for c in range(2):
                packed[d, c, q] = done[c * m + d % m]


def merge_kernel(chips, fields, means, out):
    parts = fields.shape[0] // chips
    for e in range(fields.shape[0]):
        x, y = divmod(e, parts)
        out[e, :2] = fields[e]
        out[e, 2:] = means[y * chips + x]


def put_coarse(mine, other, refs, offsets, parts, skip):
    k = lax.axis_index("gz")
    _, _, pairs, rows, _ = mine.shape
    for e in range(mine.shape[0]):
        s, y = divmod(e, parts)
        for came, z in ((mine, k), (other, 1 - k)):
            for j, ref in enumerate(refs):
                ref[pl.ds(2 * pairs * s + pairs * z + offsets[j], pairs), y * rows : (y + 1) * rows] = came[e, skip + j]


def halve(sums, narrow, ny, count, total, values):
    nz = sums.shape[1]

    def body(q):
        for j, v in enumerate(values(q)):
            sums[pl.ds((j * total + q) * ny, ny), :] = v

    loop(total, body)
    n = count * total * ny // 2
    narrow[pl.ds(0, n), :] = dot(sums[pl.ds(0, n, 2), :] + sums[pl.ds(1, n, 2), :], pick(nz, nz, True, 0.125))


def levels(mine, other, si1, bx1, by1, bz1, wr1, wi1, dr1, bx2, by2, bz2, wr2, wi2, rho1, sr1, rho2, sr2, si2, dr2, sums, narrow):
    n1, ny, nz = si1.shape
    zero = jnp.zeros((1, ny, nz), F32)
    rho1[pl.ds(0, 1)] = zero
    rho1[pl.ds(n1 + 1, 1)] = zero
    put_coarse(mine, other, (rho1, sr1, si1), (1, 0, 0), ny // mine.shape[3], 2)
    level_coefs(rho1, sr1, si1, 0.25, bx1, by1, bz1, wr1, wi1, dr1, 8, 0, n1)
    n2, ny2 = sr2.shape[:2]
    halve(sums, narrow, ny, 3, n2, lambda q: (rho1[2 * q + 1] + rho1[2 * q + 2], sr1[2 * q] + sr1[2 * q + 1], si1[2 * q] + si1[2 * q + 1]))
    zero2 = jnp.zeros((1, ny2, nz), F32)
    rho2[pl.ds(0, 1)] = zero2
    rho2[pl.ds(n2 + 1, 1)] = zero2
    n = n2 * ny2
    for j, ref in enumerate((rho2.at[pl.ds(1, n2)], sr2, si2)):
        ref[...] = narrow[j * n : (j + 1) * n, :].reshape(n2, ny2, nz)
    level_coefs(rho2, sr2, si2, 0.0625, bx2, by2, bz2, wr2, wi2, dr2, n2, 0, n2)


def coarse_kernel(mine, other, out, si1, bx1, by1, bz1, wr1, wi1, dr1, bx2, by2, bz2, wr2, wi2, rho1, sr1, rho2, sr2, si2, dr2, sums, narrow, g1, ua1, ub1, g2, ua2, ub2, wide, tall):
    levels(mine, other, si1, bx1, by1, bz1, wr1, wi1, dr1, bx2, by2, bz2, wr2, wi2, rho1, sr1, rho2, sr2, si2, dr2, sums, narrow)
    k = lax.axis_index("gz")
    chip = lax.axis_index("gx")
    pairs = mine.shape[2]
    n1, ny, nz = si1.shape
    zero = jnp.zeros((1, ny, nz), F32)
    for u in (ua1, ub1):
        for c in range(2):
            u[c, pl.ds(0, 1)] = zero
            u[c, pl.ds(n1 + 1, 1)] = zero
    put_coarse(mine, other, (g1.at[0], g1.at[1]), (0, 0), ny // mine.shape[3], 0)
    step1 = 4
    coefs1 = (bx1, by1, bz1, wr1, wi1)

    def first(i):
        p = i * step1
        r, m = weigh(g1[0, pl.ds(p, step1)], g1[1, pl.ds(p, step1)], p, step1, wr1, wi1)
        ua1[0, pl.ds(p + 1, step1)], ua1[1, pl.ds(p + 1, step1)] = r, m

    loop(n1 // step1, first)

    def sweep1(src, dst):
        def body(i):
            p = i * step1
            r, m = sweep_planes(src, (0, 1), p + 1, g1, p, p, step1, coefs1)
            dst[0, pl.ds(p + 1, step1)], dst[1, pl.ds(p + 1, step1)] = r, m

        loop(n1 // step1, body)

    sweep1(ua1, ub1)
    n2, ny2 = n1 // 2, ny // 2

    def down(q):
        r, m = resid_planes(ub1, (0, 1), 2 * q + 1, g1, 2 * q, 2 * q, 2, coefs1, dr1, si1)
        return r[0] + r[1], m[0] + m[1]

    halve(sums, narrow, ny, 2, n2, down)
    zero2 = jnp.zeros((1, ny2, nz), F32)
    n = n2 * ny2
    for c in range(2):
        g2[c] = narrow[c * n : (c + 1) * n, :].reshape(n2, ny2, nz)
        for u in (ua2, ub2):
            u[c, pl.ds(0, 1)] = zero2
            u[c, pl.ds(n2 + 1, 1)] = zero2
    coefs2 = (bx2, by2, bz2, wr2, wi2)
    ua2[0, pl.ds(1, n2)], ua2[1, pl.ds(1, n2)] = weigh(g2[0], g2[1], 0, n2, wr2, wi2)
    src, dst = ua2, ub2
    for _ in range(CSWEEPS - 1):
        dst[0, pl.ds(1, n2)], dst[1, pl.ds(1, n2)] = sweep_planes(src, (0, 1), 1, g2, 0, 0, n2, coefs2)
        src, dst = dst, src

    widen = pick(nz, nz, False, 1.0)
    for c in range(2):
        wide[pl.ds(c * n, n), :] = dot(src[c, pl.ds(1, n2)].reshape(n, nz), widen)
    twice = wide[pl.ds(0, 2 * n), :]
    tall[pl.ds(0, 2 * n, 2), :] = twice
    tall[pl.ds(1, 2 * n, 2), :] = twice

    def lift(q):
        for c in range(2):
            v = tall[pl.ds((c * n2 + q) * ny, ny), :]
            for j in range(2):
                ub1[c, 2 * q + j + 1] = ub1[c, 2 * q + j + 1] + v

    loop(n2, lift)
    sweep1(ub1, ua1)
    sweep1(ua1, ub1)
    out[...] = ub1[:, pl.ds((2 * chip + k) * pairs, 2 + pairs)]


def pack_kernel(u1, up_gy, from_gz, from_gx, *refs):
    *outs, edges, blocks = refs
    k = lax.axis_index("gz")
    me = lax.axis_index("gy")
    edges[k] = from_gz[...]
    edges[1 - k] = from_gx[...]
    _, quads, ny, nz = u1.shape
    parts = len(outs)
    rows = ny // parts
    edge = SIDE // 2
    tall_rows = rows + 2 * edge
    for y in range(parts):
        low, high = max(y * rows - edge, 0), min((y + 1) * rows + edge, ny)
        for c in range(2):
            for q in range(quads):
                at = (c * quads + q) * tall_rows
                skip = low - (y * rows - edge)
                end = skip + high - low
                if skip:
                    blocks[y, at : at + skip, :] = jnp.zeros((skip, nz), F32)
                blocks[y, at + skip : at + end, :] = u1[c, q, low:high, :]
                if end < tall_rows:
                    blocks[y, at + end : at + tall_rows, :] = jnp.zeros((tall_rows - end, nz), F32)
    used = 2 * quads * tall_rows
    for v, out in enumerate(outs):
        out[:used, :] = blocks[me ^ v]
        out[used:, :] = up_gy[jnp.where(me < (me ^ v), 1, 0)]


def last_kernel(*refs):
    *back, own, edges, g, bx, by, bz, wr, wi, out, ua, ub, tall, flat = refs
    k = lax.axis_index("gz")
    y = lax.axis_index("gy")
    m2, pad, ny, nz = ua.shape
    m = m2 // 2
    half = pad - 2 * HALO
    rows = ny - 2 * SIDE
    quads = pad // 2
    lanes = nz // 2
    ua[:, pl.ds(1, pad - 2)] = own[...]
    blank = jnp.zeros((m2, ny, nz), F32)
    for p, side in ((0, 1), (pad - 1, 0)):
        ua[:, p] = blank
        ua[:, p, SIDE : SIDE + rows, :] = edges[side]
    used = 2 * quads * ny // 2
    for v, ref in enumerate(back):
        flat[y ^ v] = ref[...]
    for high in range(2):
        there = jnp.where(y < m - 1, 1.0, 0.0) if high else jnp.where(y > 0, 1.0, 0.0)
        peer = jnp.minimum(y + 1, m - 1) if high else jnp.maximum(y - 1, 0)
        row = SIDE + rows + 1 if high else SIDE - 2
        block = flat[peer, used:, :] * there
        for z in range(2):
            for f in range(m2):
                for i in range(half):
                    at = z * m2 * half + f * half + i
                    ua[f, HALO + i, row : row + 1, z * lanes : (z + 1) * lanes] = block[at : at + 1, :]
    u1 = flat[:, :used, :].reshape(m * used, lanes)
    for h in range(2):
        col = lax.broadcasted_iota(jnp.int32, (lanes, lanes), 1) + h * lanes
        line = lax.broadcasted_iota(jnp.int32, (lanes, lanes), 0)
        v = dot(u1, jnp.where(line == col // 2, 1.0, 0.0).astype(F32))
        tall[pl.ds(0, m * used, 2), :] = v
        tall[pl.ds(1, m * used, 2), :] = v
        spot = slice(h * lanes, (h + 1) * lanes)
        for r in range(m):
            for c in range(2):
                for q in range(quads):
                    at = ((r * 2 + c) * quads + q) * ny
                    w = tall[at : at + ny, :]
                    f = c * m + r
                    for j in range(2):
                        ua[f, 2 * q + j, :, spot] = ua[f, 2 * q + j, :, spot] + w
    coefs = (bx, by, bz, wr, wi)

    def third(i):
        p = i + 1
        for r in range(m):
            ub[r, pl.ds(p, 1)], ub[m + r, pl.ds(p, 1)] = sweep_planes(ua, (r, m + r), p, g, p, p, 1, coefs)

    loop(pad - 2, third)

    def fourth(i):
        p = i + HALO
        for r in range(m):
            for c, v in enumerate(sweep_planes(ub, (r, m + r), p, g, p, p, 1, coefs)):
                for z in range(2):
                    slot = jnp.where(k == z, 0, 1)
                    out[slot, c, r, i] = v[0, SIDE : SIDE + rows, z * lanes : (z + 1) * lanes]

    loop(half, fourth)


def gather_kernel(kept, came, out):
    k = lax.axis_index("gz")
    half = kept.shape[2]
    for side, ref in ((k, kept), (1 - k, came)):
        for c in range(2):
            for r in range(kept.shape[1]):
                out[c, r, pl.ds(side * half, half)] = ref[c, r]


def call(kernel, outs, args, scratch=(), limit=14, space=pltpu.VMEM, sems=None, cost=None, aliases=None):
    single = not isinstance(outs, list)
    shapes = [outs] if single else outs
    result = pl.pallas_call(
        kernel,
        out_shape=[jax.ShapeDtypeStruct(s, F32) for s in shapes],
        in_specs=[pl.BlockSpec(memory_space=space)] * len(args),
        out_specs=[pl.BlockSpec(memory_space=pltpu.VMEM)] * len(shapes),
        scratch_shapes=[pltpu.VMEM(s, F32) for s in scratch] + ([pltpu.SemaphoreType.DMA((sems,))] if sems else []),
        compiler_params=pltpu.CompilerParams(vmem_limit_bytes=limit * MIB),
        input_output_aliases=aliases or {},
        cost_estimate=cost and pl.CostEstimate(flops=cost, bytes_accessed=0, transcendentals=0),
    )(*args)
    return result[0] if single else result


def local_planes(rhs, density, shift_real, shift_imag):
    _, m, xs, rows, lanes = rhs.shape
    half = xs // 2
    chips = lax.axis_size("gx")
    ny, nz = rows * m, 2 * lanes
    pad = half + 2 * HALO
    swap = [(0, 1), (1, 0)]
    ends = [p for c in range(chips - 1) for p in ((2 * c + 1, 2 * c + 2), (2 * c + 2, 2 * c + 1))]
    fields = (rhs, density, shift_real, shift_imag)

    own_half = (2 * m + 3, half, rows, lanes)
    placed = tuple(pltpu.with_memory_space_constraint(f, pltpu.HBM) for f in fields)
    away, kept = call(send_kernel, [own_half, own_half], placed, space=pltpu.HBM, sems=10)
    came = lax.ppermute(away, "gz", swap)
    pairs = half // 2
    means = (3, pairs, rows // 2, lanes)
    n = 3 * pairs * rows
    coarse = call(means_kernel, means, (kept, came), scratch=[(n, lanes), (2, n // 2, lanes)])

    def spread(array, axis, count):
        return [lax.ppermute(array, axis, [(i, i ^ v) for i in range(count)]) if v else array for v in range(count)]

    coarse = spread(coarse, "gx", chips)

    rim = ((2 * m + 3) * HALO + 1) * half
    rim = (2, -(-rim // 8) * 8, lanes)
    to_even, to_odd = call(rows_kernel, [rim, rim], (kept, came), scratch=[(2,) + rim])
    even = lax.ppermute(to_even, "gy", [(i, i ^ 1) for i in range(m)])
    odd = lax.ppermute(to_odd, "gy", [(i, (i + 2 * (i % 2) - 1) % m) for i in range(m)])

    plane = (rows + 2 * SIDE, nz)
    laid = [(2 * m, pad) + plane, (pad + 2,) + plane, (pad,) + plane, (pad,) + plane]
    edges = (HALO * (2 * m + 2) * (rows + 2 * HALO) + (HALO + 1) * plane[0], nz)
    *state, to_gz, to_gx, coarse = call(lay_kernel, laid + [edges, edges, (chips, *means)], (kept, came, even, odd, *coarse), scratch=[(2,) + rim])
    from_gx = lax.ppermute(to_gx, ("gx", "gz"), ends)
    from_gz = lax.ppermute(to_gz, "gz", swap)

    brow = (rows, nz)
    tall0 = 2 * m * pairs * plane[0]
    full = laid + [(pad + 1,) + plane] + [(pad,) + plane] * 5 + [(2 * m, pad) + plane, (2 * m, pad - 2) + plane]
    *state, coarse = call(beside_kernel, laid + [(chips, *means)], (from_gz, *state, coarse), aliases={i + 1: i for i in range(len(laid))})
    coarse = spread(coarse, "gy", m)
    state = call(near_kernel, full, tuple(state), aliases={i: i for i in range(len(laid))}, cost=NEAR_COST)
    g, _, _, _, bx, by, bz, wr, wi, _, _, own, up_gz, up_gx, up_gy, packed, coarse = call(
        fine_kernel,
        full + [(2 * m,) + brow, (2 * m,) + brow, (2, 4 * m * half, lanes), (chips * m, 2, pairs, rows // 2, lanes), (m * chips, *means)],
        (from_gx, *state, *coarse),
        scratch=[(tall0, lanes), (tall0, lanes), (tall0 // 2, lanes)],
        aliases={i + 1: i for i in range(len(full))},
    )
    u_gx = lax.ppermute(up_gx, ("gx", "gz"), ends)
    u_gz = lax.ppermute(up_gz, "gz", swap)
    mine = lax.all_to_all(packed, ("gx", "gy"), 0, 0, tiled=True)
    mine = call(functools.partial(merge_kernel, chips), (chips * m, 5) + packed.shape[2:], (mine, coarse))
    other = lax.ppermute(mine, "gz", swap)

    n1, n2 = chips * xs // 2, chips * xs // 4
    p1, p2 = (ny // 2, nz // 2), (ny // 4, nz // 2)

    u1 = call(
        coarse_kernel,
        (2, 2 + pairs) + p1,
        (mine, other),
        scratch=[(n1,) + p1, (n1 + 1,) + p1]
        + [(n1,) + p1] * 5
        + [(n2 + 1,) + p2]
        + [(n2,) + p2] * 4
        + [(n1 + 2,) + p1, (n1,) + p1, (n2 + 2,) + p2, (n2,) + p2, (n2,) + p2, (n2,) + p2, (3 * n2 * p1[0], lanes), (3 * n2 * p2[0], lanes)]
        + [(2, n1) + p1, (2, n1 + 2) + p1, (2, n1 + 2) + p1, (2, n2) + p2, (2, n2 + 2) + p2, (2, n2 + 2) + p2]
        + [(2 * n2 * p2[0], lanes), (2 * n2 * p1[0], lanes)],
        cost=COARSE_COST,
    )
    used = (2 + pairs) * plane[0]
    block = (used + 4 * m * half, lanes)
    *blocks, halo = call(pack_kernel, [block] * m + [(2, 2 * m) + brow], (u1, up_gy, u_gz, u_gx), scratch=[(m, used, lanes)])
    back = [lax.ppermute(b, "gy", [(i, i ^ v) for i in range(m)]) if v else b for v, b in enumerate(blocks)]
    result = call(
        last_kernel,
        (2, 2, m, half, rows, lanes),
        (*back, own, halo, g, bx, by, bz, wr, wi),
        scratch=[(2 * m, pad) + plane, (2 * m, pad) + plane, (2 * m * used, lanes), (m,) + block],
    )
    last = lax.ppermute(result[1], "gz", swap)
    return call(gather_kernel, rhs.shape, (result[0], last))


def solution(mesh):
    sizes = dict(mesh.shape)

    def local(rhs, density, shift_real, shift_imag):
        _, m, xs, rows, lanes = rhs.shape
        planes = sizes["gz"] == 2 and sizes["gy"] == m == 4 and sizes["gx"] in (2, 4, 8) and xs == 8 and rows % 16 == 0 and lanes == 128
        return (local_planes if planes else local_general)(rhs, density, shift_real, shift_imag)

    placed = (
        P(None, None, "gx", "gy", "gz"),
        P("gx", "gy", "gz"),
        P("gx", "gy", "gz"),
        P("gx", "gy", "gz"),
    )
    return jax.shard_map(
        local,
        mesh=mesh,
        in_specs=placed,
        out_specs=P(None, None, "gx", "gy", "gz"),
        check_vma=False,
    )
```

```python
import functools

import jax
import jax.numpy as jnp
from jax import lax
from jax.experimental import pallas as pl
from jax.experimental.pallas import tpu as pltpu
from jax.sharding import PartitionSpec as P

NU = 2
CSWEEPS = 4


omega_damp = 0.8


def padded(cells, sides, width):
    for axis, dim in sides:
        count = lax.axis_size(axis)
        ends = count - 1
        head = lax.slice_in_dim(cells, 0, width, axis=dim)
        tail = lax.slice_in_dim(cells, cells.shape[dim] - width, cells.shape[dim], axis=dim)
        cells = jnp.concatenate(
            [
                lax.ppermute(tail, axis, [(i, (i + 1) % count) for i in range(ends)]),
                cells,
                lax.ppermute(head, axis, [((i + 1) % count, i) for i in range(ends)]),
            ],
            axis=dim,
        )
    return cells


def face_coefs(rho_pad):
    center = rho_pad[1:-1, 1:-1, 1:-1]
    others = [
        rho_pad[2:, 1:-1, 1:-1],
        rho_pad[:-2, 1:-1, 1:-1],
        rho_pad[1:-1, 2:, 1:-1],
        rho_pad[1:-1, :-2, 1:-1],
        rho_pad[1:-1, 1:-1, 2:],
        rho_pad[1:-1, 1:-1, :-2],
    ]
    result = []
    for other in others:
        total = center + other
        result.append(2.0 / jnp.where(total > 0.0, total, 1.0))
    return result


def make_level(rho_pad, shift_re, shift_im, scale):
    coefs = face_coefs(rho_pad)
    bsum = coefs[0] + coefs[1] + coefs[2] + coefs[3] + coefs[4] + coefs[5]
    diag_re = scale * bsum - shift_re
    diag_im = -shift_im
    magnitude = diag_re * diag_re + diag_im * diag_im
    return (coefs, bsum, shift_re, shift_im, scale, diag_re / magnitude, -diag_im / magnitude)


def apply_op(upad, level):
    coefs, bsum, shift_re, shift_im, scale, inv_re, inv_im = level
    center = upad[:, :, 1:-1, 1:-1, 1:-1]
    nbsum = coefs[0] * upad[:, :, 2:, 1:-1, 1:-1] + coefs[1] * upad[:, :, :-2, 1:-1, 1:-1]
    nbsum = nbsum + coefs[2] * upad[:, :, 1:-1, 2:, 1:-1] + coefs[3] * upad[:, :, 1:-1, :-2, 1:-1]
    nbsum = nbsum + coefs[4] * upad[:, :, 1:-1, 1:-1, 2:] + coefs[5] * upad[:, :, 1:-1, 1:-1, :-2]
    lap = scale * (bsum * center - nbsum)
    out_re = lap[0] - shift_re * center[0] + shift_im * center[1]
    out_im = lap[1] - shift_re * center[1] - shift_im * center[0]
    return jnp.stack([out_re, out_im])


def precondition(resid, level):
    inv_re, inv_im = (level[5], level[6])
    upd_re = inv_re * resid[0] - inv_im * resid[1]
    upd_im = inv_re * resid[1] + inv_im * resid[0]
    return omega_damp * jnp.stack([upd_re, upd_im])


def smooth(field, target, level, padder, count):
    for sweep in range(count):
        field = field + precondition(target - apply_op(padder(field), level), level)
    return field


def restrict(field):
    lead = field.shape[:-3]
    sx, sy, sz = field.shape[-3:]
    blocks = field.reshape(lead + (sx // 2, 2, sy // 2, 2, sz // 2, 2))
    return jnp.mean(blocks, axis=(-5, -3, -1))


def prolong(field):
    return jnp.repeat(jnp.repeat(jnp.repeat(field, 2, -3), 2, -2), 2, -1)


def field_pad(field):
    return padded(field, (("gx", 2), ("gy", 3), ("gz", 4)), 1)


def brick_density(rho):
    return padded(rho, (("gx", 0), ("gy", 1), ("gz", 2)), 1)


def local_general(rhs, density, shift_real, shift_imag):
    rho1, sr1, si1 = (restrict(density), restrict(shift_real), restrict(shift_imag))
    level1 = make_level(brick_density(rho1), sr1, si1, 0.25)
    rho2, sr2, si2 = (restrict(rho1), restrict(sr1), restrict(si1))
    level0 = make_level(brick_density(density), shift_real, shift_imag, 1.0)
    fine = precondition(rhs, level0)
    fine = smooth(fine, rhs, level0, field_pad, NU - 1)
    coarse_rhs = restrict(rhs - apply_op(field_pad(fine), level0))
    middle = precondition(coarse_rhs, level1)
    middle = smooth(middle, coarse_rhs, level1, field_pad, NU - 1)
    lowest_rhs = restrict(coarse_rhs - apply_op(field_pad(middle), level1))
    level2 = make_level(brick_density(rho2), sr2, si2, 0.0625)
    lowest = precondition(lowest_rhs, level2)
    lowest = smooth(lowest, lowest_rhs, level2, field_pad, CSWEEPS - 1)
    middle = smooth(middle + prolong(lowest), coarse_rhs, level1, field_pad, NU)
    corrected = fine + prolong(middle)
    return smooth(corrected, rhs, level0, field_pad, NU)


HALO = 2
SIDE = 4
MIB = 1 << 20
COARSE_COST = 5 * 10**9
NEAR_COST = 2 * 10**9
JOIN_COST = 10**9
F32 = jnp.float32


def loop(count, body):
    for i in range(count):
        body(i)


def safe(total):
    return jnp.where(total > 0.0, total, 1.0)


def level_coefs(rho, sr, si, scale, bx, by, bz, wr, wi, dr, step, start, count):
    ny, nz = sr.shape[1:]
    two = 2.0 * scale
    bx[pl.ds(start, 1)] = two / safe(rho[pl.ds(start, 1)] + rho[pl.ds(start + 1, 1)])

    def body(i):
        p = start + i * step
        r = rho[pl.ds(p + 1, step)]
        row = lax.broadcasted_iota(jnp.int32, r.shape, 1)
        lane = lax.broadcasted_iota(jnp.int32, r.shape, 2)
        last_y, last_z = row == ny - 1, lane == nz - 1
        tx = safe(r + rho[pl.ds(p + 2, step)])
        ty = safe(r + jnp.where(last_y, 0.0, pltpu.roll(r, ny - 1, 1)))
        tz = safe(r + jnp.where(last_z, 0.0, pltpu.roll(r, nz - 1, 2)))
        te = safe(r)
        pair, other = tx * ty, tz * te
        whole = two / (pair * other)
        per_pair, per_other = whole * other, whole * pair
        bx[pl.ds(p + 1, step)] = per_pair * ty
        edge = per_other * tz
        bsum = bx[pl.ds(p, step)] + bx[pl.ds(p + 1, step)]
        face = per_pair * tx
        bsum = bsum + face + jnp.where(row == 0, edge, pltpu.roll(face, 1, 1))
        by[pl.ds(p, step)] = jnp.where(last_y, 0.0, face)
        face = per_other * te
        bsum = bsum + face + jnp.where(lane == 0, edge, pltpu.roll(face, 1, 2))
        bz[pl.ds(p, step)] = jnp.where(last_z, 0.0, face)
        d = bsum - sr[pl.ds(p, step)]
        e = si[pl.ds(p, step)]
        w = jnp.where(r > 0.0, omega_damp, 0.0) / (d * d + e * e)
        wr[pl.ds(p, step)] = w * d
        wi[pl.ds(p, step)] = w * e
        dr[pl.ds(p, step)] = d

    loop(count // step, body)


def near(u, f, at, p, step, bx, by, bz):
    mid = u[f, pl.ds(at, step)]
    ny, nz = mid.shape[1:]
    b = by[pl.ds(p, step)]
    total = bx[pl.ds(p, step)] * u[f, pl.ds(at - 1, step)] + bx[pl.ds(p + 1, step)] * u[f, pl.ds(at + 1, step)]
    total = total + (b * pltpu.roll(mid, ny - 1, 1) + pltpu.roll(b * mid, 1, 1))
    b = bz[pl.ds(p, step)]
    return mid, total + (b * pltpu.roll(mid, nz - 1, 2) + pltpu.roll(b * mid, 1, 2))


def weigh(tr, ti, p, step, wr, wi):
    a, b = wr[pl.ds(p, step)], wi[pl.ds(p, step)]
    return a * tr - b * ti, a * ti + b * tr


def sweep_planes(u, fields, at, g, gat, p, step, coefs):
    bx, by, bz, wr, wi = coefs
    re, im = fields
    mr, nr = near(u, re, at, p, step, bx, by, bz)
    mi, ni = near(u, im, at, p, step, bx, by, bz)
    vr, vi = weigh(g[re, pl.ds(gat, step)] + nr, g[im, pl.ds(gat, step)] + ni, p, step, wr, wi)
    rest = 1.0 - omega_damp
    return rest * mr + vr, rest * mi + vi


def resid_planes(u, fields, at, g, gat, p, step, coefs, dr, si):
    bx, by, bz = coefs[:3]
    re, im = fields
    mr, nr = near(u, re, at, p, step, bx, by, bz)
    mi, ni = near(u, im, at, p, step, bx, by, bz)
    d, e = dr[pl.ds(p, step)], si[pl.ds(p, step)]
    return g[re, pl.ds(gat, step)] + nr - (d * mr + e * mi), g[im, pl.ds(gat, step)] + ni - (d * mi - e * mr)


def pick(nrow, ncol, down, value):
    row = lax.broadcasted_iota(jnp.int32, (nrow, ncol), 0)
    col = lax.broadcasted_iota(jnp.int32, (nrow, ncol), 1)
    hit = (row // 2 == col) if down else (row == col // 2)
    return jnp.where(hit, value, 0.0).astype(F32)


def dot(a, b):
    b = b.astype(jnp.bfloat16)
    high = a.astype(jnp.bfloat16)
    a = a - high.astype(F32)
    middle = a.astype(jnp.bfloat16)
    low = (a - middle.astype(F32)).astype(jnp.bfloat16)
    parts = [jnp.dot(part, b, preferred_element_type=F32) for part in (low, middle, high)]
    return parts[0] + parts[1] + parts[2]


def send_kernel(rhs, rho, sr, si, away, kept, sems):
    half = away.shape[1]
    m = rhs.shape[1]
    k = lax.axis_index("gz")
    copies = []
    for n, (out, side) in enumerate(((away, 1 - k), (kept, k))):
        planes = pl.ds(side * half, half)
        pieces = [(rhs.at[c, :, planes], out.at[pl.ds(c * m, m)]) for c in range(2)]
        pieces += [(ref.at[planes], out.at[2 * m + j]) for j, ref in enumerate((rho, sr, si))]
        copies += [pltpu.make_async_copy(src, dst, sems.at[5 * n + j]) for j, (src, dst) in enumerate(pieces)]
    for copy in copies:
        copy.start()
    for copy in copies:
        copy.wait()


def rows_kernel(kept, came, to_even, to_odd, ends):
    y = lax.axis_index("gy")
    fields, half, rows, _ = kept.shape
    rho = fields - 3
    for t, ref in enumerate((kept, came)):
        for h in range(2):
            at = 0
            for f in range(fields):
                n = HALO + 1 if f == rho else HALO
                for i in range(half):
                    ends[h, t, at : at + n, :] = ref[f, i, (rows - n if h else 0) : (rows if h else n), :]
                    at += n
    even = lax.rem(y, 2)
    to_even[...] = ends[1 - even]
    to_odd[...] = ends[even]


def means_kernel(kept, away, out, slots, sums):
    k = lax.axis_index("gz")
    fields, half, rows, lanes = kept.shape
    pairs = half // 2
    for t, ref in enumerate((kept, away)):
        for j in range(3):
            for q in range(pairs):
                at = (j * pairs + q) * rows
                slots[at : at + rows, :] = ref[fields - 3 + j, 2 * q] + ref[fields - 3 + j, 2 * q + 1]
        n = 3 * pairs * rows // 2
        sums[t] = slots[pl.ds(0, n, 2), :] + slots[pl.ds(1, n, 2), :]
    done = dot(jnp.concatenate([sums[k], sums[1 - k]], axis=1), pick(2 * lanes, lanes, True, 0.125))
    out[...] = done.reshape(3, pairs, rows // 2, lanes)


def join(axis, parts, out):
    me = lax.axis_index(axis)
    n = out.shape[0] // len(parts)
    for v, ref in enumerate(parts):
        out[pl.ds((me ^ v) * n, n)] = ref[...].reshape((n,) + out.shape[1:])


def double_kernel(level, mine, other, out):
    bit = lax.rem(lax.axis_index("gx") // level, 2)
    out[pl.ds(bit * level, level)] = mine[...].reshape((level,) + out.shape[1:])
    out[pl.ds((1 - bit) * level, level)] = other[...].reshape((level,) + out.shape[1:])


def lay_kernel(kept, came, even, odd, *refs):
    means, other, g, rho, sr, si, to_gz, to_gx, joined, ends = refs
    double_kernel(joined.shape[0] // 2, means, other, joined)
    k = lax.axis_index("gz")
    y = lax.axis_index("gy")
    fields, half, rows, lanes = kept.shape
    m2 = fields - 3
    arrays = [g.at[f] for f in range(m2)] + [rho, sr, si]
    for f, ref in enumerate(arrays):
        first = HALO + 1 if f == m2 else HALO
        for i in range(half):
            ref[first + i] = jnp.zeros(ref.shape[1:], F32)
        for t, src in enumerate((kept, came)):
            z = k if t == 0 else 1 - k
            spot = pl.ds(pl.multiple_of(z * lanes, lanes), lanes)
            for i in range(half):
                ref[first + i, SIDE : SIDE + rows, spot] = src[f, i]
    ends[0] = even[...]
    ends[1] = odd[...]
    for high in range(2):
        there = jnp.where(y < lax.axis_size("gy") - 1, 1.0, 0.0) if high else jnp.where(y > 0, 1.0, 0.0)
        peer = lax.rem(y, 2) if high else 1 - lax.rem(y, 2)
        for z in range(2):
            slot = jnp.where(k == z, 0, 1)
            at = 0
            for f, ref in enumerate(arrays):
                n = HALO + 1 if f == m2 else HALO
                row = SIDE + rows if high else SIDE - n
                for i in range(half):
                    ref[n + i, row : row + n, z * lanes : (z + 1) * lanes] = ends[peer, slot, at : at + n, :] * there
                    at += n
    for out, up in ((to_gz, 1 - k), (to_gx, k)):
        two, three = HALO + up * (half - HALO), HALO + 1 + up * (half - HALO - 1)
        rows, ny = ref.shape[1] - 2 * (SIDE - HALO), ref.shape[1]
        for j, ref in enumerate(arrays[:m2] + [sr, si]):
            for i in range(HALO):
                at = (HALO * j + i) * rows
                out[at : at + rows, :] = ref[two + i, SIDE - HALO : SIDE - HALO + rows, :]
        for i in range(HALO + 1):
            at = HALO * (m2 + 2) * rows + i * ny
            out[at : at + ny, :] = rho[three + i]


def lay_side(came, low, g, rho, sr, si):
    m2, pad = g.shape[:2]
    half = pad - 2 * HALO
    two, three = low * (half + HALO), low * (half + HALO + 1)
    ny, nz = sr.shape[1:]
    rows = ny - 2 * (SIDE - HALO)
    blank = jnp.zeros((ny, nz), F32)
    for j, ref in enumerate([g.at[f] for f in range(m2)] + [sr, si]):
        for i in range(HALO):
            at = (HALO * j + i) * rows
            ref[two + i] = blank
            ref[two + i, SIDE - HALO : SIDE - HALO + rows, :] = came[at : at + rows, :]
    for i in range(HALO + 1):
        at = HALO * (m2 + 2) * rows + i * ny
        rho[three + i] = came[at : at + ny, :]


def side_planes(low, g, rho, sr, si, bx, by, bz, wr, wi, dr, ua, own, rest):
    m2, pad = g.shape[:2]
    m = m2 // 2
    half = pad - 2 * HALO
    count = HALO + 1 if rest else pad - HALO - 1
    start = low * (pad - count)
    level_coefs(rho, sr, si, 1.0, bx, by, bz, wr, wi, dr, count, start, count)

    def first(i):
        p = start + i
        for r in range(m):
            ua[r, pl.ds(p, 1)], ua[m + r, pl.ds(p, 1)] = weigh(g[r, pl.ds(p, 1)], g[m + r, pl.ds(p, 1)], p, 1, wr, wi)

    loop(count, first)
    done = HALO + 1 if rest else half - 1
    begin = low * (pad - 2 - done)

    def second(i):
        at = begin + i
        p = at + 1
        for r in range(m):
            own[r, pl.ds(at, 1)], own[m + r, pl.ds(at, 1)] = sweep_planes(ua, (r, m + r), p, g, p, p, 1, (bx, by, bz, wr, wi))

    loop(done, second)


def beside_kernel(from_gz, _g, _rho, _sr, _si, means, g, rho, sr, si, out):
    lay_side(from_gz, 1 - lax.axis_index("gz"), g, rho, sr, si)
    out[...] = means[...]


def near_kernel(_g, _rho, _sr, _si, *state):
    side_planes(1 - lax.axis_index("gz"), *state, False)


def fine_kernel(from_gx, *refs):
    g, rho, sr, si, bx, by, bz, wr, wi, dr, ua, own, up_gz, up_gx, up_gy, packed, joined, left, right, narrow = refs[-20:]
    join("gy", refs[12:-20], joined)
    k = lax.axis_index("gz")
    lay_side(from_gx, k, g, rho, sr, si)
    side_planes(k, g, rho, sr, si, bx, by, bz, wr, wi, dr, ua, own, True)
    coefs = (bx, by, bz, wr, wi)
    m2, pad, ny, nz = g.shape
    m = m2 // 2
    half = pad - 2 * HALO
    rows = ny - 2 * SIDE
    lanes = nz // 2
    for f in range(m2):
        up_gz[f] = own[f, 2 + (1 - k) * (half - 3), SIDE : SIDE + rows, :]
        up_gx[f] = own[f, 2 + k * (half - 3), SIDE : SIDE + rows, :]
        for i in range(half):
            for h, row in enumerate((SIDE + 1, SIDE + rows - 2)):
                for z in range(2):
                    at = z * m2 * half + f * half + i
                    up_gy[h, at : at + 1, :] = own[f, i + 1, row : row + 1, z * lanes : (z + 1) * lanes]
    pairs = half // 2

    def down(q):
        p = HALO + 2 * q
        totals = {}
        for r in range(m):
            ar, ai = resid_planes(own, (r, m + r), p - 1, g, p, p, 1, coefs, dr, si)
            br, bi = resid_planes(own, (r, m + r), p, g, p + 1, p + 1, 1, coefs, dr, si)
            totals[r], totals[m + r] = ar + br, ai + bi
        for j, v in totals.items():
            spot = pl.ds((j * pairs + q) * ny, ny)
            left[spot, :] = v[0, :, :lanes]
            right[spot, :] = v[0, :, lanes:]

    loop(pairs, down)
    n = m2 * pairs * ny // 2
    both = [ref[pl.ds(0, n, 2), :] + ref[pl.ds(1, n, 2), :] for ref in (left, right)]
    narrow[...] = dot(jnp.concatenate(both, axis=1), pick(nz, lanes, True, 0.125))
    for q in range(pairs):
        done = []
        for j in range(m2):
            at = (j * pairs + q) * (ny // 2) + SIDE // 2
            done.append(narrow[at : at + rows // 2, :])
        for d in range(packed.shape[0]):
            for c in range(2):
                packed[d, c, q] = done[c * m + d % m]


def merge_kernel(chips, fields, means, out):
    parts = fields.shape[0] // chips
    for e in range(fields.shape[0]):
        x, y = divmod(e, parts)
        out[e, :2] = fields[e]
        out[e, 2:] = means[y * chips + x]


def put_means(mine, other, refs, offsets, parts, skip):
    k = lax.axis_index("gz")
    _, _, pairs, rows, lanes = mine.shape
    first = lax.broadcasted_iota(jnp.int32, (pairs, rows, lanes), 2) < lanes // 2
    for e in range(mine.shape[0]):
        s, y = divmod(e, parts)
        for j, ref in enumerate(refs):
            a, b = mine[e, skip + j], other[e, skip + j]
            low, high = jnp.where(k == 0, a, b), jnp.where(k == 0, b, a)
            for h, whole in enumerate((jnp.where(first, low, pltpu.roll(high, lanes // 2, 2)), jnp.where(first, pltpu.roll(low, lanes // 2, 2), high))):
                at = 2 * pairs * s + pairs * h + offsets[j]
                ref[at : at + pairs, y * rows : (y + 1) * rows] = whole


def put_coarse(mine, other, refs, offsets, parts):
    k = lax.axis_index("gz")
    _, _, pairs, rows, _ = mine.shape
    for e in range(mine.shape[0]):
        s, y = divmod(e, parts)
        for came, z in ((mine, k), (other, 1 - k)):
            for j, ref in enumerate(refs):
                ref[pl.ds(2 * pairs * s + pairs * z + offsets[j], pairs), y * rows : (y + 1) * rows] = came[e, j]


def halve(sums, narrow, ny, count, total, values):
    nz = sums.shape[1]

    def body(q):
        for j, v in enumerate(values(q)):
            sums[pl.ds((j * total + q) * ny, ny), :] = v

    loop(total, body)
    n = count * total * ny // 2
    narrow[pl.ds(0, n), :] = dot(sums[pl.ds(0, n, 2), :] + sums[pl.ds(1, n, 2), :], pick(nz, nz, True, 0.125))


def levels(mine, other, si1, bx1, by1, bz1, wr1, wi1, dr1, bx2, by2, bz2, wr2, wi2, rho1, sr1, rho2, sr2, si2, dr2, sums, narrow):
    n1, ny, nz = si1.shape
    zero = jnp.zeros((1, ny, nz), F32)
    rho1[pl.ds(0, 1)] = zero
    rho1[pl.ds(n1 + 1, 1)] = zero
    put_means(mine, other, (rho1, sr1, si1), (1, 0, 0), ny // mine.shape[3], 2)
    level_coefs(rho1, sr1, si1, 0.25, bx1, by1, bz1, wr1, wi1, dr1, 8, 0, n1)
    n2, ny2 = sr2.shape[:2]
    halve(sums, narrow, ny, 3, n2, lambda q: (rho1[2 * q + 1] + rho1[2 * q + 2], sr1[2 * q] + sr1[2 * q + 1], si1[2 * q] + si1[2 * q + 1]))
    zero2 = jnp.zeros((1, ny2, nz), F32)
    rho2[pl.ds(0, 1)] = zero2
    rho2[pl.ds(n2 + 1, 1)] = zero2
    n = n2 * ny2
    for j, ref in enumerate((rho2.at[pl.ds(1, n2)], sr2, si2)):
        ref[...] = narrow[j * n : (j + 1) * n, :].reshape(n2, ny2, nz)
    level_coefs(rho2, sr2, si2, 0.0625, bx2, by2, bz2, wr2, wi2, dr2, n2, 0, n2)


def coarse_kernel(mine, other, out, si1, bx1, by1, bz1, wr1, wi1, dr1, bx2, by2, bz2, wr2, wi2, rho1, sr1, rho2, sr2, si2, dr2, sums, narrow, g1, ua1, ub1, g2, ua2, ub2, wide, tall):
    levels(mine, other, si1, bx1, by1, bz1, wr1, wi1, dr1, bx2, by2, bz2, wr2, wi2, rho1, sr1, rho2, sr2, si2, dr2, sums, narrow)
    k = lax.axis_index("gz")
    chip = lax.axis_index("gx")
    pairs = mine.shape[2]
    n1, ny, nz = si1.shape
    zero = jnp.zeros((1, ny, nz), F32)
    for u in (ua1, ub1):
        for c in range(2):
            u[c, pl.ds(0, 1)] = zero
            u[c, pl.ds(n1 + 1, 1)] = zero
    put_coarse(mine, other, (g1.at[0], g1.at[1]), (0, 0), ny // mine.shape[3])
    step1 = 4
    coefs1 = (bx1, by1, bz1, wr1, wi1)

    def first(i):
        p = i * step1
        r, m = weigh(g1[0, pl.ds(p, step1)], g1[1, pl.ds(p, step1)], p, step1, wr1, wi1)
        ua1[0, pl.ds(p + 1, step1)], ua1[1, pl.ds(p + 1, step1)] = r, m

    loop(n1 // step1, first)

    def sweep1(src, dst):
        def body(i):
            p = i * step1
            r, m = sweep_planes(src, (0, 1), p + 1, g1, p, p, step1, coefs1)
            dst[0, pl.ds(p + 1, step1)], dst[1, pl.ds(p + 1, step1)] = r, m

        loop(n1 // step1, body)

    sweep1(ua1, ub1)
    n2, ny2 = n1 // 2, ny // 2

    def down(q):
        r, m = resid_planes(ub1, (0, 1), 2 * q + 1, g1, 2 * q, 2 * q, 2, coefs1, dr1, si1)
        return r[0] + r[1], m[0] + m[1]

    halve(sums, narrow, ny, 2, n2, down)
    zero2 = jnp.zeros((1, ny2, nz), F32)
    n = n2 * ny2
    for c in range(2):
        g2[c] = narrow[c * n : (c + 1) * n, :].reshape(n2, ny2, nz)
        for u in (ua2, ub2):
            u[c, pl.ds(0, 1)] = zero2
            u[c, pl.ds(n2 + 1, 1)] = zero2
    coefs2 = (bx2, by2, bz2, wr2, wi2)
    ua2[0, pl.ds(1, n2)], ua2[1, pl.ds(1, n2)] = weigh(g2[0], g2[1], 0, n2, wr2, wi2)
    src, dst = ua2, ub2
    for _ in range(CSWEEPS - 1):
        dst[0, pl.ds(1, n2)], dst[1, pl.ds(1, n2)] = sweep_planes(src, (0, 1), 1, g2, 0, 0, n2, coefs2)
        src, dst = dst, src

    widen = pick(nz, nz, False, 1.0)
    for c in range(2):
        wide[pl.ds(c * n, n), :] = dot(src[c, pl.ds(1, n2)].reshape(n, nz), widen)
    twice = wide[pl.ds(0, 2 * n), :]
    tall[pl.ds(0, 2 * n, 2), :] = twice
    tall[pl.ds(1, 2 * n, 2), :] = twice

    def lift(q):
        for c in range(2):
            v = tall[pl.ds((c * n2 + q) * ny, ny), :]
            for j in range(2):
                ub1[c, 2 * q + j + 1] = ub1[c, 2 * q + j + 1] + v

    loop(n2, lift)
    sweep1(ub1, ua1)
    sweep1(ua1, ub1)
    out[...] = ub1[:, pl.ds((2 * chip + k) * pairs, 2 + pairs)]


def pack_kernel(u1, up_gy, from_gz, from_gx, *refs):
    *outs, edges, blocks = refs
    k = lax.axis_index("gz")
    me = lax.axis_index("gy")
    edges[k] = from_gz[...]
    edges[1 - k] = from_gx[...]
    _, quads, ny, nz = u1.shape
    parts = len(outs)
    rows = ny // parts
    edge = SIDE // 2
    tall_rows = rows + 2 * edge
    for y in range(parts):
        low, high = max(y * rows - edge, 0), min((y + 1) * rows + edge, ny)
        for c in range(2):
            for q in range(quads):
                at = (c * quads + q) * tall_rows
                skip = low - (y * rows - edge)
                end = skip + high - low
                if skip:
                    blocks[y, at : at + skip, :] = jnp.zeros((skip, nz), F32)
                blocks[y, at + skip : at + end, :] = u1[c, q, low:high, :]
                if end < tall_rows:
                    blocks[y, at + end : at + tall_rows, :] = jnp.zeros((tall_rows - end, nz), F32)
    used = 2 * quads * tall_rows
    for v, out in enumerate(outs):
        out[:used, :] = blocks[me ^ v]
        out[used:, :] = up_gy[jnp.where(me < (me ^ v), 1, 0)]


def last_kernel(*refs):
    *back, own, edges, g, bx, by, bz, wr, wi, out, ua, ub, tall, flat = refs
    k = lax.axis_index("gz")
    y = lax.axis_index("gy")
    m2, pad, ny, nz = ua.shape
    m = m2 // 2
    half = pad - 2 * HALO
    rows = ny - 2 * SIDE
    quads = pad // 2
    lanes = nz // 2
    ua[:, pl.ds(1, pad - 2)] = own[...]
    blank = jnp.zeros((m2, ny, nz), F32)
    for p, side in ((0, 1), (pad - 1, 0)):
        ua[:, p] = blank
        ua[:, p, SIDE : SIDE + rows, :] = edges[side]
    used = 2 * quads * ny // 2
    for v, ref in enumerate(back):
        flat[y ^ v] = ref[...]
    for high in range(2):
        there = jnp.where(y < m - 1, 1.0, 0.0) if high else jnp.where(y > 0, 1.0, 0.0)
        peer = jnp.minimum(y + 1, m - 1) if high else jnp.maximum(y - 1, 0)
        row = SIDE + rows + 1 if high else SIDE - 2
        block = flat[peer, used:, :] * there
        for z in range(2):
            for f in range(m2):
                for i in range(half):
                    at = z * m2 * half + f * half + i
                    ua[f, HALO + i, row : row + 1, z * lanes : (z + 1) * lanes] = block[at : at + 1, :]
    u1 = flat[:, :used, :].reshape(m * used, lanes)
    for h in range(2):
        col = lax.broadcasted_iota(jnp.int32, (lanes, lanes), 1) + h * lanes
        line = lax.broadcasted_iota(jnp.int32, (lanes, lanes), 0)
        v = dot(u1, jnp.where(line == col // 2, 1.0, 0.0).astype(F32))
        tall[pl.ds(0, m * used, 2), :] = v
        tall[pl.ds(1, m * used, 2), :] = v
        spot = slice(h * lanes, (h + 1) * lanes)
        for r in range(m):
            for c in range(2):
                for q in range(quads):
                    at = ((r * 2 + c) * quads + q) * ny
                    w = tall[at : at + ny, :]
                    f = c * m + r
                    for j in range(2):
                        ua[f, 2 * q + j, :, spot] = ua[f, 2 * q + j, :, spot] + w
    coefs = (bx, by, bz, wr, wi)

    def third(i):
        p = i + 1
        for r in range(m):
            ub[r, pl.ds(p, 1)], ub[m + r, pl.ds(p, 1)] = sweep_planes(ua, (r, m + r), p, g, p, p, 1, coefs)

    loop(pad - 2, third)

    def fourth(i):
        p = i + HALO
        for r in range(m):
            for c, v in enumerate(sweep_planes(ub, (r, m + r), p, g, p, p, 1, coefs)):
                for z in range(2):
                    slot = jnp.where(k == z, 0, 1)
                    out[slot, c, r, i] = v[0, SIDE : SIDE + rows, z * lanes : (z + 1) * lanes]

    loop(half, fourth)


def gather_kernel(kept, came, out):
    k = lax.axis_index("gz")
    half = kept.shape[2]
    for side, ref in ((k, kept), (1 - k, came)):
        for c in range(2):
            for r in range(kept.shape[1]):
                out[c, r, pl.ds(side * half, half)] = ref[c, r]


def call(kernel, outs, args, scratch=(), limit=14, space=pltpu.VMEM, sems=None, cost=None, aliases=None):
    single = not isinstance(outs, list)
    shapes = [outs] if single else outs
    result = pl.pallas_call(
        kernel,
        out_shape=[jax.ShapeDtypeStruct(s, F32) for s in shapes],
        in_specs=[pl.BlockSpec(memory_space=space)] * len(args),
        out_specs=[pl.BlockSpec(memory_space=pltpu.VMEM)] * len(shapes),
        scratch_shapes=[pltpu.VMEM(s, F32) for s in scratch] + ([pltpu.SemaphoreType.DMA((sems,))] if sems else []),
        compiler_params=pltpu.CompilerParams(vmem_limit_bytes=limit * MIB),
        input_output_aliases=aliases or {},
        cost_estimate=cost and pl.CostEstimate(flops=cost, bytes_accessed=0, transcendentals=0),
    )(*args)
    return result[0] if single else result


def local_planes(rhs, density, shift_real, shift_imag):
    _, m, xs, rows, lanes = rhs.shape
    half = xs // 2
    chips = lax.axis_size("gx")
    ny, nz = rows * m, 2 * lanes
    pad = half + 2 * HALO
    swap = [(0, 1), (1, 0)]
    ends = [p for c in range(chips - 1) for p in ((2 * c + 1, 2 * c + 2), (2 * c + 2, 2 * c + 1))]
    fields = (rhs, density, shift_real, shift_imag)

    own_half = (2 * m + 3, half, rows, lanes)
    placed = tuple(pltpu.with_memory_space_constraint(f, pltpu.HBM) for f in fields)
    away, kept = call(send_kernel, [own_half, own_half], placed, space=pltpu.HBM, sems=10)
    came = lax.ppermute(away, "gz", swap)
    pairs = half // 2
    means = (3, pairs, rows // 2, lanes)
    n = 3 * pairs * rows
    coarse = call(means_kernel, means, (kept, away), scratch=[(n, lanes), (2, n // 2, lanes)])

    def spread(array, axis, count):
        return [lax.ppermute(array, axis, [(i, i ^ v) for i in range(count)]) if v else array for v in range(count)]

    level = 1
    while level < chips:
        coarse = (coarse, lax.ppermute(coarse, "gx", [(i, i ^ level) for i in range(chips)]))
        level *= 2
        if level < chips:
            coarse = call(functools.partial(double_kernel, level // 2), (level, *means), coarse, cost=JOIN_COST)

    rim = ((2 * m + 3) * HALO + 1) * half
    rim = (2, -(-rim // 8) * 8, lanes)
    to_even, to_odd = call(rows_kernel, [rim, rim], (kept, came), scratch=[(2,) + rim])
    even = lax.ppermute(to_even, "gy", [(i, i ^ 1) for i in range(m)])
    odd = lax.ppermute(to_odd, "gy", [(i, (i + 2 * (i % 2) - 1) % m) for i in range(m)])

    plane = (rows + 2 * SIDE, nz)
    laid = [(2 * m, pad) + plane, (pad + 2,) + plane, (pad,) + plane, (pad,) + plane]
    edges = (HALO * (2 * m + 2) * (rows + 2 * HALO) + (HALO + 1) * plane[0], nz)
    *state, to_gz, to_gx, coarse = call(lay_kernel, laid + [edges, edges, (chips, *means)], (kept, came, even, odd, *coarse), scratch=[(2,) + rim])
    from_gx = lax.ppermute(to_gx, ("gx", "gz"), ends)
    from_gz = lax.ppermute(to_gz, "gz", swap)

    brow = (rows, nz)
    tall0 = 2 * m * pairs * plane[0]
    full = laid + [(pad + 1,) + plane] + [(pad,) + plane] * 5 + [(2 * m, pad) + plane, (2 * m, pad - 2) + plane]
    *state, coarse = call(beside_kernel, laid + [(chips, *means)], (from_gz, *state, coarse), aliases={i + 1: i for i in range(len(laid))})
    coarse = spread(coarse, "gy", m)
    state = call(near_kernel, full, tuple(state), aliases={i: i for i in range(len(laid))}, cost=NEAR_COST)
    g, _, _, _, bx, by, bz, wr, wi, _, _, own, up_gz, up_gx, up_gy, packed, coarse = call(
        fine_kernel,
        full + [(2 * m,) + brow, (2 * m,) + brow, (2, 4 * m * half, lanes), (chips * m, 2, pairs, rows // 2, lanes), (m * chips, *means)],
        (from_gx, *state, *coarse),
        scratch=[(tall0, lanes), (tall0, lanes), (tall0 // 2, lanes)],
        aliases={i + 1: i for i in range(len(full))},
    )
    u_gx = lax.ppermute(up_gx, ("gx", "gz"), ends)
    u_gz = lax.ppermute(up_gz, "gz", swap)
    mine = lax.all_to_all(packed, ("gx", "gy"), 0, 0, tiled=True)
    mine = call(functools.partial(merge_kernel, chips), (chips * m, 5) + packed.shape[2:], (mine, coarse))
    other = lax.ppermute(mine, "gz", swap)

    n1, n2 = chips * xs // 2, chips * xs // 4
    p1, p2 = (ny // 2, nz // 2), (ny // 4, nz // 2)

    u1 = call(
        coarse_kernel,
        (2, 2 + pairs) + p1,
        (mine, other),
        scratch=[(n1,) + p1, (n1 + 1,) + p1]
        + [(n1,) + p1] * 5
        + [(n2 + 1,) + p2]
        + [(n2,) + p2] * 4
        + [(n1 + 2,) + p1, (n1,) + p1, (n2 + 2,) + p2, (n2,) + p2, (n2,) + p2, (n2,) + p2, (3 * n2 * p1[0], lanes), (3 * n2 * p2[0], lanes)]
        + [(2, n1) + p1, (2, n1 + 2) + p1, (2, n1 + 2) + p1, (2, n2) + p2, (2, n2 + 2) + p2, (2, n2 + 2) + p2]
        + [(2 * n2 * p2[0], lanes), (2 * n2 * p1[0], lanes)],
        cost=COARSE_COST,
    )
    used = (2 + pairs) * plane[0]
    block = (used + 4 * m * half, lanes)
    *blocks, halo = call(pack_kernel, [block] * m + [(2, 2 * m) + brow], (u1, up_gy, u_gz, u_gx), scratch=[(m, used, lanes)])
    back = [lax.ppermute(b, "gy", [(i, i ^ v) for i in range(m)]) if v else b for v, b in enumerate(blocks)]
    result = call(
        last_kernel,
        (2, 2, m, half, rows, lanes),
        (*back, own, halo, g, bx, by, bz, wr, wi),
        scratch=[(2 * m, pad) + plane, (2 * m, pad) + plane, (2 * m * used, lanes), (m,) + block],
    )
    last = lax.ppermute(result[1], "gz", swap)
    return call(gather_kernel, rhs.shape, (result[0], last))


def solution(mesh):
    sizes = dict(mesh.shape)

    def local(rhs, density, shift_real, shift_imag):
        _, m, xs, rows, lanes = rhs.shape
        planes = sizes["gz"] == 2 and sizes["gy"] == m == 4 and sizes["gx"] in (2, 4, 8) and xs == 8 and rows % 16 == 0 and lanes == 128
        return (local_planes if planes else local_general)(rhs, density, shift_real, shift_imag)

    placed = (
        P(None, None, "gx", "gy", "gz"),
        P("gx", "gy", "gz"),
        P("gx", "gy", "gz"),
        P("gx", "gy", "gz"),
    )
    return jax.shard_map(
        local,
        mesh=mesh,
        in_specs=placed,
        out_specs=P(None, None, "gx", "gy", "gz"),
        check_vma=False,
    )
```
